32 devices in a mesh: groups: 2 (over y), ep: 4 (over z), half: 2 (over x), tp: 2 (over core).
Axes of the slice: x: 2, y: 2, z: 4, core: 2. Of those that a mesh axis runs over, the one named last changes fastest.
Arguments:
- queries: bfloat16 [512, 2048], P(('groups', 'ep', 'half'), 'tp'), parts along dimension 0, may hold values from -6 to 6
- new_keys: bfloat16 [512, 256], P(('groups', 'ep', 'half'), 'tp'), parts along dimension 0, may hold values from -4 to 4
- new_values: bfloat16 [512, 256], P(('groups', 'ep', 'half'), 'tp'), parts along dimension 0, may hold values from -4 to 4
- cache_keys: bfloat16 [512, 2, 64, 128], P(('groups', 'ep', 'half'), 'tp'), parts along dimension 0, may hold values from -4 to 4
- cache_values: bfloat16 [512, 2, 64, 128], P(('groups', 'ep', 'half'), 'tp'), parts along dimension 0, may hold values from -4 to 4
- lengths: int32 [512], P(('groups', 'ep', 'half')), parts along dimension 0, may hold values from 1 to 64, as said below
- out_weight: bfloat16 [2048, 2048], P('tp', 'half'), may hold values from -0.375 to 0.375
- residual: bfloat16 [512, 2048], P(('groups', 'ep'), 'half'), parts along dimension 0, may hold values from -5 to 5
- norm_gain: float32 [2048], P('half'), may hold values from 0.1 to 1.9
- expert_ids: int32 [512, 8], P(('groups', 'ep')), parts along dimension 0, may hold values from 0 to 63, all different within a row; in each aligned block of 64 rows (0 to 63, 64 to 127, ...) at most 12 rows name the same one
- gate_weights: float32 [512, 8], P(('groups', 'ep')), parts along dimension 0, may hold values from 0.05 to 1
- w_gate: bfloat16 [64, 768, 2048], P(('ep', 'tp'), 'half'), may hold values from -0.125 to 0.125
- w_up: bfloat16 [64, 768, 2048], P(('ep', 'tp'), 'half'), may hold values from -0.125 to 0.125
- w_down: bfloat16 [64, 768, 2048], P(('ep', 'tp'), 'half'), may hold values from -0.625 to 0.625
Outputs:
- layer_out: bfloat16 [512, 2048], P(('groups', 'ep'), ('half', 'tp')), parts along dimension 0
The draws below stay inside these ranges and needn't reach their ends.
There are 2 independent parts, one for each index of `groups`. The reference program is written for one: setup_inputs(seed, part) draws one part's arguments, and reference() takes and returns one part's arrays. A program takes and returns all parts, laid end to end along the dimension named above; an argument that names none is the same for every part. Nothing has to cross between parts.
Inputs may be any that keep to these rules, and one draw needn't show every extreme that they name: `expert_ids`: in each block of 64 consecutive rows (the tokens of one index of ep) no expert is named by more than 12 rows. `lengths`: among each device's 32 requests one has 64 cached tokens.
All inputs are finite; a program needn't handle non-finite values.
Results may differ from the reference program's by a relative error of at most 0.014.
Values may be sent and summed in bfloat16 or wider, within the bound.
No kernel may reach another device: no remote copies, remote signals or barrier semaphores. Data moves between devices by JAX's collectives and lax.ppermute only.
A program may use at most 128 MiB of HBM per device.

```python
import math
import jax
import jax.numpy as jnp
import numpy as np
from jax import lax

D = 2048
HEADS = 16
KVH = 2
HD = 128
FF = 768
EXPERTS = 64
TOPK = 8
REQ_DEV = 32
CTX = 64
GROUP = 8
TOK_EP = 64
REQS = 256
CAP = 12
N_EP = 4
N_HALF = 2


def draw_queries(key, part):
    values = jnp.clip(jax.random.normal(jax.random.fold_in(key, 102), (REQS, HEADS, HD)), -4.0, 4.0)
    return values.reshape(REQS, HEADS * HD).astype(jnp.bfloat16)


def draw_cache_keys(key, part):
    values = jnp.clip(jax.random.normal(jax.random.fold_in(key, 104), (REQS, KVH, CTX, HD)), -4.0, 4.0)
    return values.astype(jnp.bfloat16)


def draw_lengths(key, part):
    drawn = jax.random.randint(jax.random.fold_in(key, 111), (REQS,), 1, CTX + 1)
    offsets = jax.random.randint(jax.random.fold_in(key, 112), (REQS // REQ_DEV,), 0, REQ_DEV)
    longest = (jnp.arange(REQ_DEV)[None, :] == offsets[:, None]).reshape(REQS)
    return jnp.where(longest, CTX, drawn).astype(jnp.int32)


def levels(rng, shape, cuts, smallest, high):
    level = 1.0
    for dim, shards_of in cuts:
        heights = jax.random.uniform(jax.random.fold_in(jax.random.fold_in(rng, 6), dim), (shards_of,), jnp.float32, smallest / len(cuts), high / len(cuts))
        level = level * jnp.repeat(jnp.exp(heights), shape[dim] // shards_of).reshape((-1,) + (1,) * (len(shape) - 1 - dim))
    return level


def shared_out(own_key, own, number, rows, number_of, top, reach, slope):
    sequence = jax.random.permutation(own_key, number_of)
    heavy_load, usual = shares(number_of, rows * top, reach, slope, True), shares(number_of, rows * top, reach, slope, False)
    places = jnp.arange(number_of)

    def named(sizes, offset_by):
        used = int((sizes > 0).sum())
        fixed = max(1, used // 4)
        passed = fixed + (places - fixed + offset_by * (used - fixed)) % max(1, number_of - fixed)
        return jnp.zeros((number_of,), jnp.int32).at[sequence[jnp.where(places < fixed, places, passed)]].set(jnp.asarray(sizes, jnp.int32))

    sizes = jnp.where(number % 4 == 0, named(heavy_load, number // 4), named(usual, number - number // 4 - 1))
    mixed = jax.random.permutation(jax.random.fold_in(own, 3), number_of)
    donor, sink = mixed[0:number_of // 2 * 2:2], mixed[1:number_of // 2 * 2:2]
    room = jnp.minimum(sizes[donor] - 1, reach - sizes[sink]) // 2
    room = jnp.where((donor == sequence[0]) | (sink == sequence[0]) | (sizes[sink] == 0), 0, jnp.maximum(room, 0))
    passed = jax.random.randint(jax.random.fold_in(own, 4), (number_of // 2,), 0, 1 << 20) % (room + 1)
    sizes = sizes.at[donor].add(-passed).at[sink].add(passed)
    labels = jnp.searchsorted(jnp.cumsum(sizes), jnp.arange(rows * top), side="right").astype(jnp.int32)
    listing = labels.reshape(top, rows).T
    listing = listing[jax.random.permutation(jax.random.fold_in(own, 1), rows)]
    offset_by = jax.random.randint(jax.random.fold_in(own, 2), (rows, 1), 0, top)
    return jnp.take_along_axis(listing, (jnp.arange(top)[None, :] + offset_by) % top, axis=1)


def shares(number_of, total, reach, slope, full):
    loads = [(1 << 20) // math.isqrt(standing ** slope) + 1 for standing in range(1, number_of + 1)]
    largest = reach if full else min(reach, max(-(-total // number_of), total * loads[0] // sum(loads)))
    least = 1 if total - largest >= number_of - 1 else 0
    counts, surplus = [largest] + [least] * (number_of - 1), total - largest - least * (number_of - 1)
    while surplus > 0:
        candidates = [i for i in range(1, number_of) if counts[i] < largest] or [i for i in range(1, number_of) if counts[i] < reach]
        whole, budget = sum([loads[i] for i in candidates]), surplus
        for i in candidates:
            addition = min(reach - counts[i], max(1, budget * loads[i] // whole), surplus)
            counts[i] = counts[i] + addition
            surplus = surplus - addition
    return np.array(counts)


def normal_values(rng, extent, deviation, limit, cuts=(), kind=jnp.bfloat16):
    entries = jax.random.normal(rng, extent, jnp.float32) * deviation
    if len(cuts) > 0:
        entries = levels(rng, extent, cuts, -0.22, 0.18) * entries
    return jnp.clip(entries, min=-limit, max=limit).astype(kind)


def setup_inputs(seed: int = 0, part: int = 0) -> dict:
    key_list = jax.random.split(jax.random.key(seed), 15)
    part_keys = jax.random.split(jax.random.fold_in(key_list[14], part), 15)
    queries = draw_queries(jax.random.fold_in(jax.random.fold_in(key_list[14], part), 71), part)
    new_keys = normal_values(part_keys[1], (REQS, KVH * HD), 1.0, 4.0, ((0, 8), (1, 2)))
    new_values = normal_values(part_keys[2], (REQS, KVH * HD), 1.0, 4.0, ((0, 8), (1, 2)))
    cache_keys = draw_cache_keys(jax.random.fold_in(jax.random.fold_in(key_list[14], part), 71), part)
    cache_values = normal_values(part_keys[4], (REQS, KVH, CTX, HD), 1.0, 4.0, ((0, 8), (1, 2)))
    lengths = draw_lengths(jax.random.fold_in(jax.random.fold_in(key_list[14], part), 71), part)
    out_weight = normal_values(key_list[6], (HEADS * HD, D), (HEADS * HD // 8) ** -0.5, 0.375, ((0, 2), (1, 2)))
    residual = normal_values(part_keys[7], (REQS, D), 1.0, 5.0, ((0, 4), (1, 2)))
    norm_gain = jnp.clip(1.0 + 0.18 * jax.random.normal(key_list[8], (D,), jnp.float32), 0.1, 1.9)
    expert_ids_keys = jax.random.split(jax.random.fold_in(part_keys[9], 1), REQS // TOK_EP)
    expert_ids_turns = jax.random.permutation(jax.random.fold_in(part_keys[9], 3), REQS // TOK_EP)
    expert_ids = jax.vmap(lambda own, number: shared_out(jax.random.fold_in(part_keys[9], 2), own, number, TOK_EP, EXPERTS, TOPK, CAP, 2))(expert_ids_keys, expert_ids_turns).reshape((REQS, TOPK))
    gate_weights = jnp.clip(0.05 + 0.95 * jax.random.uniform(part_keys[10], (REQS, TOPK), jnp.float32) ** levels(part_keys[10], (REQS, TOPK), ((0, 4),), -0.2, 0.2), 0.05, 1.0)
    w_gate = normal_values(key_list[11], (EXPERTS, FF, D), D ** -0.5, 0.125, ((0, 8), (1, 2)))
    w_up = normal_values(key_list[12], (EXPERTS, FF, D), D ** -0.5, 0.125, ((0, 8), (1, 2)))
    w_down = normal_values(key_list[13], (EXPERTS, FF, D), (FF // 8) ** -0.5, 0.625, ((0, 8), (1, 2)))
    return dict(queries=queries, new_keys=new_keys, new_values=new_values, cache_keys=cache_keys, cache_values=cache_values, lengths=lengths, out_weight=out_weight, residual=residual, norm_gain=norm_gain, expert_ids=expert_ids, gate_weights=gate_weights, w_gate=w_gate, w_up=w_up, w_down=w_down)


def attention(queries, new_keys, new_values, cache_keys, cache_values, lengths):
    query_blocks = queries.reshape(REQS, KVH, GROUP, HD).astype(jnp.float32)
    score_scale = 1.0 / math.sqrt(HD)
    scores = jnp.einsum('rkgd,rkcd->rkgc', query_blocks, cache_keys.astype(jnp.float32)) * score_scale
    own_score = jnp.einsum('rkgd,rkd->rkg', query_blocks, new_keys.reshape(REQS, KVH, HD).astype(jnp.float32)) * score_scale
    valid = lax.iota(jnp.int32, CTX)[None, :] < lengths[:, None]
    scores = jnp.where(valid[:, None, None, :], scores, -1e+30)
    highest = jnp.maximum(lax.optimization_barrier(jnp.max(scores, axis=-1)), own_score)
    weights = jnp.exp(scores - highest[..., None])
    own_weight = jnp.exp(own_score - highest)
    denominator = lax.optimization_barrier(jnp.sum(weights, axis=-1)) + own_weight
    probs = (weights / denominator[..., None]).astype(jnp.bfloat16)
    own_prob = (own_weight / denominator).astype(jnp.bfloat16)
    mixture = jnp.einsum('rkgc,rkcd->rkgd', probs.astype(jnp.float32), cache_values.astype(jnp.float32))
    mixture = mixture + own_prob.astype(jnp.float32)[..., None] * new_values.reshape(REQS, KVH, 1, HD).astype(jnp.float32)
    return mixture.astype(jnp.bfloat16).reshape(REQS, HEADS * HD)

def reference(queries, new_keys, new_values, cache_keys, cache_values, lengths, out_weight, residual, norm_gain, expert_ids, gate_weights, w_gate, w_up, w_down):
    attended = attention(queries, new_keys, new_values, cache_keys, cache_values, lengths)
    mixed = jnp.dot(attended, out_weight, preferred_element_type=jnp.float32)
    hidden = residual.astype(jnp.float32) + mixed
    inverse = lax.rsqrt(lax.optimization_barrier(jnp.mean(hidden * hidden, axis=1)) + 1e-06)
    normed = (hidden * inverse[:, None] * norm_gain[None, :]).astype(jnp.bfloat16)
    gates = gate_weights / lax.optimization_barrier(jnp.sum(gate_weights, axis=1, keepdims=True))
    id_blocks = expert_ids.reshape(N_EP, TOK_EP * TOPK)
    one_hot = (id_blocks[:, :, None] == jnp.arange(EXPERTS, dtype=jnp.int32)[None, None, :]).astype(jnp.int32)
    earlier = jnp.cumsum(one_hot, axis=1) - one_hot
    slot = lax.optimization_barrier(jnp.sum(earlier * one_hot, axis=2)).astype(jnp.int32)
    block_index = jnp.broadcast_to(jnp.arange(N_EP, dtype=jnp.int32)[:, None], slot.shape)
    token_index = block_index * TOK_EP + (jnp.arange(TOK_EP * TOPK, dtype=jnp.int32) // TOPK)[None, :]
    table = jnp.full((EXPERTS, N_EP, CAP), REQS, jnp.int32).at[id_blocks, block_index, slot].set(token_index)
    gate_table = jnp.zeros((EXPERTS, N_EP, CAP), jnp.float32).at[id_blocks, block_index, slot].set(gates.reshape(N_EP, TOK_EP * TOPK))
    padded = jnp.concatenate([normed, jnp.zeros((1, D), jnp.bfloat16)], axis=0)
    block_width = FF // N_HALF

    def expert_step(carry, pieces):
        rows_index, row_gates, gate_matrix, up_matrix, down_matrix = pieces
        flat_index = rows_index.reshape(-1)
        rows = padded[flat_index].astype(jnp.float32)
        gate_part = jnp.dot(rows, gate_matrix.astype(jnp.float32).T, precision=lax.Precision.HIGHEST)
        up_part = jnp.dot(rows, up_matrix.astype(jnp.float32).T, precision=lax.Precision.HIGHEST)
        activation = (jax.nn.silu(gate_part) * up_part).astype(jnp.bfloat16).astype(jnp.float32)
        summed = jnp.zeros((rows.shape[0], D), jnp.float32)
        for block in range(N_HALF):
            lower = block * block_width
            part = jnp.dot(activation[:, lower:lower + block_width], down_matrix[lower:lower + block_width].astype(jnp.float32), precision=lax.Precision.HIGHEST)
            part = lax.optimization_barrier(part.astype(jnp.bfloat16))
            summed = summed + part.astype(jnp.float32)
        carry = carry.at[flat_index].add(row_gates.reshape(-1)[:, None] * summed)
        return (carry, None)
    start_sum = jnp.zeros((REQS + 1, D), jnp.float32)
    combined, unused = lax.scan(expert_step, start_sum, (table, gate_table, w_gate, w_up, w_down))
    return (hidden + combined[:REQS]).astype(jnp.bfloat16)
```

```python
import functools
import math

import jax
import jax.numpy as jnp
from jax import lax
from jax.experimental import pallas as pl
from jax.experimental.pallas import tpu as pltpu
from jax.sharding import PartitionSpec as P

EXPERTS = 64


EPSILON = 1e-06

MIB = 2**20


def attend(queries, new_keys, new_values, cache_keys, cache_values, lengths):
    requests, key_heads, context, head_size = cache_keys.shape
    sharing = queries.shape[1] // (key_heads * head_size)
    query_blocks = queries.reshape(requests, key_heads, sharing, head_size)
    score_scale = 1.0 / math.sqrt(head_size)
    scores = (
        jnp.einsum("rkgd,rkcd->rkgc", query_blocks, cache_keys, preferred_element_type=jnp.float32)
        * score_scale
    )
    own_score = (
        jnp.einsum(
            "rkgd,rkd->rkg",
            query_blocks,
            new_keys.reshape(requests, key_heads, head_size),
            preferred_element_type=jnp.float32,
        )
        * score_scale
    )
    valid = lax.iota(jnp.int32, context)[None, :] < lengths[:, None]
    scores = jnp.where(valid[:, None, None, :], scores, -1e30)
    highest = jnp.maximum(jnp.max(scores, axis=-1), own_score)
    weights = jnp.exp(scores - highest[..., None])
    own_weight = jnp.exp(own_score - highest)
    denominator = jnp.sum(weights, axis=-1) + own_weight
    probs = (weights / denominator[..., None]).astype(jnp.bfloat16)
    own_prob = (own_weight / denominator).astype(jnp.bfloat16)
    mixture = jnp.einsum("rkgc,rkcd->rkgd", probs, cache_values, preferred_element_type=jnp.float32)
    mixture = mixture + own_prob.astype(jnp.float32)[..., None] * new_values.reshape(
        requests, key_heads, 1, head_size
    ).astype(jnp.float32)
    return mixture.astype(jnp.bfloat16).reshape(requests, key_heads * sharing * head_size)


def combine_rows(returned_rows, target, gates):
    token_rows, top_count = target.shape
    safe_target = jnp.maximum(target, 0).reshape(-1)
    picked = jnp.take(returned_rows, safe_target, axis=0).reshape(
        token_rows, top_count, returned_rows.shape[1]
    )
    weighting = jnp.where(target >= 0, gates, 0.0)
    return jnp.sum(picked.astype(jnp.float32) * weighting[..., None], axis=1)


def by_slots(
    queries,
    new_keys,
    new_values,
    cache_keys,
    cache_values,
    lengths,
    out_weight,
    residual,
    norm_gain,
    expert_ids,
    gate_weights,
    w_gate,
    w_up,
    w_down,
):
    attended = attend(queries, new_keys, new_values, cache_keys, cache_values, lengths)
    partial_mix = jnp.dot(
        lax.all_gather(attended, "half", axis=0, tiled=True),
        out_weight,
        preferred_element_type=jnp.float32,
    )
    mixed = lax.psum(partial_mix.astype(jnp.bfloat16), "tp").astype(jnp.float32)
    hidden = residual.astype(jnp.float32) + mixed
    squares = lax.psum(jnp.sum(hidden * hidden, axis=1), "half")
    half_width = hidden.shape[1]
    width = half_width * lax.axis_size("half")
    normed = (hidden * lax.rsqrt(squares / width + EPSILON)[:, None] * norm_gain[None, :]).astype(
        jnp.bfloat16
    )
    token_rows, top_count = expert_ids.shape
    ep_count = lax.axis_size("ep")
    tp_count = lax.axis_size("tp")
    local_experts = w_gate.shape[0]
    capacity = token_rows * top_count * 3 // (2 * EXPERTS)
    slot_count = ep_count * local_experts * capacity
    flat_ids = expert_ids.reshape(-1)
    one_hot = (flat_ids[:, None] == lax.iota(jnp.int32, EXPERTS)[None, :]).astype(jnp.int32)
    earlier = jnp.cumsum(one_hot, axis=0) - one_hot
    slot = jnp.sum(earlier * one_hot, axis=1)
    owner_ep = flat_ids // (local_experts * tp_count)
    owner_tp = flat_ids // local_experts % tp_count
    target = owner_ep * (local_experts * capacity) + flat_ids % local_experts * capacity + slot
    target = jnp.where(owner_tp == lax.axis_index("tp"), target, -1).reshape(token_rows, top_count)
    dispatch_matrix = jnp.any(
        lax.iota(jnp.int32, slot_count)[:, None, None] == target[None, :, :], axis=2
    ).astype(jnp.bfloat16)
    gates = gate_weights / jnp.sum(gate_weights, axis=1, keepdims=True)
    full_rows = lax.all_gather(normed, "half", axis=1, tiled=True)
    outgoing = jnp.dot(dispatch_matrix, full_rows, preferred_element_type=jnp.float32).astype(
        jnp.bfloat16
    )
    arrived = lax.all_to_all(
        outgoing.reshape(ep_count, local_experts, capacity, width),
        "ep",
        split_axis=0,
        concat_axis=0,
        tiled=True,
    )
    gate_part = jnp.einsum("secd,efd->secf", arrived, w_gate, preferred_element_type=jnp.float32)
    up_part = jnp.einsum("secd,efd->secf", arrived, w_up, preferred_element_type=jnp.float32)
    activation = (jax.nn.silu(gate_part) * up_part).astype(jnp.bfloat16)
    expert_out = jnp.einsum(
        "secf,efd->secd", activation, w_down, preferred_element_type=jnp.float32
    ).astype(jnp.bfloat16)
    summed = lax.psum_scatter(
        expert_out.astype(jnp.float32).astype(jnp.bfloat16), "half", scatter_dimension=3, tiled=True
    ).astype(jnp.float32)
    returned = lax.all_to_all(
        summed.reshape(ep_count, local_experts * capacity, half_width).astype(jnp.bfloat16),
        "ep",
        split_axis=0,
        concat_axis=0,
        tiled=True,
    ).astype(jnp.float32)
    term = combine_rows(returned.reshape(slot_count, half_width), target, gates)
    expert_sum = lax.psum_scatter(
        term.astype(jnp.bfloat16), "tp", scatter_dimension=1, tiled=True
    ).astype(jnp.float32)
    slice_width = expert_sum.shape[1]
    own_columns = lax.dynamic_slice_in_dim(
        hidden, lax.axis_index("tp") * slice_width, slice_width, 1
    )
    return (own_columns + expert_sum).astype(jnp.bfloat16)


VMEM_SPEC = pl.BlockSpec(memory_space=pltpu.VMEM)
SMEM_SPEC = pl.BlockSpec(memory_space=pltpu.SMEM)
NT = (((1,), (1,)), ((), ()))
TN = (((0,), (0,)), ((), ()))
F32 = jnp.float32
BF16 = jnp.bfloat16


def kernel_call(body, name, outs, specs=None, scratch=(), flops=1000, vmem=8, args=()):
    return pl.pallas_call(
        body,
        name=name,
        out_shape=tuple(jax.ShapeDtypeStruct(s, d) for s, d in outs),
        in_specs=specs or [VMEM_SPEC] * len(args),
        out_specs=tuple(VMEM_SPEC for _ in outs),
        scratch_shapes=list(scratch),
        cost_estimate=pl.CostEstimate(flops=flops, bytes_accessed=1000, transcendentals=0),
        compiler_params=pltpu.CompilerParams(vmem_limit_bytes=vmem * MIB),
    )(*args)


def attend_body(sharing, context, len_ref, q_ref, nk_ref, nv_ref, k_ref, v_ref, ids_ref, gw_ref, out_ref, rt_ref):
    requests = q_ref.shape[0]
    head_size = nk_ref.shape[1]
    top_count, token_rows = ids_ref.shape
    group = 8
    rows = group * sharing
    keys = group * context
    score_scale = 1.0 / math.sqrt(head_size)
    row_request = lax.broadcasted_iota(jnp.int32, (rows, 1), 0) % group
    lane = lax.broadcasted_iota(jnp.int32, (rows, keys), 1)
    position = jnp.where(
        lane // context == lax.broadcasted_iota(jnp.int32, (rows, keys), 0) % group,
        lane % context,
        context,
    )
    for j in range(requests // group):
        here = slice(group * j, group * (j + 1))
        q = q_ref[here, :].astype(F32)
        q = jnp.concatenate(
            [q[:, g * head_size : (g + 1) * head_size] for g in range(sharing)], axis=0
        )
        own_key = jnp.concatenate([nk_ref[here, :].astype(F32)] * sharing, axis=0)
        own_value = jnp.concatenate([nv_ref[here, :].astype(F32)] * sharing, axis=0)
        length = jnp.zeros((rows, 1), jnp.int32)
        for r in range(group):
            length = jnp.where(row_request == r, len_ref[group * j + r], length)
        scores = (
            lax.dot_general(
                q.astype(BF16), k_ref[keys * j : keys * (j + 1), :], NT, preferred_element_type=F32
            )
            * score_scale
        )
        scores = jnp.where(position < length, scores, -1e30)
        own_score = jnp.sum(q * own_key, axis=1, keepdims=True) * score_scale
        highest = jnp.maximum(jnp.max(scores, axis=1, keepdims=True), own_score)
        weights = jnp.exp(scores - highest)
        own_weight = jnp.exp(own_score - highest)
        inverse = 1.0 / (jnp.sum(weights, axis=1, keepdims=True) + own_weight)
        probs = (weights * inverse).astype(BF16)
        own_prob = (own_weight * inverse).astype(BF16).astype(F32)
        mixture = jnp.dot(probs, v_ref[keys * j : keys * (j + 1), :], preferred_element_type=F32)
        mixture = (mixture + own_prob * own_value).astype(BF16)
        for g in range(sharing):
            out_ref[here, g * head_size : (g + 1) * head_size] = mixture[group * g : group * (g + 1), :]
    gw = gw_ref[...]
    rt_ref[...] = jnp.zeros(rt_ref.shape, F32)
    rt_ref[0:top_count, 0:token_rows] = ids_ref[...].astype(F32)
    rt_ref[top_count : 2 * top_count, 0:token_rows] = gw / jnp.sum(gw, axis=0, keepdims=True)


def project_body(own_ref, other_ref, w_ref, keep_ref, send_ref, rows_ref):
    x = lax.axis_index("half")
    t = lax.axis_index("tp")
    count = own_ref.shape[0]
    cols = keep_ref.shape[1]
    rows_ref[pl.ds(pl.multiple_of(x * count, count), count), :] = own_ref[...]
    rows_ref[pl.ds(pl.multiple_of((1 - x) * count, count), count), :] = other_ref[...]
    rows = rows_ref[...]
    send_ref[...] = jnp.dot(
        rows, w_ref[:, pl.ds(pl.multiple_of((1 - t) * cols, cols), cols)], preferred_element_type=F32
    )
    keep_ref[...] = jnp.dot(
        rows, w_ref[:, pl.ds(pl.multiple_of(t * cols, cols), cols)], preferred_element_type=F32
    )


def hidden_body(res_ref, keep_ref, got_ref, h32_ref, h16_ref):
    t = lax.axis_index("tp")
    cols = keep_ref.shape[1]
    res = res_ref[:, pl.ds(pl.multiple_of(t * cols, cols), cols)]
    hidden = res.astype(F32) + (keep_ref[...] + got_ref[...])
    h32_ref[...] = hidden
    h16_ref[...] = hidden.astype(BF16)


def place_columns(x_ref, mine, theirs):
    t = lax.axis_index("tp")
    for j, (a, b) in enumerate(zip(mine, theirs)):
        rows, cols = a.shape
        x_ref[rows * j : rows * (j + 1), pl.ds(pl.multiple_of(t * cols, cols), cols)] = a[...]
        x_ref[rows * j : rows * (j + 1), pl.ds(pl.multiple_of((1 - t) * cols, cols), cols)] = b[...]


def gathered_rows(pick, x_ref, gain_ref):
    rows = jnp.dot(pick, x_ref[...], preferred_element_type=F32)
    squares = jnp.sum(rows * rows, axis=1, keepdims=True)
    return (rows * gain_ref[...]).astype(BF16), squares


def first_half_body(
    blocks, top_count, *refs
):
    mine, theirs, routes = refs[:blocks], refs[blocks : 2 * blocks], refs[2 * blocks : 3 * blocks]
    gain_ref, wg_ref, wu_ref = refs[3 * blocks : 3 * blocks + 3]
    pick_ref, gate_ref, squares_ref, ga_ref, ua_ref, x_ref, rows_ref = refs[3 * blocks + 3 :]
    experts, hidden_units, width = wg_ref.shape
    half_width = x_ref.shape[1]
    token_rows = mine[0].shape[0]
    tokens = token_rows * blocks
    slots = pick_ref.shape[0] // experts
    place_columns(x_ref, mine, theirs)
    lanes = routes[0].shape[1]
    low = lax.broadcasted_iota(jnp.int32, routes[0].shape, 1) < token_rows
    pairs = [
        jnp.where(low, routes[j][...], pltpu.roll(routes[j + 1][...], lanes - token_rows, 1))
        for j in range(0, blocks, 2)
    ]
    table = jnp.concatenate(pairs, axis=1)
    ids, gates = table[:top_count], table[top_count : 2 * top_count]
    first = (lax.axis_index("ep") * lax.axis_size("tp") + lax.axis_index("tp")) * experts
    number = (first + lax.broadcasted_iota(jnp.int32, (experts, top_count, tokens), 0)).astype(F32)
    named = ids[None] == number
    chosen = jnp.sum(jnp.where(named, 1.0, 0.0), axis=1)
    gate = jnp.sum(jnp.where(named, gates[None], 0.0), axis=1)
    before = (
        lax.broadcasted_iota(jnp.int32, (tokens, tokens), 0)
        < lax.broadcasted_iota(jnp.int32, (tokens, tokens), 1)
    )
    earlier = jnp.dot(
        chosen.astype(BF16), jnp.where(before, 1.0, 0.0).astype(BF16), preferred_element_type=F32
    )
    place = jnp.where(chosen > 0.0, earlier, -1.0)
    slot = lax.broadcasted_iota(jnp.int32, (experts, slots, tokens), 1).astype(F32)
    pick = jnp.where(slot == place[:, None, :], 1.0, 0.0)
    gate_ref[...] = jnp.sum(pick * gate[:, None, :], axis=2, keepdims=True).reshape(
        experts * slots, 1
    )
    pick_ref[...] = pick.reshape(experts * slots, tokens).astype(BF16)
    rows, squares = gathered_rows(pick_ref[...], x_ref, gain_ref)
    squares_ref[...] = squares
    rows_ref[...] = rows
    start = pl.multiple_of(lax.axis_index("half") * half_width, half_width)

    def one(e, carry):
        here = pl.ds(pl.multiple_of(e * slots, slots), slots)
        part = rows_ref[here, :]
        ga_ref[here, :] = lax.dot_general(
            part, wg_ref[e, :, pl.ds(start, half_width)], NT, preferred_element_type=F32
        )
        ua_ref[here, :] = lax.dot_general(
            part, wu_ref[e, :, pl.ds(start, half_width)], NT, preferred_element_type=F32
        )
        return carry

    lax.fori_loop(0, experts, one, 0, unroll=2)


def weigh(pick_ref, y_ref, keep_ref, send_ref):
    t = lax.axis_index("tp")
    cols = keep_ref.shape[1]
    pick = pick_ref[...]
    send_ref[...] = lax.dot_general(
        pick, y_ref[:, pl.ds(pl.multiple_of((1 - t) * cols, cols), cols)], TN, preferred_element_type=F32
    ).astype(BF16)
    keep_ref[...] = lax.dot_general(
        pick, y_ref[:, pl.ds(pl.multiple_of(t * cols, cols), cols)], TN, preferred_element_type=F32
    )


def second_half_body(blocks, *refs):
    mine, theirs = refs[:blocks], refs[blocks : 2 * blocks]
    (gain_ref, wg_ref, wu_ref, wd_ref, pick_ref, gate_ref, squares_ref, ga_ref, ua_ref) = refs[
        2 * blocks : 2 * blocks + 9
    ]
    act_ref, keep_ref, send_ref, x_ref, rows_ref, y_ref, inv_ref = refs[2 * blocks + 9 :]
    experts, hidden_units, width = wg_ref.shape
    half_width = x_ref.shape[1]
    slots = pick_ref.shape[0] // experts
    place_columns(x_ref, mine, theirs)
    rows, squares = gathered_rows(pick_ref[...], x_ref, gain_ref)
    inv_ref[...] = lax.rsqrt((squares_ref[...] + squares) / width + EPSILON)
    rows_ref[...] = rows
    start = pl.multiple_of((1 - lax.axis_index("half")) * half_width, half_width)

    def one(e, carry):
        here = pl.ds(pl.multiple_of(e * slots, slots), slots)
        part = rows_ref[here, :]
        inverse = inv_ref[here, :]
        gate_part = inverse * (
            ga_ref[here, :]
            + lax.dot_general(
                part, wg_ref[e, :, pl.ds(start, half_width)], NT, preferred_element_type=F32
            )
        )
        up_part = inverse * (
            ua_ref[here, :]
            + lax.dot_general(
                part, wu_ref[e, :, pl.ds(start, half_width)], NT, preferred_element_type=F32
            )
        )
        act = (jax.nn.silu(gate_part) * up_part).astype(BF16)
        act_ref[here, :] = act
        y = jnp.dot(act, wd_ref[e, :, pl.ds(start, half_width)], preferred_element_type=F32)
        y_ref[here, :] = (y * gate_ref[here, :]).astype(BF16)
        return carry

    lax.fori_loop(0, experts, one, 0, unroll=2)
    weigh(pick_ref, y_ref, keep_ref, send_ref)


def down_body(wd_ref, pick_ref, gate_ref, act_ref, keep_ref, send_ref, y_ref):
    experts, hidden_units, width = wd_ref.shape
    half_width = y_ref.shape[1]
    slots = pick_ref.shape[0] // experts
    start = pl.multiple_of(lax.axis_index("half") * half_width, half_width)

    def one(e, carry):
        here = pl.ds(pl.multiple_of(e * slots, slots), slots)
        y = jnp.dot(
            act_ref[here, :], wd_ref[e, :, pl.ds(start, half_width)], preferred_element_type=F32
        )
        y_ref[here, :] = (y * gate_ref[here, :]).astype(BF16)
        return carry

    lax.fori_loop(0, experts, one, 0, unroll=2)
    weigh(pick_ref, y_ref, keep_ref, send_ref)


def pair_sum_body(keep_ref, got_ref, *outs):
    rows = outs[0].shape[0]
    for j, out in enumerate(outs):
        here = slice(rows * j, rows * (j + 1))
        out[...] = (keep_ref[here, :] + got_ref[here, :].astype(F32)).astype(BF16)


def block_sum_body(j, keep_ref, got_ref, other_ref, out_ref):
    rows = out_ref.shape[0]
    here = slice(rows * j, rows * (j + 1))
    total = keep_ref[here, :] + got_ref[here, :].astype(F32) + other_ref[...].astype(F32)
    out_ref[...] = total.astype(BF16)


def final_body(h32_ref, keep_ref, got_ref, other_ref, *refs):
    out_ref = refs[-1]
    rows = out_ref.shape[0]
    total = keep_ref[0:rows, :] + got_ref[0:rows, :].astype(F32) + other_ref[...].astype(F32)
    for ref in refs[:-1]:
        total = total + ref[...].astype(F32)
    out_ref[...] = (h32_ref[...] + total).astype(BF16)


def shift(value, axis, step):
    count = lax.axis_size(axis)
    return lax.ppermute(value, axis, [(i, (i + step) % count) for i in range(count)])


def by_rows(
    queries,
    new_keys,
    new_values,
    cache_keys,
    cache_values,
    lengths,
    out_weight,
    residual,
    norm_gain,
    expert_ids,
    gate_weights,
    w_gate,
    w_up,
    w_down,
):
    requests, _, context, head_size = cache_keys.shape
    sharing = queries.shape[1] // head_size
    token_rows, top_count = expert_ids.shape
    blocks = lax.axis_size("ep")
    tokens = blocks * token_rows
    experts, hidden_units, width = w_gate.shape
    half_width = residual.shape[1]
    cols = half_width // lax.axis_size("tp")
    slots = token_rows * top_count * 3 // (2 * EXPERTS) * blocks
    lanes = 128

    gain = norm_gain.reshape(1, half_width)
    other_gain = shift(gain, "half", 1)
    args = (
        lengths,
        queries,
        new_keys,
        new_values,
        cache_keys.reshape(requests * context, head_size),
        cache_values.reshape(requests * context, head_size),
        expert_ids.T,
        gate_weights.T,
    )
    attended, route = kernel_call(
        functools.partial(attend_body, sharing, context),
        "attend",
        [((requests, sharing * head_size), BF16), ((2 * top_count, lanes), F32)],
        specs=[SMEM_SPEC] + [VMEM_SPEC] * 7,
        flops=10**11,
        args=args,
    )
    other_attended = shift(attended, "half", 1)
    routes = [route] + [shift(route, "ep", j) for j in range(1, blocks)]
    keep, send = kernel_call(
        project_body,
        "project",
        [((token_rows, cols), F32)] * 2,
        scratch=[pltpu.VMEM((token_rows, sharing * head_size), BF16)],
        args=(attended, other_attended, out_weight),
    )
    h32, h16 = kernel_call(
        hidden_body,
        "hidden",
        [((token_rows, cols), F32), ((token_rows, cols), BF16)],
        args=(residual, keep, shift(send, "tp", 1)),
    )
    mine = [h16] + [shift(h16, "ep", j) for j in range(1, blocks)]
    mine_x = [shift(b, "half", 1) for b in mine]
    theirs = [shift(b, "tp", 1) for b in mine]
    theirs_x = [shift(b, "tp", 1) for b in mine_x]

    slot_rows = experts * slots
    pick, gate, squares, gate_acc, up_acc = kernel_call(
        functools.partial(first_half_body, blocks, top_count),
        "first_half",
        [
            ((slot_rows, tokens), BF16),
            ((slot_rows, 1), F32),
            ((slot_rows, 1), F32),
            ((slot_rows, hidden_units), F32),
            ((slot_rows, hidden_units), F32),
        ],
        scratch=[pltpu.VMEM((tokens, half_width), BF16), pltpu.VMEM((slot_rows, half_width), BF16)],
        vmem=14,
        args=(*mine, *theirs, *routes, gain, w_gate, w_up),
    )
    act, keep_a, send_a = kernel_call(
        functools.partial(second_half_body, blocks),
        "second_half",
        [((slot_rows, hidden_units), BF16), ((tokens, cols), F32), ((tokens, cols), BF16)],
        scratch=[
            pltpu.VMEM((tokens, half_width), BF16),
            pltpu.VMEM((slot_rows, half_width), BF16),
            pltpu.VMEM((slot_rows, half_width), BF16),
            pltpu.VMEM((slot_rows, 1), F32),
        ],
        vmem=14,
        args=(
            *mine_x, *theirs_x, other_gain, w_gate, w_up, w_down, pick, gate, squares, gate_acc, up_acc,
        ),
    )
    got_a = shift(send_a, "tp", 1)
    to_x = kernel_call(
        pair_sum_body, "pair_sum", [((token_rows, cols), BF16)] * blocks, args=(keep_a, got_a)
    )
    from_x = [None] * blocks
    for j in list(range(1, blocks)) + [0]:
        from_x[j] = shift(to_x[j], "half", 1)
    keep_b, send_b = kernel_call(
        down_body,
        "down",
        [((tokens, cols), F32), ((tokens, cols), BF16)],
        scratch=[pltpu.VMEM((slot_rows, half_width), BF16)],
        vmem=14,
        args=(w_down, pick, gate, act),
    )
    got_b = shift(send_b, "tp", 1)
    home = []
    for j in range(1, blocks):
        (total,) = kernel_call(
            functools.partial(block_sum_body, j),
            f"block_sum_{j}",
            [((token_rows, cols), BF16)],
            args=(keep_b, got_b, from_x[j]),
        )
        home.append(shift(total, "ep", -j))
    (out,) = kernel_call(
        final_body,
        "final",
        [((token_rows, cols), BF16)],
        args=(h32, keep_b, got_b, from_x[0], *home),
    )
    return out


def solution(mesh):
    placed = (
        P(("groups", "ep", "half"), "tp"),
        P(("groups", "ep", "half"), "tp"),
        P(("groups", "ep", "half"), "tp"),
        P(("groups", "ep", "half"), "tp", None, None),
        P(("groups", "ep", "half"), "tp", None, None),
        P(("groups", "ep", "half")),
        P("tp", "half"),
        P(("groups", "ep"), "half"),
        P("half"),
        P(("groups", "ep"), None),
        P(("groups", "ep"), None),
        P(("ep", "tp"), "half", None),
        P(("ep", "tp"), "half", None),
        P(("ep", "tp"), "half", None),
    )
    few = mesh.shape["half"] == 2 and mesh.shape["tp"] == 2 and mesh.shape["ep"] in (2, 4)

    def on_device(*args):
        fits = args[9].shape[0] == 64 and args[11].shape[2] == 2 * args[7].shape[1]
        return by_rows(*args) if few and fits else by_slots(*args)

    return jax.shard_map(
        on_device,
        mesh=mesh,
        in_specs=placed,
        out_specs=P(("groups", "ep"), ("half", "tp")),
        check_vma=False,
    )
```

```python
import functools
import math

import jax
import jax.numpy as jnp
from jax import lax
from jax.experimental import pallas as pl
from jax.experimental.pallas import tpu as pltpu
from jax.sharding import PartitionSpec as P

EXPERTS = 64


EPSILON = 1e-06

MIB = 2**20


def attend(queries, new_keys, new_values, cache_keys, cache_values, lengths):
    requests, key_heads, context, head_size = cache_keys.shape
    sharing = queries.shape[1] // (key_heads * head_size)
    query_blocks = queries.reshape(requests, key_heads, sharing, head_size)
    score_scale = 1.0 / math.sqrt(head_size)
    scores = (
        jnp.einsum("rkgd,rkcd->rkgc", query_blocks, cache_keys, preferred_element_type=jnp.float32)
        * score_scale
    )
    own_score = (
        jnp.einsum(
            "rkgd,rkd->rkg",
            query_blocks,
            new_keys.reshape(requests, key_heads, head_size),
            preferred_element_type=jnp.float32,
        )
        * score_scale
    )
    valid = lax.iota(jnp.int32, context)[None, :] < lengths[:, None]
    scores = jnp.where(valid[:, None, None, :], scores, -1e30)
    highest = jnp.maximum(jnp.max(scores, axis=-1), own_score)
    weights = jnp.exp(scores - highest[..., None])
    own_weight = jnp.exp(own_score - highest)
    denominator = jnp.sum(weights, axis=-1) + own_weight
    probs = (weights / denominator[..., None]).astype(jnp.bfloat16)
    own_prob = (own_weight / denominator).astype(jnp.bfloat16)
    mixture = jnp.einsum("rkgc,rkcd->rkgd", probs, cache_values, preferred_element_type=jnp.float32)
    mixture = mixture + own_prob.astype(jnp.float32)[..., None] * new_values.reshape(
        requests, key_heads, 1, head_size
    ).astype(jnp.float32)
    return mixture.astype(jnp.bfloat16).reshape(requests, key_heads * sharing * head_size)


def combine_rows(returned_rows, target, gates):
    token_rows, top_count = target.shape
    safe_target = jnp.maximum(target, 0).reshape(-1)
    picked = jnp.take(returned_rows, safe_target, axis=0).reshape(
        token_rows, top_count, returned_rows.shape[1]
    )
    weighting = jnp.where(target >= 0, gates, 0.0)
    return jnp.sum(picked.astype(jnp.float32) * weighting[..., None], axis=1)


def by_slots(
    queries,
    new_keys,
    new_values,
    cache_keys,
    cache_values,
    lengths,
    out_weight,
    residual,
    norm_gain,
    expert_ids,
    gate_weights,
    w_gate,
    w_up,
    w_down,
):
    attended = attend(queries, new_keys, new_values, cache_keys, cache_values, lengths)
    partial_mix = jnp.dot(
        lax.all_gather(attended, "half", axis=0, tiled=True),
        out_weight,
        preferred_element_type=jnp.float32,
    )
    mixed = lax.psum(partial_mix.astype(jnp.bfloat16), "tp").astype(jnp.float32)
    hidden = residual.astype(jnp.float32) + mixed
    squares = lax.psum(jnp.sum(hidden * hidden, axis=1), "half")
    half_width = hidden.shape[1]
    width = half_width * lax.axis_size("half")
    normed = (hidden * lax.rsqrt(squares / width + EPSILON)[:, None] * norm_gain[None, :]).astype(
        jnp.bfloat16
    )
    token_rows, top_count = expert_ids.shape
    ep_count = lax.axis_size("ep")
    tp_count = lax.axis_size("tp")
    local_experts = w_gate.shape[0]
    capacity = token_rows * top_count * 3 // (2 * EXPERTS)
    slot_count = ep_count * local_experts * capacity
    flat_ids = expert_ids.reshape(-1)
    one_hot = (flat_ids[:, None] == lax.iota(jnp.int32, EXPERTS)[None, :]).astype(jnp.int32)
    earlier = jnp.cumsum(one_hot, axis=0) - one_hot
    slot = jnp.sum(earlier * one_hot, axis=1)
    owner_ep = flat_ids // (local_experts * tp_count)
    owner_tp = flat_ids // local_experts % tp_count
    target = owner_ep * (local_experts * capacity) + flat_ids % local_experts * capacity + slot
    target = jnp.where(owner_tp == lax.axis_index("tp"), target, -1).reshape(token_rows, top_count)
    dispatch_matrix = jnp.any(
        lax.iota(jnp.int32, slot_count)[:, None, None] == target[None, :, :], axis=2
    ).astype(jnp.bfloat16)
    gates = gate_weights / jnp.sum(gate_weights, axis=1, keepdims=True)
    full_rows = lax.all_gather(normed, "half", axis=1, tiled=True)
    outgoing = jnp.dot(dispatch_matrix, full_rows, preferred_element_type=jnp.float32).astype(
        jnp.bfloat16
    )
    arrived = lax.all_to_all(
        outgoing.reshape(ep_count, local_experts, capacity, width),
        "ep",
        split_axis=0,
        concat_axis=0,
        tiled=True,
    )
    gate_part = jnp.einsum("secd,efd->secf", arrived, w_gate, preferred_element_type=jnp.float32)
    up_part = jnp.einsum("secd,efd->secf", arrived, w_up, preferred_element_type=jnp.float32)
    activation = (jax.nn.silu(gate_part) * up_part).astype(jnp.bfloat16)
    expert_out = jnp.einsum(
        "secf,efd->secd", activation, w_down, preferred_element_type=jnp.float32
    ).astype(jnp.bfloat16)
    summed = lax.psum_scatter(
        expert_out.astype(jnp.float32).astype(jnp.bfloat16), "half", scatter_dimension=3, tiled=True
    ).astype(jnp.float32)
    returned = lax.all_to_all(
        summed.reshape(ep_count, local_experts * capacity, half_width).astype(jnp.bfloat16),
        "ep",
        split_axis=0,
        concat_axis=0,
        tiled=True,
    ).astype(jnp.float32)
    term = combine_rows(returned.reshape(slot_count, half_width), target, gates)
    expert_sum = lax.psum_scatter(
        term.astype(jnp.bfloat16), "tp", scatter_dimension=1, tiled=True
    ).astype(jnp.float32)
    slice_width = expert_sum.shape[1]
    own_columns = lax.dynamic_slice_in_dim(
        hidden, lax.axis_index("tp") * slice_width, slice_width, 1
    )
    return (own_columns + expert_sum).astype(jnp.bfloat16)


VMEM_SPEC = pl.BlockSpec(memory_space=pltpu.VMEM)
HBM_SPEC = pl.BlockSpec(memory_space=pltpu.HBM)
SMEM_SPEC = pl.BlockSpec(memory_space=pltpu.SMEM)
NT = (((1,), (1,)), ((), ()))
TN = (((0,), (0,)), ((), ()))
F32 = jnp.float32
BF16 = jnp.bfloat16


def kernel_call(body, name, outs, specs=None, scratch=(), flops=1000, vmem=8, args=()):
    return pl.pallas_call(
        body,
        name=name,
        out_shape=tuple(jax.ShapeDtypeStruct(s, d) for s, d in outs),
        in_specs=specs or [VMEM_SPEC] * len(args),
        out_specs=tuple(VMEM_SPEC for _ in outs),
        scratch_shapes=list(scratch),
        cost_estimate=pl.CostEstimate(flops=flops, bytes_accessed=1000, transcendentals=0),
        compiler_params=pltpu.CompilerParams(vmem_limit_bytes=vmem * MIB),
    )(*args)


def attend_body(sharing, context, len_ref, *refs):
    sources, (out_ref,), buffers, sems = refs[:5], refs[5:6], refs[6:11], refs[11]
    copies = [
        pltpu.make_async_copy(source, buffer, sems.at[i])
        for i, (source, buffer) in enumerate(zip(sources, buffers))
    ]
    for copy in copies:
        copy.start()
    for copy in copies:
        copy.wait()
    q_ref, nk_ref, nv_ref, k_ref, v_ref = buffers
    requests = q_ref.shape[0]
    head_size = nk_ref.shape[1]
    group = 8
    rows = group * sharing
    keys = group * context
    score_scale = 1.0 / math.sqrt(head_size)
    row_request = lax.broadcasted_iota(jnp.int32, (rows, 1), 0) % group
    lane = lax.broadcasted_iota(jnp.int32, (rows, keys), 1)
    position = jnp.where(
        lane // context == lax.broadcasted_iota(jnp.int32, (rows, keys), 0) % group,
        lane % context,
        context,
    )
    for j in range(requests // group):
        here = slice(group * j, group * (j + 1))
        q = q_ref[here, :].astype(F32)
        q = jnp.concatenate(
            [q[:, g * head_size : (g + 1) * head_size] for g in range(sharing)], axis=0
        )
        own_key = jnp.concatenate([nk_ref[here, :].astype(F32)] * sharing, axis=0)
        own_value = jnp.concatenate([nv_ref[here, :].astype(F32)] * sharing, axis=0)
        length = jnp.zeros((rows, 1), jnp.int32)
        for r in range(group):
            length = jnp.where(row_request == r, len_ref[group * j + r], length)
        scores = (
            lax.dot_general(
                q.astype(BF16), k_ref[keys * j : keys * (j + 1), :], NT, preferred_element_type=F32
            )
            * score_scale
        )
        scores = jnp.where(position < length, scores, -1e30)
        own_score = jnp.sum(q * own_key, axis=1, keepdims=True) * score_scale
        highest = jnp.maximum(jnp.max(scores, axis=1, keepdims=True), own_score)
        weights = jnp.exp(scores - highest)
        own_weight = jnp.exp(own_score - highest)
        inverse = 1.0 / (jnp.sum(weights, axis=1, keepdims=True) + own_weight)
        probs = (weights * inverse).astype(BF16)
        own_prob = (own_weight * inverse).astype(BF16).astype(F32)
        mixture = jnp.dot(probs, v_ref[keys * j : keys * (j + 1), :], preferred_element_type=F32)
        mixture = (mixture + own_prob * own_value).astype(BF16)
        for g in range(sharing):
            out_ref[here, g * head_size : (g + 1) * head_size] = mixture[group * g : group * (g + 1), :]


def route_body(ids_ref, gw_ref, rt_ref):
    top_count, token_rows = ids_ref.shape
    gw = gw_ref[...]
    rt_ref[...] = jnp.zeros(rt_ref.shape, F32)
    rt_ref[0:top_count, 0:token_rows] = ids_ref[...].astype(F32)
    rt_ref[top_count : 2 * top_count, 0:token_rows] = gw / jnp.sum(gw, axis=0, keepdims=True)


def project_body(own_ref, other_ref, w_ref, keep_ref, send_ref, rows_ref):
    x = lax.axis_index("half")
    t = lax.axis_index("tp")
    count = own_ref.shape[0]
    cols = keep_ref.shape[1]
    rows_ref[pl.ds(pl.multiple_of(x * count, count), count), :] = own_ref[...]
    rows_ref[pl.ds(pl.multiple_of((1 - x) * count, count), count), :] = other_ref[...]
    rows = rows_ref[...]
    send_ref[...] = jnp.dot(
        rows, w_ref[:, pl.ds(pl.multiple_of((1 - t) * cols, cols), cols)], preferred_element_type=F32
    )
    keep_ref[...] = jnp.dot(
        rows, w_ref[:, pl.ds(pl.multiple_of(t * cols, cols), cols)], preferred_element_type=F32
    )


def hidden_body(res_ref, keep_ref, got_ref, h32_ref, h16_ref):
    t = lax.axis_index("tp")
    cols = keep_ref.shape[1]
    res = res_ref[:, pl.ds(pl.multiple_of(t * cols, cols), cols)]
    hidden = res.astype(F32) + (keep_ref[...] + got_ref[...])
    h32_ref[...] = hidden
    h16_ref[...] = hidden.astype(BF16)


def merge_body(blocks, *refs):
    rows = refs[0].shape[0]
    all_ref, on_ref = refs[-2:]
    for j in range(blocks):
        all_ref[rows * j : rows * (j + 1), :] = refs[j][...]
        if j > 0:
            on_ref[rows * (j - 1) : rows * j, :] = refs[j][...]


def join_body(first_ref, rest_ref, out_ref):
    rows = first_ref.shape[0]
    out_ref[0:rows, :] = first_ref[...]
    out_ref[rows:, :] = rest_ref[...]


def pick_body(blocks, top_count, *refs):
    routes = refs[:blocks]
    token_rows, pick_ref, gate_ref = refs[blocks].shape[0], refs[blocks + 1], refs[blocks + 2]
    slot_rows, tokens = pick_ref.shape
    experts = EXPERTS // (lax.axis_size("ep") * lax.axis_size("tp"))
    slots = slot_rows // experts
    lanes = routes[0].shape[1]
    low = lax.broadcasted_iota(jnp.int32, routes[0].shape, 1) < token_rows
    pairs = [
        jnp.where(low, routes[j][...], pltpu.roll(routes[j + 1][...], lanes - token_rows, 1))
        for j in range(0, blocks, 2)
    ]
    table = jnp.concatenate(pairs, axis=1)
    ids, gates = table[:top_count], table[top_count : 2 * top_count]
    first = (lax.axis_index("ep") * lax.axis_size("tp") + lax.axis_index("tp")) * experts
    number = (first + lax.broadcasted_iota(jnp.int32, (experts, top_count, tokens), 0)).astype(F32)
    named = ids[None] == number
    chosen = jnp.sum(jnp.where(named, 1.0, 0.0), axis=1)
    gate = jnp.sum(jnp.where(named, gates[None], 0.0), axis=1)
    before = (
        lax.broadcasted_iota(jnp.int32, (tokens, tokens), 0)
        < lax.broadcasted_iota(jnp.int32, (tokens, tokens), 1)
    )
    earlier = jnp.dot(
        chosen.astype(BF16), jnp.where(before, 1.0, 0.0).astype(BF16), preferred_element_type=F32
    )
    place = jnp.where(chosen > 0.0, earlier, -1.0)
    slot = lax.broadcasted_iota(jnp.int32, (experts, slots, tokens), 1).astype(F32)
    pick = jnp.where(slot == place[:, None, :], 1.0, 0.0)
    gate_ref[...] = jnp.sum(pick * gate[:, None, :], axis=2, keepdims=True).reshape(
        slot_rows, 1
    )
    pick_ref[...] = pick.reshape(slot_rows, tokens).astype(BF16)


def gathered_rows(pick, mine_ref, theirs_ref, gain_ref, rows_ref):
    cols = mine_ref.shape[1]
    t = lax.axis_index("tp")
    total = 0.0
    for owner, ref in ((t, mine_ref), (1 - t, theirs_ref)):
        here = pl.ds(pl.multiple_of(owner * cols, cols), cols)
        rows = jnp.dot(pick, ref[...], preferred_element_type=F32)
        total = total + jnp.sum(rows * rows, axis=1, keepdims=True)
        rows_ref[:, here] = (rows * gain_ref[:, here]).astype(BF16)
    return total


def first_half_body(
    mine_ref, theirs_ref, gain_ref, wg_ref, wu_ref, pick_ref, squares_ref, ga_ref, ua_ref, rows_ref
):
    experts = wg_ref.shape[0]
    half_width = rows_ref.shape[1]
    slots = pick_ref.shape[0] // experts
    squares_ref[...] = gathered_rows(pick_ref[...], mine_ref, theirs_ref, gain_ref, rows_ref)
    start = pl.multiple_of(lax.axis_index("half") * half_width, half_width)

    def one(e, carry):
        here = pl.ds(pl.multiple_of(e * slots, slots), slots)
        part = rows_ref[here, :]
        ga_ref[here, :] = lax.dot_general(
            part, wg_ref[e, :, pl.ds(start, half_width)], NT, preferred_element_type=F32
        )
        ua_ref[here, :] = lax.dot_general(
            part, wu_ref[e, :, pl.ds(start, half_width)], NT, preferred_element_type=F32
        )
        return carry

    lax.fori_loop(0, experts, one, 0, unroll=2)


def second_half_body(
    mine_ref, theirs_ref, gain_ref, wg_ref, wu_ref, pick_ref, squares_ref, ga_ref, ua_ref,
    act_ref, rows_ref, inv_ref,
):
    experts, hidden_units, width = wg_ref.shape
    half_width = rows_ref.shape[1]
    slots = pick_ref.shape[0] // experts
    squares = gathered_rows(pick_ref[...], mine_ref, theirs_ref, gain_ref, rows_ref)
    inv_ref[...] = lax.rsqrt((squares_ref[...] + squares) / width + EPSILON)
    start = pl.multiple_of((1 - lax.axis_index("half")) * half_width, half_width)

    def one(e, carry):
        here = pl.ds(pl.multiple_of(e * slots, slots), slots)
        part = rows_ref[here, :]
        inverse = inv_ref[here, :]
        gate_part = inverse * (
            ga_ref[here, :]
            + lax.dot_general(
                part, wg_ref[e, :, pl.ds(start, half_width)], NT, preferred_element_type=F32
            )
        )
        up_part = inverse * (
            ua_ref[here, :]
            + lax.dot_general(
                part, wu_ref[e, :, pl.ds(start, half_width)], NT, preferred_element_type=F32
            )
        )
        act_ref[here, :] = (jax.nn.silu(gate_part) * up_part).astype(BF16)
        return carry

    lax.fori_loop(0, experts, one, 0, unroll=2)


def down_body(other_half, other_core, act_ref, gate_ref, pick_ref, wd_ref, out_ref, y_ref):
    experts = wd_ref.shape[0]
    cols = out_ref.shape[1]
    slots = pick_ref.shape[0] // experts
    x, t = lax.axis_index("half"), lax.axis_index("tp")
    quarter = (1 - x if other_half else x) * lax.axis_size("tp") + (1 - t if other_core else t)
    columns = pl.ds(pl.multiple_of(quarter * cols, cols), cols)

    def one(e, carry):
        here = pl.ds(pl.multiple_of(e * slots, slots), slots)
        y = jnp.dot(act_ref[here, :], wd_ref[e, :, columns], preferred_element_type=F32)
        y_ref[here, :] = (y * gate_ref[here, :]).astype(BF16)
        return carry

    lax.fori_loop(0, experts, one, 0, unroll=4)
    out_ref[...] = lax.dot_general(
        pick_ref[...], y_ref[...], TN, preferred_element_type=F32
    ).astype(out_ref.dtype)


def pair_sum_body(keep_ref, got_ref, far_ref, near_ref):
    rows = near_ref.shape[0]
    for out, start in ((near_ref, 0), (far_ref, rows)):
        here = slice(start, start + out.shape[0])
        out[...] = (keep_ref[here, :] + got_ref[here, :].astype(F32)).astype(BF16)


def block_sum_body(start, keep_ref, got_ref, other_ref, *outs):
    rows = outs[0].shape[0]
    for j, out in enumerate(outs):
        here = slice(start + rows * j, start + rows * (j + 1))
        total = keep_ref[here, :] + got_ref[here, :].astype(F32)
        total = total + other_ref[rows * j : rows * (j + 1), :].astype(F32)
        out[...] = total.astype(out.dtype)


def final_body(h32_ref, own_ref, *refs):
    out_ref = refs[-1]
    total = own_ref[...]
    for ref in refs[:-1]:
        total = total + ref[...].astype(F32)
    out_ref[...] = (h32_ref[...] + total).astype(BF16)


def swap(value, axis, partner=1):
    return lax.ppermute(value, axis, [(i, i ^ partner) for i in range(lax.axis_size(axis))])


def by_rows(
    queries,
    new_keys,
    new_values,
    cache_keys,
    cache_values,
    lengths,
    out_weight,
    residual,
    norm_gain,
    expert_ids,
    gate_weights,
    w_gate,
    w_up,
    w_down,
):
    requests, _, context, head_size = cache_keys.shape
    sharing = queries.shape[1] // head_size
    token_rows, top_count = expert_ids.shape
    blocks = lax.axis_size("ep")
    tokens = blocks * token_rows
    experts, hidden_units, width = w_gate.shape
    half_width = residual.shape[1]
    cols = half_width // lax.axis_size("tp")
    slots = token_rows * top_count * 3 // (2 * EXPERTS) * blocks
    slot_rows = experts * slots
    lanes = 128
    w_gate, w_up, w_down = (
        pltpu.with_memory_space_constraint(w, pltpu.VMEM) for w in (w_gate, w_up, w_down)
    )

    gain = norm_gain.reshape(1, half_width)
    cache = (requests * context, head_size)
    args = (
        lengths,
        queries,
        new_keys,
        new_values,
        cache_keys.reshape(cache),
        cache_values.reshape(cache),
    )
    args = args[:1] + tuple(pltpu.with_memory_space_constraint(v, pltpu.HBM) for v in args[1:])
    (attended,) = kernel_call(
        functools.partial(attend_body, sharing, context),
        "attend",
        [((requests, sharing * head_size), BF16)],
        specs=[SMEM_SPEC] + [HBM_SPEC] * 5,
        scratch=[pltpu.VMEM(v.shape, BF16) for v in args[1:]] + [pltpu.SemaphoreType.DMA((5,))],
        flops=10**11,
        args=args,
    )
    other_attended = swap(attended, "half")
    (route,) = kernel_call(
        route_body,
        "route",
        [((2 * top_count, lanes), F32)],
        args=(expert_ids.T, gate_weights.T),
    )
    keep, send = kernel_call(
        project_body,
        "project",
        [((token_rows, cols), F32)] * 2,
        scratch=[pltpu.VMEM((token_rows, sharing * head_size), BF16)],
        args=(attended, other_attended, out_weight),
    )
    h32, h16 = kernel_call(
        hidden_body,
        "hidden",
        [((token_rows, cols), F32), ((token_rows, cols), BF16)],
        args=(residual, keep, swap(send, "tp")),
    )
    arrived = [h16] + [swap(h16, "ep", j) for j in range(1, blocks)]
    first_x = swap(h16, "half")
    routes = [route] + [swap(route, "ep", j) for j in range(1, blocks)]
    other_gain = swap(gain, "half")
    tied = lax.optimization_barrier((*arrived, *routes, other_gain, first_x))
    arrived, routes = tied[:blocks], tied[blocks : 2 * blocks]
    other_gain, first_x = tied[2 * blocks :]
    mine, on = kernel_call(
        functools.partial(merge_body, blocks),
        "merge",
        [((tokens, cols), BF16), ((tokens - token_rows, cols), BF16)],
        args=arrived,
    )
    theirs = swap(mine, "tp")
    rest_x = swap(on, "half")
    pick, gate = kernel_call(
        functools.partial(pick_body, blocks, top_count),
        "pick",
        [((slot_rows, tokens), BF16), ((slot_rows, 1), F32)],
        args=(*routes, h16),
    )
    squares, gate_acc, up_acc = kernel_call(
        first_half_body,
        "first_half",
        [
            ((slot_rows, 1), F32),
            ((slot_rows, hidden_units), F32),
            ((slot_rows, hidden_units), F32),
        ],
        scratch=[pltpu.VMEM((slot_rows, half_width), BF16)],
        args=(mine, theirs, gain, w_gate, w_up, pick),
    )
    rest_x, squares = lax.optimization_barrier((rest_x, squares))
    (mine_x,) = kernel_call(join_body, "join", [((tokens, cols), BF16)], args=(first_x, rest_x))
    theirs_x = swap(mine_x, "tp")
    (act,) = kernel_call(
        second_half_body,
        "second_half",
        [((slot_rows, hidden_units), BF16)],
        scratch=[pltpu.VMEM((slot_rows, half_width), BF16), pltpu.VMEM((slot_rows, 1), F32)],
        args=(
            mine_x, theirs_x, other_gain, w_gate, w_up, pick, squares, gate_acc, up_acc,
        ),
    )

    def down(act, other_half, other_core):
        return kernel_call(
            functools.partial(down_body, other_half, other_core),
            f"down_{int(other_half)}{int(other_core)}",
            [((tokens, cols), BF16 if other_core else F32)],
            scratch=[pltpu.VMEM((slot_rows, cols), BF16)],
            flops=10**9,
            args=(act, gate, pick, w_down),
        )[0]

    got_a = swap(down(act, True, True), "tp")
    keep_a = down(act, True, False)
    near_rows = tokens // 2
    far, near = kernel_call(
        pair_sum_body,
        "pair_sum",
        [((tokens - near_rows, cols), BF16), ((near_rows, cols), BF16)],
        args=(keep_a, got_a),
    )
    act, far, near = lax.optimization_barrier((act, far, near))
    far_x = swap(far, "half")
    near_x = swap(near, "half")
    got_b = swap(down(act, False, True), "tp")
    keep_b = down(act, False, False)
    far_sums = kernel_call(
        functools.partial(block_sum_body, near_rows),
        "far_sum",
        [((token_rows, cols), BF16)] * (blocks // 2),
        args=(keep_b, got_b, far_x),
    )
    near_sums = kernel_call(
        functools.partial(block_sum_body, 0),
        "near_sum",
        [((token_rows, cols), F32)] + [((token_rows, cols), BF16)] * (blocks // 2 - 1),
        args=(keep_b, got_b, near_x),
    )
    home = [swap(v, "ep", blocks // 2 + j) for j, v in enumerate(far_sums)]
    home += [swap(v, "ep", 1 + j) for j, v in enumerate(near_sums[1:])]
    (out,) = kernel_call(
        final_body,
        "final",
        [((token_rows, cols), BF16)],
        args=(h32, near_sums[0], *home),
    )
    return out


def solution(mesh):
    placed = (
        P(("groups", "ep", "half"), "tp"),
        P(("groups", "ep", "half"), "tp"),
        P(("groups", "ep", "half"), "tp"),
        P(("groups", "ep", "half"), "tp", None, None),
        P(("groups", "ep", "half"), "tp", None, None),
        P(("groups", "ep", "half")),
        P("tp", "half"),
        P(("groups", "ep"), "half"),
        P("half"),
        P(("groups", "ep"), None),
        P(("groups", "ep"), None),
        P(("ep", "tp"), "half", None),
        P(("ep", "tp"), "half", None),
        P(("ep", "tp"), "half", None),
    )
    few = mesh.shape["half"] == 2 and mesh.shape["tp"] == 2 and mesh.shape["ep"] in (2, 4)

    def on_device(*args):
        fits = args[9].shape[0] == 64 and args[11].shape[2] == 2 * args[7].shape[1]
        return by_rows(*args) if few and fits else by_slots(*args)

    return jax.shard_map(
        on_device,
        mesh=mesh,
        in_specs=placed,
        out_specs=P(("groups", "ep"), ("half", "tp")),
        check_vma=False,
    )
```

```python
import functools
import math

import jax
import jax.numpy as jnp
from jax import lax
from jax.experimental import pallas as pl
from jax.experimental.pallas import tpu as pltpu
from jax.sharding import PartitionSpec as P


EXPERTS = 64


EPSILON = 1e-06

MIB = 2**20


def attend(queries, new_keys, new_values, cache_keys, cache_values, lengths):
    requests, key_heads, context, head_size = cache_keys.shape
    sharing = queries.shape[1] // (key_heads * head_size)
    query_blocks = queries.reshape(requests, key_heads, sharing, head_size)
    score_scale = 1.0 / math.sqrt(head_size)
    scores = (
        jnp.einsum("rkgd,rkcd->rkgc", query_blocks, cache_keys, preferred_element_type=jnp.float32)
        * score_scale
    )
    own_score = (
        jnp.einsum(
            "rkgd,rkd->rkg",
            query_blocks,
            new_keys.reshape(requests, key_heads, head_size),
            preferred_element_type=jnp.float32,
        )
        * score_scale
    )
    valid = lax.iota(jnp.int32, context)[None, :] < lengths[:, None]
    scores = jnp.where(valid[:, None, None, :], scores, -1e30)
    highest = jnp.maximum(jnp.max(scores, axis=-1), own_score)
    weights = jnp.exp(scores - highest[..., None])
    own_weight = jnp.exp(own_score - highest)
    denominator = jnp.sum(weights, axis=-1) + own_weight
    probs = (weights / denominator[..., None]).astype(jnp.bfloat16)
    own_prob = (own_weight / denominator).astype(jnp.bfloat16)
    mixture = jnp.einsum("rkgc,rkcd->rkgd", probs, cache_values, preferred_element_type=jnp.float32)
    mixture = mixture + own_prob.astype(jnp.float32)[..., None] * new_values.reshape(
        requests, key_heads, 1, head_size
    ).astype(jnp.float32)
    return mixture.astype(jnp.bfloat16).reshape(requests, key_heads * sharing * head_size)


def combine_rows(returned_rows, target, gates):
    token_rows, top_count = target.shape
    safe_target = jnp.maximum(target, 0).reshape(-1)
    picked = jnp.take(returned_rows, safe_target, axis=0).reshape(
        token_rows, top_count, returned_rows.shape[1]
    )
    weighting = jnp.where(target >= 0, gates, 0.0)
    return jnp.sum(picked.astype(jnp.float32) * weighting[..., None], axis=1)


def by_slots(
    queries,
    new_keys,
    new_values,
    cache_keys,
    cache_values,
    lengths,
    out_weight,
    residual,
    norm_gain,
    expert_ids,
    gate_weights,
    w_gate,
    w_up,
    w_down,
):
    attended = attend(queries, new_keys, new_values, cache_keys, cache_values, lengths)
    partial_mix = jnp.dot(
        lax.all_gather(attended, "half", axis=0, tiled=True),
        out_weight,
        preferred_element_type=jnp.float32,
    )
    mixed = lax.psum(partial_mix.astype(jnp.bfloat16), "tp").astype(jnp.float32)
    hidden = residual.astype(jnp.float32) + mixed
    squares = lax.psum(jnp.sum(hidden * hidden, axis=1), "half")
    half_width = hidden.shape[1]
    width = half_width * lax.axis_size("half")
    normed = (hidden * lax.rsqrt(squares / width + EPSILON)[:, None] * norm_gain[None, :]).astype(
        jnp.bfloat16
    )
    token_rows, top_count = expert_ids.shape
    ep_count = lax.axis_size("ep")
    tp_count = lax.axis_size("tp")
    local_experts = w_gate.shape[0]
    capacity = token_rows * top_count * 3 // (2 * EXPERTS)
    slot_count = ep_count * local_experts * capacity
    flat_ids = expert_ids.reshape(-1)
    one_hot = (flat_ids[:, None] == lax.iota(jnp.int32, EXPERTS)[None, :]).astype(jnp.int32)
    earlier = jnp.cumsum(one_hot, axis=0) - one_hot
    slot = jnp.sum(earlier * one_hot, axis=1)
    owner_ep = flat_ids // (local_experts * tp_count)
    owner_tp = flat_ids // local_experts % tp_count
    target = owner_ep * (local_experts * capacity) + flat_ids % local_experts * capacity + slot
    target = jnp.where(owner_tp == lax.axis_index("tp"), target, -1).reshape(token_rows, top_count)
    dispatch_matrix = jnp.any(
        lax.iota(jnp.int32, slot_count)[:, None, None] == target[None, :, :], axis=2
    ).astype(jnp.bfloat16)
    gates = gate_weights / jnp.sum(gate_weights, axis=1, keepdims=True)
    full_rows = lax.all_gather(normed, "half", axis=1, tiled=True)
    outgoing = jnp.dot(dispatch_matrix, full_rows, preferred_element_type=jnp.float32).astype(
        jnp.bfloat16
    )
    arrived = lax.all_to_all(
        outgoing.reshape(ep_count, local_experts, capacity, width),
        "ep",
        split_axis=0,
        concat_axis=0,
        tiled=True,
    )
    gate_part = jnp.einsum("secd,efd->secf", arrived, w_gate, preferred_element_type=jnp.float32)
    up_part = jnp.einsum("secd,efd->secf", arrived, w_up, preferred_element_type=jnp.float32)
    activation = (jax.nn.silu(gate_part) * up_part).astype(jnp.bfloat16)
    expert_out = jnp.einsum(
        "secf,efd->secd", activation, w_down, preferred_element_type=jnp.float32
    ).astype(jnp.bfloat16)
    summed = lax.psum_scatter(
        expert_out.astype(jnp.float32).astype(jnp.bfloat16), "half", scatter_dimension=3, tiled=True
    ).astype(jnp.float32)
    returned = lax.all_to_all(
        summed.reshape(ep_count, local_experts * capacity, half_width).astype(jnp.bfloat16),
        "ep",
        split_axis=0,
        concat_axis=0,
        tiled=True,
    ).astype(jnp.float32)
    term = combine_rows(returned.reshape(slot_count, half_width), target, gates)
    expert_sum = lax.psum_scatter(
        term.astype(jnp.bfloat16), "tp", scatter_dimension=1, tiled=True
    ).astype(jnp.float32)
    slice_width = expert_sum.shape[1]
    own_columns = lax.dynamic_slice_in_dim(
        hidden, lax.axis_index("tp") * slice_width, slice_width, 1
    )
    return (own_columns + expert_sum).astype(jnp.bfloat16)


VMEM_SPEC = pl.BlockSpec(memory_space=pltpu.VMEM)
HBM_SPEC = pl.BlockSpec(memory_space=pltpu.HBM)
SMEM_SPEC = pl.BlockSpec(memory_space=pltpu.SMEM)
NT = (((1,), (1,)), ((), ()))
TN = (((0,), (0,)), ((), ()))
F32 = jnp.float32
BF16 = jnp.bfloat16


def kernel_call(body, outs, specs=None, scratch=(), flops=1000, vmem=8, args=()):
    return pallas_kernel(body, outs, specs, scratch, flops, vmem, args)


def pallas_kernel(body, outs, specs, scratch, flops, vmem, args):
    return pl.pallas_call(
        body,
        out_shape=tuple(jax.ShapeDtypeStruct(s, d) for s, d in outs),
        in_specs=specs or [VMEM_SPEC] * len(args),
        out_specs=tuple(VMEM_SPEC for _ in outs),
        scratch_shapes=list(scratch),
        cost_estimate=pl.CostEstimate(flops=flops, bytes_accessed=1000, transcendentals=0),
        compiler_params=pltpu.CompilerParams(vmem_limit_bytes=vmem * MIB),
    )(*args)


def load_body(*refs):
    count = len(refs) // 2
    sems = refs[-1]
    copies = [
        pltpu.make_async_copy(refs[i], refs[count + i], sems.at[i]) for i in range(count)
    ]
    for copy in copies:
        copy.start()
    for copy in copies:
        copy.wait()


def attend_body(sharing, context, q_ref, nk_ref, nv_ref, k_ref, v_ref, len_ref, out_ref):
    requests = q_ref.shape[0]
    head_size = nk_ref.shape[1]
    group = 8
    rows = group * sharing
    keys = group * context
    score_scale = 1.0 / math.sqrt(head_size)
    lane = lax.broadcasted_iota(jnp.int32, (rows, keys), 1)
    position = jnp.where(
        lane // context == lax.broadcasted_iota(jnp.int32, (rows, keys), 0) % group,
        lane % context,
        context,
    )
    request = lax.broadcasted_iota(jnp.int32, (group, requests), 1)
    offset = request - lax.broadcasted_iota(jnp.int32, (group, requests), 0)
    for j in range(requests // group):
        here = slice(group * j, group * (j + 1))
        q = q_ref[here, :].astype(F32)
        q = jnp.concatenate(
            [q[:, g * head_size : (g + 1) * head_size] for g in range(sharing)], axis=0
        )
        own_key = jnp.concatenate([nk_ref[here, :].astype(F32)] * sharing, axis=0)
        own_value = jnp.concatenate([nv_ref[here, :].astype(F32)] * sharing, axis=0)
        length = jnp.sum(
            jnp.where(offset == group * j, len_ref[...], 0).astype(F32), axis=1, keepdims=True
        ).astype(jnp.int32)
        length = jnp.concatenate([length] * sharing, axis=0)
        scores = (
            lax.dot_general(
                q.astype(BF16), k_ref[keys * j : keys * (j + 1), :], NT, preferred_element_type=F32
            )
            * score_scale
        )
        scores = jnp.where(position < length, scores, -1e30)
        own_score = jnp.sum(q * own_key, axis=1, keepdims=True) * score_scale
        highest = jnp.maximum(jnp.max(scores, axis=1, keepdims=True), own_score)
        weights = jnp.exp(scores - highest)
        own_weight = jnp.exp(own_score - highest)
        inverse = 1.0 / (jnp.sum(weights, axis=1, keepdims=True) + own_weight)
        probs = (weights * inverse).astype(BF16)
        own_prob = (own_weight * inverse).astype(BF16).astype(F32)
        mixture = jnp.dot(probs, v_ref[keys * j : keys * (j + 1), :], preferred_element_type=F32)
        mixture = (mixture + own_prob * own_value).astype(BF16)
        for g in range(sharing):
            out_ref[here, g * head_size : (g + 1) * head_size] = mixture[group * g : group * (g + 1), :]


def project_body(own_ref, other_ref, w_ref, keep_ref, send_ref, rows_ref):
    x = lax.axis_index("half")
    t = lax.axis_index("tp")
    count = own_ref.shape[0]
    cols = keep_ref.shape[1]
    rows_ref[pl.ds(pl.multiple_of(x * count, count), count), :] = own_ref[...]
    rows_ref[pl.ds(pl.multiple_of((1 - x) * count, count), count), :] = other_ref[...]
    rows = rows_ref[...]
    send_ref[...] = jnp.dot(
        rows, w_ref[:, pl.ds(pl.multiple_of((1 - t) * cols, cols), cols)], preferred_element_type=F32
    )
    keep_ref[...] = jnp.dot(
        rows, w_ref[:, pl.ds(pl.multiple_of(t * cols, cols), cols)], preferred_element_type=F32
    )


LANES = 128
TAIL = 8


def hidden_body(res_ref, ids_ref, gw_ref, gain_ref, keep_ref, got_ref, h32_ref, load_ref, tail_ref):
    t = lax.axis_index("tp")
    rows, cols = keep_ref.shape
    here = pl.ds(pl.multiple_of(t * cols, cols), cols)
    hidden = res_ref[:, here].astype(F32) + (keep_ref[...] + got_ref[...])
    h32_ref[...] = hidden
    load_ref[0:rows, :] = hidden.astype(BF16)
    gw = gw_ref[...]
    gates = gw / jnp.sum(gw, axis=0, keepdims=True)
    high = gates.astype(BF16).astype(F32)
    gain = gain_ref[:, here]
    gain_high = gain.astype(BF16).astype(F32)
    tail_ref[...] = jnp.zeros(tail_ref.shape, F32)
    tail_ref[:, 0:rows] = ids_ref[...].astype(F32)
    tail_ref[:, LANES : LANES + rows] = high
    tail_ref[:, 2 * LANES : 2 * LANES + rows] = gates - high
    for i in range(cols // LANES):
        part = slice(LANES * i, LANES * (i + 1))
        tail_ref[i : i + 1, 3 * LANES :] = gain_high[:, part]
        tail_ref[TAIL // 2 + i : TAIL // 2 + i + 1, 3 * LANES :] = (gain - gain_high)[:, part]
    load_ref[rows:, :] = tail_ref[...].astype(BF16)


def merge_body(blocks, *refs):
    all_ref, far_ref = refs[-2:]
    rows = all_ref.shape[0] // blocks
    for j in range(blocks):
        all_ref[rows * j : rows * (j + 1), :] = refs[j][0:rows, :]
    for j in range(blocks // 2, blocks):
        start = rows * (j - blocks // 2)
        far_ref[start : start + rows, :] = refs[j][0:rows, :]


def join_body(near, *refs):
    out_ref = refs[-1]
    rows = refs[0].shape[0] - TAIL
    for j in range(near):
        out_ref[rows * j : rows * (j + 1), :] = refs[j][0:rows, :]
    out_ref[rows * near : out_ref.shape[0] - TAIL, :] = refs[near][...]
    out_ref[out_ref.shape[0] - TAIL :, :] = refs[0][rows:, :]


def pick_body(blocks, *refs):
    loads, pick_ref, gate_ref = refs[:blocks], refs[blocks], refs[blocks + 1]
    token_rows = loads[0].shape[0] - TAIL
    slot_rows, tokens = pick_ref.shape
    experts = EXPERTS // (lax.axis_size("ep") * lax.axis_size("tp"))
    slots = slot_rows // experts
    low = lax.broadcasted_iota(jnp.int32, (TAIL, LANES), 1) < token_rows
    tails = [ref[token_rows:, :].astype(F32) for ref in loads]

    def side_by_side(values):
        pairs = [
            jnp.where(low, values[j], pltpu.roll(values[j + 1], LANES - token_rows, 1))
            for j in range(0, blocks, 2)
        ]
        return jnp.concatenate(pairs, axis=1)

    ids = side_by_side([v[:, 0:LANES] for v in tails])
    gates = side_by_side([v[:, LANES : 2 * LANES] + v[:, 2 * LANES : 3 * LANES] for v in tails])
    first = (lax.axis_index("ep") * lax.axis_size("tp") + lax.axis_index("tp")) * experts
    number = (first + lax.broadcasted_iota(jnp.int32, (experts, TAIL, tokens), 0)).astype(F32)
    named = ids[None] == number
    chosen = jnp.sum(jnp.where(named, 1.0, 0.0), axis=1)
    gate = jnp.sum(jnp.where(named, gates[None], 0.0), axis=1)
    before = (
        lax.broadcasted_iota(jnp.int32, (tokens, tokens), 0)
        < lax.broadcasted_iota(jnp.int32, (tokens, tokens), 1)
    )
    earlier = jnp.dot(
        chosen.astype(BF16), jnp.where(before, 1.0, 0.0).astype(BF16), preferred_element_type=F32
    )
    place = jnp.where(chosen > 0.0, earlier, -1.0)
    slot = lax.broadcasted_iota(jnp.int32, (experts, slots, tokens), 1).astype(F32)
    pick = jnp.where(slot == place[:, None, :], 1.0, 0.0)
    gate_ref[...] = jnp.sum(pick * gate[:, None, :], axis=2, keepdims=True).reshape(
        slot_rows, 1
    )
    pick_ref[...] = pick.reshape(slot_rows, tokens).astype(BF16)


def gathered_rows(pick, parts, rows_ref):
    total = 0.0
    tokens = pick.shape[1]
    for owner, ref, gain in parts:
        cols = ref.shape[1]
        rows = jnp.dot(pick, ref[0:tokens, :], preferred_element_type=F32)
        total = total + jnp.sum(rows * rows, axis=1, keepdims=True)
        rows_ref[:, pl.ds(pl.multiple_of(owner * cols, cols), cols)] = (rows * gain).astype(BF16)
    return total


def tail_gain(ref):
    rows, cols = ref.shape
    tail = ref[rows - TAIL :, 3 * LANES :].astype(F32)
    gain = tail + pltpu.roll(tail, TAIL // 2, 0)
    return jnp.concatenate([gain[i : i + 1, :] for i in range(cols // LANES)], axis=1)


def products(rows_ref, w_ref, e, slots, start):
    half_width = rows_ref.shape[1]
    return lax.dot_general(
        rows_ref[slots * e : slots * (e + 1), :],
        w_ref[e, :, pl.ds(pl.multiple_of(start, half_width), half_width)],
        NT,
        preferred_element_type=F32,
    )


def first_half_body(
    slots, mine_ref, theirs_ref, gain_ref, wg_ref, wu_ref, pick_ref, squares_ref, rows_ref, ga_ref, ua_ref
):
    t = lax.axis_index("tp")
    cols = mine_ref.shape[1]
    parts = [
        (owner, ref, gain_ref[:, pl.ds(pl.multiple_of(owner * cols, cols), cols)])
        for owner, ref in ((t, mine_ref), (1 - t, theirs_ref))
    ]
    squares_ref[...] = gathered_rows(pick_ref[...], parts, rows_ref)
    start = lax.axis_index("half") * rows_ref.shape[1]
    for e in range(ga_ref.shape[0] // slots):
        here = slice(slots * e, slots * (e + 1))
        ga_ref[here, :] = products(rows_ref, wg_ref, e, slots, start)
        ua_ref[here, :] = products(rows_ref, wu_ref, e, slots, start)


def more_first_half_body(slots, done, rows_ref, wg_ref, wu_ref, ga_ref, ua_ref):
    start = lax.axis_index("half") * rows_ref.shape[1]
    for e in range(ga_ref.shape[0] // slots):
        here = slice(slots * e, slots * (e + 1))
        ga_ref[here, :] = products(rows_ref, wg_ref, done + e, slots, start)
        ua_ref[here, :] = products(rows_ref, wu_ref, done + e, slots, start)


def second_half_body(
    slots, mine_ref, theirs_ref, wg_ref, wu_ref, pick_ref, squares_ref, ga_ref, ua_ref, gb_ref, ub_ref,
    act_ref, rows_ref, inv_ref,
):
    experts, _, width = wg_ref.shape
    t = lax.axis_index("tp")
    parts = [(t, mine_ref, tail_gain(mine_ref)), (1 - t, theirs_ref, tail_gain(theirs_ref))]
    squares = gathered_rows(pick_ref[...], parts, rows_ref)
    inv_ref[...] = lax.rsqrt((squares_ref[...] + squares) / width + EPSILON)
    start = (1 - lax.axis_index("half")) * rows_ref.shape[1]
    done = ga_ref.shape[0] // slots
    for e in range(experts):
        here = slice(slots * e, slots * (e + 1))
        gate_acc, up_acc = (ga_ref, ua_ref) if e < done else (gb_ref, ub_ref)
        row = slots * (e if e < done else e - done)
        there = slice(row, row + slots)
        inverse = inv_ref[here, :]
        gate_part = inverse * (gate_acc[there, :] + products(rows_ref, wg_ref, e, slots, start))
        up_part = inverse * (up_acc[there, :] + products(rows_ref, wu_ref, e, slots, start))
        act_ref[here, :] = (jax.nn.silu(gate_part) * up_part).astype(BF16)


def down_body(other_half, other_core, act_ref, gate_ref, pick_ref, wd_ref, out_ref, y_ref):
    experts = wd_ref.shape[0]
    cols = out_ref.shape[1]
    slots = pick_ref.shape[0] // experts
    x, t = lax.axis_index("half"), lax.axis_index("tp")
    quarter = (1 - x if other_half else x) * lax.axis_size("tp") + (1 - t if other_core else t)
    columns = pl.ds(pl.multiple_of(quarter * cols, cols), cols)

    def one(e, carry):
        here = pl.ds(pl.multiple_of(e * slots, slots), slots)
        y = jnp.dot(act_ref[here, :], wd_ref[e, :, columns], preferred_element_type=F32)
        y_ref[here, :] = (y * gate_ref[here, :]).astype(BF16)
        return carry

    lax.fori_loop(0, experts, one, 0, unroll=True)
    out_ref[...] = lax.dot_general(
        pick_ref[...], y_ref[...], TN, preferred_element_type=F32
    ).astype(out_ref.dtype)


def pair_sum_body(keep_ref, got_ref, far_ref, near_ref):
    rows = near_ref.shape[0]
    for out, start in ((near_ref, 0), (far_ref, rows)):
        here = slice(start, start + out.shape[0])
        out[...] = (keep_ref[here, :] + got_ref[here, :].astype(F32)).astype(BF16)


def block_sum_body(start, keep_ref, got_ref, other_ref, *outs):
    rows = outs[0].shape[0]
    for j, out in enumerate(outs):
        here = slice(start + rows * j, start + rows * (j + 1))
        total = keep_ref[here, :] + got_ref[here, :].astype(F32)
        total = total + other_ref[rows * j : rows * (j + 1), :].astype(F32)
        out[...] = total.astype(out.dtype)


def final_body(h32_ref, own_ref, *refs):
    out_ref = refs[-1]
    total = own_ref[...]
    for ref in refs[:-1]:
        total = total + ref[...].astype(F32)
    out_ref[...] = (h32_ref[...] + total).astype(BF16)


def swap(value, axis, partner=1):
    return lax.ppermute(
        value, axis, [(i, i ^ partner) for i in range(lax.axis_size(axis))]
    )


def by_rows(
    queries,
    new_keys,
    new_values,
    cache_keys,
    cache_values,
    lengths,
    out_weight,
    residual,
    norm_gain,
    expert_ids,
    gate_weights,
    w_gate,
    w_up,
    w_down,
):
    requests, _, context, head_size = cache_keys.shape
    sharing = queries.shape[1] // head_size
    token_rows, top_count = expert_ids.shape
    blocks = lax.axis_size("ep")
    tokens = blocks * token_rows
    experts, hidden_units, _ = w_gate.shape
    half_width = residual.shape[1]
    cols = half_width // lax.axis_size("tp")
    slots = token_rows * top_count * 3 // (2 * EXPERTS) * blocks
    slot_rows = experts * slots
    w_gate, w_up, w_down = (
        pltpu.with_memory_space_constraint(w, pltpu.VMEM) for w in (w_gate, w_up, w_down)
    )

    gain = norm_gain.reshape(1, half_width)
    cache = (requests * context, head_size)
    sources = tuple(
        pltpu.with_memory_space_constraint(v, pltpu.HBM)
        for v in (
            queries,
            new_keys,
            new_values,
            cache_keys.reshape(cache),
            cache_values.reshape(cache),
            lengths.reshape(1, requests),
        )
    )
    loaded = kernel_call(
        load_body,
        [(v.shape, v.dtype) for v in sources],
        specs=[HBM_SPEC] * len(sources),
        scratch=[pltpu.SemaphoreType.DMA((len(sources),))],
        args=sources,
    )
    (attended,) = kernel_call(
        functools.partial(attend_body, sharing, context),
        [((requests, sharing * head_size), BF16)],
        flops=10**11,
        args=loaded,
    )
    other_attended = swap(attended, "half")
    keep, send = kernel_call(
        project_body,
        [((token_rows, cols), F32)] * 2,
        scratch=[pltpu.VMEM((token_rows, sharing * head_size), BF16)],
        args=(attended, other_attended, out_weight),
    )
    h32, payload = kernel_call(
        hidden_body,
        [((token_rows, cols), F32), ((token_rows + TAIL, cols), BF16)],
        scratch=[pltpu.VMEM((TAIL, cols), F32)],
        args=(residual, expert_ids.T, gate_weights.T, gain, keep, swap(send, "tp")),
    )
    arrived = [payload] + [swap(payload, "ep", j) for j in range(1, blocks)]
    near = blocks // 2
    near_x = [swap(arrived[j], "half") for j in range(near)]
    mine, far = kernel_call(
        functools.partial(merge_body, blocks),
        [((tokens, cols), BF16), ((tokens // 2, cols), BF16)],
        args=arrived,
    )
    theirs = swap(mine, "tp")
    far_x = swap(far, "half")
    pick, gate = kernel_call(
        functools.partial(pick_body, blocks),
        [((slot_rows, tokens), BF16), ((slot_rows, 1), F32)],
        args=arrived,
    )
    early = experts * 3 // 4
    squares, rows, gate_a, up_a = kernel_call(
        functools.partial(first_half_body, slots),
        [
            ((slot_rows, 1), F32),
            ((slot_rows, half_width), BF16),
            ((slots * early, hidden_units), F32),
            ((slots * early, hidden_units), F32),
        ],
        args=(mine, theirs, gain, w_gate, w_up, pick),
    )
    far_x, squares, near_x = lax.optimization_barrier((far_x, squares, near_x))
    (mine_x,) = kernel_call(
        functools.partial(join_body, near), [((tokens + TAIL, cols), BF16)], args=(*near_x, far_x)
    )
    theirs_x = swap(mine_x, "tp")
    gate_b, up_b = kernel_call(
        functools.partial(more_first_half_body, slots, early),
        [((slots * (experts - early), hidden_units), F32)] * 2,
        args=(rows, w_gate, w_up),
    )
    (act,) = kernel_call(
        functools.partial(second_half_body, slots),
        [((slot_rows, hidden_units), BF16)],
        scratch=[pltpu.VMEM((slot_rows, half_width), BF16), pltpu.VMEM((slot_rows, 1), F32)],
        args=(
            mine_x, theirs_x, w_gate, w_up, pick, squares, gate_a, up_a, gate_b, up_b,
        ),
    )

    def down(act, other_half, other_core):
        return kernel_call(
            functools.partial(down_body, other_half, other_core),
            [((tokens, cols), BF16 if other_core else F32)],
            scratch=[pltpu.VMEM((slot_rows, cols), BF16)],
            flops=10**9,
            args=(act, gate, pick, w_down),
        )[0]

    got_a = swap(down(act, True, True), "tp")
    keep_a = down(act, True, False)
    near_rows = tokens // 2
    far, near = kernel_call(
        pair_sum_body,
        [((tokens - near_rows, cols), BF16), ((near_rows, cols), BF16)],
        args=(keep_a, got_a),
    )
    act, far, near = lax.optimization_barrier((act, far, near))
    far_x = swap(far, "half")
    near_x = swap(near, "half")
    got_b = swap(down(act, False, True), "tp")
    keep_b = down(act, False, False)
    far_sums = kernel_call(
        functools.partial(block_sum_body, near_rows),
        [((token_rows, cols), BF16)] * (blocks // 2),
        args=(keep_b, got_b, far_x),
    )
    near_sums = kernel_call(
        functools.partial(block_sum_body, 0),
        [((token_rows, cols), F32)] + [((token_rows, cols), BF16)] * (blocks // 2 - 1),
        args=(keep_b, got_b, near_x),
    )
    home = [swap(v, "ep", blocks // 2 + j) for j, v in enumerate(far_sums)]
    home += [swap(v, "ep", 1 + j) for j, v in enumerate(near_sums[1:])]
    (out,) = kernel_call(final_body, [((token_rows, cols), BF16)], args=(h32, near_sums[0], *home))
    return out


def solution(mesh):
    placed = (
        P(("groups", "ep", "half"), "tp"),
        P(("groups", "ep", "half"), "tp"),
        P(("groups", "ep", "half"), "tp"),
        P(("groups", "ep", "half"), "tp", None, None),
        P(("groups", "ep", "half"), "tp", None, None),
        P(("groups", "ep", "half")),
        P("tp", "half"),
        P(("groups", "ep"), "half"),
        P("half"),
        P(("groups", "ep"), None),
        P(("groups", "ep"), None),
        P(("ep", "tp"), "half", None),
        P(("ep", "tp"), "half", None),
        P(("ep", "tp"), "half", None),
    )
    few = mesh.shape["half"] == 2 and mesh.shape["tp"] == 2 and mesh.shape["ep"] == 4

    def on_device(*args):
        return by_rows(*args) if few else by_slots(*args)

    return jax.shard_map(
        on_device,
        mesh=mesh,
        in_specs=placed,
        out_specs=P(("groups", "ep"), ("half", "tp")),
        check_vma=False,
    )
```

```python
import functools
import math

import jax
import jax.numpy as jnp
from jax import lax
from jax.experimental import pallas as pl
from jax.experimental.pallas import tpu as pltpu
from jax.sharding import PartitionSpec as P


EXPERTS = 64


EPSILON = 1e-06

MIB = 2**20


def attend(queries, new_keys, new_values, cache_keys, cache_values, lengths):
    requests, key_heads, context, head_size = cache_keys.shape
    sharing = queries.shape[1] // (key_heads * head_size)
    query_blocks = queries.reshape(requests, key_heads, sharing, head_size)
    score_scale = 1.0 / math.sqrt(head_size)
    scores = (
        jnp.einsum("rkgd,rkcd->rkgc", query_blocks, cache_keys, preferred_element_type=jnp.float32)
        * score_scale
    )
    own_score = (
        jnp.einsum(
            "rkgd,rkd->rkg",
            query_blocks,
            new_keys.reshape(requests, key_heads, head_size),
            preferred_element_type=jnp.float32,
        )
        * score_scale
    )
    valid = lax.iota(jnp.int32, context)[None, :] < lengths[:, None]
    scores = jnp.where(valid[:, None, None, :], scores, -1e30)
    highest = jnp.maximum(jnp.max(scores, axis=-1), own_score)
    weights = jnp.exp(scores - highest[..., None])
    own_weight = jnp.exp(own_score - highest)
    denominator = jnp.sum(weights, axis=-1) + own_weight
    probs = (weights / denominator[..., None]).astype(jnp.bfloat16)
    own_prob = (own_weight / denominator).astype(jnp.bfloat16)
    mixture = jnp.einsum("rkgc,rkcd->rkgd", probs, cache_values, preferred_element_type=jnp.float32)
    mixture = mixture + own_prob.astype(jnp.float32)[..., None] * new_values.reshape(
        requests, key_heads, 1, head_size
    ).astype(jnp.float32)
    return mixture.astype(jnp.bfloat16).reshape(requests, key_heads * sharing * head_size)


def combine_rows(returned_rows, target, gates):
    token_rows, top_count = target.shape
    safe_target = jnp.maximum(target, 0).reshape(-1)
    picked = jnp.take(returned_rows, safe_target, axis=0).reshape(
        token_rows, top_count, returned_rows.shape[1]
    )
    weighting = jnp.where(target >= 0, gates, 0.0)
    return jnp.sum(picked.astype(jnp.float32) * weighting[..., None], axis=1)


def by_slots(
    queries,
    new_keys,
    new_values,
    cache_keys,
    cache_values,
    lengths,
    out_weight,
    residual,
    norm_gain,
    expert_ids,
    gate_weights,
    w_gate,
    w_up,
    w_down,
):
    attended = attend(queries, new_keys, new_values, cache_keys, cache_values, lengths)
    partial_mix = jnp.dot(
        lax.all_gather(attended, "half", axis=0, tiled=True),
        out_weight,
        preferred_element_type=jnp.float32,
    )
    mixed = lax.psum(partial_mix.astype(jnp.bfloat16), "tp").astype(jnp.float32)
    hidden = residual.astype(jnp.float32) + mixed
    squares = lax.psum(jnp.sum(hidden * hidden, axis=1), "half")
    half_width = hidden.shape[1]
    width = half_width * lax.axis_size("half")
    normed = (hidden * lax.rsqrt(squares / width + EPSILON)[:, None] * norm_gain[None, :]).astype(
        jnp.bfloat16
    )
    token_rows, top_count = expert_ids.shape
    ep_count = lax.axis_size("ep")
    tp_count = lax.axis_size("tp")
    local_experts = w_gate.shape[0]
    capacity = token_rows * top_count * 3 // (2 * EXPERTS)
    slot_count = ep_count * local_experts * capacity
    flat_ids = expert_ids.reshape(-1)
    one_hot = (flat_ids[:, None] == lax.iota(jnp.int32, EXPERTS)[None, :]).astype(jnp.int32)
    earlier = jnp.cumsum(one_hot, axis=0) - one_hot
    slot = jnp.sum(earlier * one_hot, axis=1)
    owner_ep = flat_ids // (local_experts * tp_count)
    owner_tp = flat_ids // local_experts % tp_count
    target = owner_ep * (local_experts * capacity) + flat_ids % local_experts * capacity + slot
    target = jnp.where(owner_tp == lax.axis_index("tp"), target, -1).reshape(token_rows, top_count)
    dispatch_matrix = jnp.any(
        lax.iota(jnp.int32, slot_count)[:, None, None] == target[None, :, :], axis=2
    ).astype(jnp.bfloat16)
    gates = gate_weights / jnp.sum(gate_weights, axis=1, keepdims=True)
    full_rows = lax.all_gather(normed, "half", axis=1, tiled=True)
    outgoing = jnp.dot(dispatch_matrix, full_rows, preferred_element_type=jnp.float32).astype(
        jnp.bfloat16
    )
    arrived = lax.all_to_all(
        outgoing.reshape(ep_count, local_experts, capacity, width),
        "ep",
        split_axis=0,
        concat_axis=0,
        tiled=True,
    )
    gate_part = jnp.einsum("secd,efd->secf", arrived, w_gate, preferred_element_type=jnp.float32)
    up_part = jnp.einsum("secd,efd->secf", arrived, w_up, preferred_element_type=jnp.float32)
    activation = (jax.nn.silu(gate_part) * up_part).astype(jnp.bfloat16)
    expert_out = jnp.einsum(
        "secf,efd->secd", activation, w_down, preferred_element_type=jnp.float32
    ).astype(jnp.bfloat16)
    summed = lax.psum_scatter(
        expert_out.astype(jnp.float32).astype(jnp.bfloat16), "half", scatter_dimension=3, tiled=True
    ).astype(jnp.float32)
    returned = lax.all_to_all(
        summed.reshape(ep_count, local_experts * capacity, half_width).astype(jnp.bfloat16),
        "ep",
        split_axis=0,
        concat_axis=0,
        tiled=True,
    ).astype(jnp.float32)
    term = combine_rows(returned.reshape(slot_count, half_width), target, gates)
    expert_sum = lax.psum_scatter(
        term.astype(jnp.bfloat16), "tp", scatter_dimension=1, tiled=True
    ).astype(jnp.float32)
    slice_width = expert_sum.shape[1]
    own_columns = lax.dynamic_slice_in_dim(
        hidden, lax.axis_index("tp") * slice_width, slice_width, 1
    )
    return (own_columns + expert_sum).astype(jnp.bfloat16)


VMEM_SPEC = pl.BlockSpec(memory_space=pltpu.VMEM)
HBM_SPEC = pl.BlockSpec(memory_space=pltpu.HBM)
SMEM_SPEC = pl.BlockSpec(memory_space=pltpu.SMEM)
NT = (((1,), (1,)), ((), ()))
TN = (((0,), (0,)), ((), ()))
F32 = jnp.float32
BF16 = jnp.bfloat16


def kernel_call(body, outs, specs=None, scratch=(), flops=1000, vmem=8, args=()):
    return pallas_kernel(body, outs, specs, scratch, flops, vmem, args)


def pallas_kernel(body, outs, specs, scratch, flops, vmem, args):
    return pl.pallas_call(
        body,
        out_shape=tuple(jax.ShapeDtypeStruct(s, d) for s, d in outs),
        in_specs=specs or [VMEM_SPEC] * len(args),
        out_specs=tuple(VMEM_SPEC for _ in outs),
        scratch_shapes=list(scratch),
        cost_estimate=pl.CostEstimate(flops=flops, bytes_accessed=1000, transcendentals=0),
        compiler_params=pltpu.CompilerParams(vmem_limit_bytes=vmem * MIB),
    )(*args)


def load_body(*refs):
    count = len(refs) // 2
    sems = refs[-1]
    copies = [
        pltpu.make_async_copy(refs[i], refs[count + i], sems.at[i]) for i in range(count)
    ]
    for copy in copies:
        copy.start()
    for copy in copies:
        copy.wait()


def attend_body(sharing, context, q_ref, nk_ref, nv_ref, k_ref, v_ref, len_ref, out_ref):
    requests = q_ref.shape[0]
    head_size = nk_ref.shape[1]
    group = 8
    rows = group * sharing
    keys = group * context
    score_scale = 1.0 / math.sqrt(head_size)
    lane = lax.broadcasted_iota(jnp.int32, (rows, keys), 1)
    position = jnp.where(
        lane // context == lax.broadcasted_iota(jnp.int32, (rows, keys), 0) % group,
        lane % context,
        context,
    )
    request = lax.broadcasted_iota(jnp.int32, (group, requests), 1)
    offset = request - lax.broadcasted_iota(jnp.int32, (group, requests), 0)
    for j in range(requests // group):
        here = slice(group * j, group * (j + 1))
        q = q_ref[here, :].astype(F32)
        q = jnp.concatenate(
            [q[:, g * head_size : (g + 1) * head_size] for g in range(sharing)], axis=0
        )
        own_key = jnp.concatenate([nk_ref[here, :].astype(F32)] * sharing, axis=0)
        own_value = jnp.concatenate([nv_ref[here, :].astype(F32)] * sharing, axis=0)
        length = jnp.sum(
            jnp.where(offset == group * j, len_ref[...], 0).astype(F32), axis=1, keepdims=True
        ).astype(jnp.int32)
        length = jnp.concatenate([length] * sharing, axis=0)
        scores = (
            lax.dot_general(
                q.astype(BF16), k_ref[keys * j : keys * (j + 1), :], NT, preferred_element_type=F32
            )
            * score_scale
        )
        scores = jnp.where(position < length, scores, -1e30)
        own_score = jnp.sum(q * own_key, axis=1, keepdims=True) * score_scale
        highest = jnp.maximum(jnp.max(scores, axis=1, keepdims=True), own_score)
        weights = jnp.exp(scores - highest)
        own_weight = jnp.exp(own_score - highest)
        inverse = 1.0 / (jnp.sum(weights, axis=1, keepdims=True) + own_weight)
        probs = (weights * inverse).astype(BF16)
        own_prob = (own_weight * inverse).astype(BF16).astype(F32)
        mixture = jnp.dot(probs, v_ref[keys * j : keys * (j + 1), :], preferred_element_type=F32)
        mixture = (mixture + own_prob * own_value).astype(BF16)
        for g in range(sharing):
            out_ref[here, g * head_size : (g + 1) * head_size] = mixture[group * g : group * (g + 1), :]


def project_body(own_ref, other_ref, w_ref, keep_ref, send_ref, rows_ref):
    x = lax.axis_index("half")
    t = lax.axis_index("tp")
    count = own_ref.shape[0]
    cols = keep_ref.shape[1]
    rows_ref[pl.ds(pl.multiple_of(x * count, count), count), :] = own_ref[...]
    rows_ref[pl.ds(pl.multiple_of((1 - x) * count, count), count), :] = other_ref[...]
    rows = rows_ref[...]
    send_ref[...] = jnp.dot(
        rows, w_ref[:, pl.ds(pl.multiple_of((1 - t) * cols, cols), cols)], preferred_element_type=F32
    )
    keep_ref[...] = jnp.dot(
        rows, w_ref[:, pl.ds(pl.multiple_of(t * cols, cols), cols)], preferred_element_type=F32
    )


LANES = 128
TAIL = 8


def hidden_body(res_ref, ids_ref, gw_ref, gain_ref, keep_ref, got_ref, h32_ref, load_ref, tail_ref):
    t = lax.axis_index("tp")
    rows, cols = keep_ref.shape
    here = pl.ds(pl.multiple_of(t * cols, cols), cols)
    hidden = res_ref[:, here].astype(F32) + (keep_ref[...] + got_ref[...])
    h32_ref[...] = hidden
    load_ref[0:rows, :] = hidden.astype(BF16)
    gw = gw_ref[...]
    gates = gw / jnp.sum(gw, axis=0, keepdims=True)
    high = gates.astype(BF16).astype(F32)
    gain = gain_ref[:, here]
    gain_high = gain.astype(BF16).astype(F32)
    tail_ref[...] = jnp.zeros(tail_ref.shape, F32)
    tail_ref[:, 0:rows] = ids_ref[...].astype(F32)
    tail_ref[:, LANES : LANES + rows] = high
    tail_ref[:, 2 * LANES : 2 * LANES + rows] = gates - high
    for i in range(cols // LANES):
        part = slice(LANES * i, LANES * (i + 1))
        tail_ref[i : i + 1, 3 * LANES :] = gain_high[:, part]
        tail_ref[TAIL // 2 + i : TAIL // 2 + i + 1, 3 * LANES :] = (gain - gain_high)[:, part]
    load_ref[rows:, :] = tail_ref[...].astype(BF16)


def merge_body(*refs):
    all_ref = refs[-1]
    rows = refs[0].shape[0] - TAIL
    for j, ref in enumerate(refs[:-1]):
        all_ref[rows * j : rows * (j + 1), :] = ref[0:rows, :]


def join_body(*refs):
    out_ref = refs[-1]
    rows = refs[0].shape[0] - TAIL
    for j, ref in enumerate(refs[:-1]):
        out_ref[rows * j : rows * (j + 1), :] = ref[0:rows, :]
    out_ref[out_ref.shape[0] - TAIL :, :] = refs[0][rows:, :]


def pick_body(blocks, *refs):
    loads, pick_ref, gate_ref = refs[:blocks], refs[blocks], refs[blocks + 1]
    token_rows = loads[0].shape[0] - TAIL
    slot_rows, tokens = pick_ref.shape
    experts = EXPERTS // (lax.axis_size("ep") * lax.axis_size("tp"))
    slots = slot_rows // experts
    low = lax.broadcasted_iota(jnp.int32, (TAIL, LANES), 1) < token_rows
    tails = [ref[token_rows:, :].astype(F32) for ref in loads]

    def side_by_side(values):
        pairs = [
            jnp.where(low, values[j], pltpu.roll(values[j + 1], LANES - token_rows, 1))
            for j in range(0, blocks, 2)
        ]
        return jnp.concatenate(pairs, axis=1)

    ids = side_by_side([v[:, 0:LANES] for v in tails])
    gates = side_by_side([v[:, LANES : 2 * LANES] + v[:, 2 * LANES : 3 * LANES] for v in tails])
    first = (lax.axis_index("ep") * lax.axis_size("tp") + lax.axis_index("tp")) * experts
    number = (first + lax.broadcasted_iota(jnp.int32, (experts, TAIL, tokens), 0)).astype(F32)
    named = ids[None] == number
    chosen = jnp.sum(jnp.where(named, 1.0, 0.0), axis=1)
    gate = jnp.sum(jnp.where(named, gates[None], 0.0), axis=1)
    before = (
        lax.broadcasted_iota(jnp.int32, (tokens, tokens), 0)
        < lax.broadcasted_iota(jnp.int32, (tokens, tokens), 1)
    )
    earlier = jnp.dot(
        chosen.astype(BF16), jnp.where(before, 1.0, 0.0).astype(BF16), preferred_element_type=F32
    )
    place = jnp.where(chosen > 0.0, earlier, -1.0)
    slot = lax.broadcasted_iota(jnp.int32, (experts, slots, tokens), 1).astype(F32)
    pick = jnp.where(slot == place[:, None, :], 1.0, 0.0)
    gate_ref[...] = jnp.sum(pick * gate[:, None, :], axis=2, keepdims=True).reshape(
        slot_rows, 1
    )
    pick_ref[...] = pick.reshape(slot_rows, tokens).astype(BF16)


def gathered_rows(pick, parts, rows_ref):
    total = 0.0
    tokens = pick.shape[1]
    for owner, ref, gain in parts:
        cols = ref.shape[1]
        rows = jnp.dot(pick, ref[0:tokens, :], preferred_element_type=F32)
        total = total + jnp.sum(rows * rows, axis=1, keepdims=True)
        rows_ref[:, pl.ds(pl.multiple_of(owner * cols, cols), cols)] = (rows * gain).astype(BF16)
    return total


def tail_gain(ref):
    rows, cols = ref.shape
    tail = ref[rows - TAIL :, 3 * LANES :].astype(F32)
    gain = tail + pltpu.roll(tail, TAIL // 2, 0)
    return jnp.concatenate([gain[i : i + 1, :] for i in range(cols // LANES)], axis=1)


def products(rows_ref, w_ref, e, slots, start):
    half_width = rows_ref.shape[1]
    return lax.dot_general(
        w_ref[e, :, pl.ds(pl.multiple_of(start, half_width), half_width)],
        rows_ref[slots * e : slots * (e + 1), :],
        NT,
        preferred_element_type=F32,
    ).T


def first_half_body(
    slots, mine_ref, theirs_ref, gain_ref, wg_ref, wu_ref, pick_ref, squares_ref, rows_ref, ga_ref, ua_ref
):
    t = lax.axis_index("tp")
    cols = mine_ref.shape[1]
    parts = [
        (owner, ref, gain_ref[:, pl.ds(pl.multiple_of(owner * cols, cols), cols)])
        for owner, ref in ((t, mine_ref), (1 - t, theirs_ref))
    ]
    squares_ref[...] = gathered_rows(pick_ref[...], parts, rows_ref)
    start = lax.axis_index("half") * rows_ref.shape[1]
    for e in range(ga_ref.shape[0] // slots):
        here = slice(slots * e, slots * (e + 1))
        ga_ref[here, :] = products(rows_ref, wg_ref, e, slots, start)
        ua_ref[here, :] = products(rows_ref, wu_ref, e, slots, start)


def more_first_half_body(slots, done, rows_ref, wg_ref, wu_ref, ga_ref, ua_ref):
    start = lax.axis_index("half") * rows_ref.shape[1]
    for e in range(ga_ref.shape[0] // slots):
        here = slice(slots * e, slots * (e + 1))
        ga_ref[here, :] = products(rows_ref, wg_ref, done + e, slots, start)
        ua_ref[here, :] = products(rows_ref, wu_ref, done + e, slots, start)


def second_half_body(
    slots, mine_ref, theirs_ref, wg_ref, wu_ref, pick_ref, squares_ref, ga_ref, ua_ref, gb_ref, ub_ref,
    act_ref, rows_ref, inv_ref,
):
    experts, _, width = wg_ref.shape
    t = lax.axis_index("tp")
    parts = [(t, mine_ref, tail_gain(mine_ref)), (1 - t, theirs_ref, tail_gain(theirs_ref))]
    squares = gathered_rows(pick_ref[...], parts, rows_ref)
    inv_ref[...] = lax.rsqrt((squares_ref[...] + squares) / width + EPSILON)
    start = (1 - lax.axis_index("half")) * rows_ref.shape[1]
    done = ga_ref.shape[0] // slots
    for e in range(experts):
        here = slice(slots * e, slots * (e + 1))
        gate_acc, up_acc = (ga_ref, ua_ref) if e < done else (gb_ref, ub_ref)
        row = slots * (e if e < done else e - done)
        there = slice(row, row + slots)
        inverse = inv_ref[here, :]
        gate_part = inverse * (gate_acc[there, :] + products(rows_ref, wg_ref, e, slots, start))
        up_part = inverse * (up_acc[there, :] + products(rows_ref, wu_ref, e, slots, start))
        act_ref[here, :] = (jax.nn.silu(gate_part) * up_part).astype(BF16)


def down_body(other_half, other_core, act_ref, gate_ref, pick_ref, wd_ref, out_ref, y_ref):
    experts = wd_ref.shape[0]
    cols = out_ref.shape[1]
    slots = pick_ref.shape[0] // experts
    x, t = lax.axis_index("half"), lax.axis_index("tp")
    quarter = (1 - x if other_half else x) * lax.axis_size("tp") + (1 - t if other_core else t)
    columns = pl.ds(pl.multiple_of(quarter * cols, cols), cols)

    def one(e, carry):
        here = pl.ds(pl.multiple_of(e * slots, slots), slots)
        y = jnp.dot(act_ref[here, :], wd_ref[e, :, columns], preferred_element_type=F32)
        y_ref[here, :] = (y * gate_ref[here, :]).astype(BF16)
        return carry

    lax.fori_loop(0, experts, one, 0, unroll=True)
    out_ref[...] = lax.dot_general(
        pick_ref[...], y_ref[...], TN, preferred_element_type=F32
    ).astype(out_ref.dtype)


def pair_sum_body(keep_ref, got_ref, *outs):
    start = 0
    for out in outs:
        here = slice(start, start + out.shape[0])
        out[...] = (keep_ref[here, :] + got_ref[here, :].astype(F32)).astype(BF16)
        start += out.shape[0]


def block_sum_body(start, keep_ref, got_ref, other_ref, out_ref):
    here = slice(start, start + out_ref.shape[0])
    total = keep_ref[here, :] + got_ref[here, :].astype(F32) + other_ref[...].astype(F32)
    out_ref[...] = total.astype(BF16)


def final_body(h32_ref, keep_ref, got_ref, *refs):
    out_ref = refs[-1]
    here = slice(0, out_ref.shape[0])
    total = keep_ref[here, :] + got_ref[here, :].astype(F32)
    for ref in refs[:-1]:
        total = total + ref[...].astype(F32)
    out_ref[...] = (h32_ref[...] + total).astype(BF16)


def swap(value, axis, partner=1):
    return lax.ppermute(
        value, axis, [(i, i ^ partner) for i in range(lax.axis_size(axis))]
    )


def by_rows(
    queries,
    new_keys,
    new_values,
    cache_keys,
    cache_values,
    lengths,
    out_weight,
    residual,
    norm_gain,
    expert_ids,
    gate_weights,
    w_gate,
    w_up,
    w_down,
):
    requests, _, context, head_size = cache_keys.shape
    sharing = queries.shape[1] // head_size
    token_rows, top_count = expert_ids.shape
    blocks = lax.axis_size("ep")
    tokens = blocks * token_rows
    experts, hidden_units, _ = w_gate.shape
    half_width = residual.shape[1]
    cols = half_width // lax.axis_size("tp")
    slots = token_rows * top_count * 3 // (2 * EXPERTS) * blocks
    slot_rows = experts * slots
    w_gate, w_up, w_down = (
        pltpu.with_memory_space_constraint(w, pltpu.VMEM) for w in (w_gate, w_up, w_down)
    )

    gain = norm_gain.reshape(1, half_width)
    cache = (requests * context, head_size)
    sources = tuple(
        pltpu.with_memory_space_constraint(v, pltpu.HBM)
        for v in (
            queries,
            new_keys,
            new_values,
            cache_keys.reshape(cache),
            cache_values.reshape(cache),
            lengths.reshape(1, requests),
        )
    )
    loaded = kernel_call(
        load_body,
        [(v.shape, v.dtype) for v in sources],
        specs=[HBM_SPEC] * len(sources),
        scratch=[pltpu.SemaphoreType.DMA((len(sources),))],
        args=sources,
    )
    (attended,) = kernel_call(
        functools.partial(attend_body, sharing, context),
        [((requests, sharing * head_size), BF16)],
        flops=10**11,
        args=loaded,
    )
    other_attended = swap(attended, "half")
    keep, send = kernel_call(
        project_body,
        [((token_rows, cols), F32)] * 2,
        scratch=[pltpu.VMEM((token_rows, sharing * head_size), BF16)],
        args=(attended, other_attended, out_weight),
    )
    h32, payload = kernel_call(
        hidden_body,
        [((token_rows, cols), F32), ((token_rows + TAIL, cols), BF16)],
        scratch=[pltpu.VMEM((TAIL, cols), F32)],
        args=(residual, expert_ids.T, gate_weights.T, gain, keep, swap(send, "tp")),
    )
    arrived = [payload] + [swap(payload, "ep", j) for j in range(1, blocks)]
    from_x = [swap(v, "half") for v in arrived]
    (mine,) = kernel_call(merge_body, [((tokens, cols), BF16)], args=arrived)
    theirs = swap(mine, "tp")
    pick, gate = kernel_call(
        functools.partial(pick_body, blocks),
        [((slot_rows, tokens), BF16), ((slot_rows, 1), F32)],
        args=arrived,
    )
    early = experts * 3 // 4
    squares, rows, gate_a, up_a = kernel_call(
        functools.partial(first_half_body, slots),
        [
            ((slot_rows, 1), F32),
            ((slot_rows, half_width), BF16),
            ((slots * early, hidden_units), F32),
            ((slots * early, hidden_units), F32),
        ],
        args=(mine, theirs, gain, w_gate, w_up, pick),
    )
    from_x, squares = lax.optimization_barrier((from_x, squares))
    (mine_x,) = kernel_call(join_body, [((tokens + TAIL, cols), BF16)], args=from_x)
    theirs_x = swap(mine_x, "tp")
    gate_b, up_b = kernel_call(
        functools.partial(more_first_half_body, slots, early),
        [((slots * (experts - early), hidden_units), F32)] * 2,
        args=(rows, w_gate, w_up),
    )
    (act,) = kernel_call(
        functools.partial(second_half_body, slots),
        [((slot_rows, hidden_units), BF16)],
        scratch=[pltpu.VMEM((slot_rows, half_width), BF16), pltpu.VMEM((slot_rows, 1), F32)],
        args=(
            mine_x, theirs_x, w_gate, w_up, pick, squares, gate_a, up_a, gate_b, up_b,
        ),
    )

    def down(act, other_half, other_core):
        return kernel_call(
            functools.partial(down_body, other_half, other_core),
            [((tokens, cols), BF16 if other_core else F32)],
            scratch=[pltpu.VMEM((slot_rows, cols), BF16)],
            flops=10**9,
            args=(act, gate, pick, w_down),
        )[0]

    got_a = swap(down(act, True, True), "tp")
    keep_a = down(act, True, False)
    sums = kernel_call(pair_sum_body, [((token_rows, cols), BF16)] * blocks, args=(keep_a, got_a))
    act, sums = lax.optimization_barrier((act, sums))
    from_x = [swap(v, "half") for v in sums]
    got_b = swap(down(act, False, True), "tp")
    keep_b = down(act, False, False)

    home = []
    for j in range(blocks - 1, 0, -1):
        (total,) = kernel_call(
            functools.partial(block_sum_body, j * token_rows),
            [((token_rows, cols), BF16)],
            args=(keep_b, got_b, from_x[j]),
        )
        home.append(swap(total, "ep", j))
    (out,) = kernel_call(
        final_body, [((token_rows, cols), BF16)], args=(h32, keep_b, got_b, from_x[0], *home)
    )
    return out


def solution(mesh):
    placed = (
        P(("groups", "ep", "half"), "tp"),
        P(("groups", "ep", "half"), "tp"),
        P(("groups", "ep", "half"), "tp"),
        P(("groups", "ep", "half"), "tp", None, None),
        P(("groups", "ep", "half"), "tp", None, None),
        P(("groups", "ep", "half")),
        P("tp", "half"),
        P(("groups", "ep"), "half"),
        P("half"),
        P(("groups", "ep"), None),
        P(("groups", "ep"), None),
        P(("ep", "tp"), "half", None),
        P(("ep", "tp"), "half", None),
        P(("ep", "tp"), "half", None),
    )
    few = mesh.shape["half"] == 2 and mesh.shape["tp"] == 2 and mesh.shape["ep"] == 4

    def on_device(*args):
        return by_rows(*args) if few else by_slots(*args)

    return jax.shard_map(
        on_device,
        mesh=mesh,
        in_specs=placed,
        out_specs=P(("groups", "ep"), ("half", "tp")),
        check_vma=False,
    )
```

```python
import functools
import math

import jax
import jax.numpy as jnp
from jax import lax
from jax.experimental import pallas as pl
from jax.experimental.pallas import tpu as pltpu
from jax.sharding import PartitionSpec as P


EXPERTS = 64


EPSILON = 1e-06

MIB = 2**20


def attend(queries, new_keys, new_values, cache_keys, cache_values, lengths):
    requests, key_heads, context, head_size = cache_keys.shape
    sharing = queries.shape[1] // (key_heads * head_size)
    query_blocks = queries.reshape(requests, key_heads, sharing, head_size)
    score_scale = 1.0 / math.sqrt(head_size)
    scores = (
        jnp.einsum("rkgd,rkcd->rkgc", query_blocks, cache_keys, preferred_element_type=jnp.float32)
        * score_scale
    )
    own_score = (
        jnp.einsum(
            "rkgd,rkd->rkg",
            query_blocks,
            new_keys.reshape(requests, key_heads, head_size),
            preferred_element_type=jnp.float32,
        )
        * score_scale
    )
    valid = lax.iota(jnp.int32, context)[None, :] < lengths[:, None]
    scores = jnp.where(valid[:, None, None, :], scores, -1e30)
    highest = jnp.maximum(jnp.max(scores, axis=-1), own_score)
    weights = jnp.exp(scores - highest[..., None])
    own_weight = jnp.exp(own_score - highest)
    denominator = jnp.sum(weights, axis=-1) + own_weight
    probs = (weights / denominator[..., None]).astype(jnp.bfloat16)
    own_prob = (own_weight / denominator).astype(jnp.bfloat16)
    mixture = jnp.einsum("rkgc,rkcd->rkgd", probs, cache_values, preferred_element_type=jnp.float32)
    mixture = mixture + own_prob.astype(jnp.float32)[..., None] * new_values.reshape(
        requests, key_heads, 1, head_size
    ).astype(jnp.float32)
    return mixture.astype(jnp.bfloat16).reshape(requests, key_heads * sharing * head_size)


def combine_rows(returned_rows, target, gates):
    token_rows, top_count = target.shape
    safe_target = jnp.maximum(target, 0).reshape(-1)
    picked = jnp.take(returned_rows, safe_target, axis=0).reshape(
        token_rows, top_count, returned_rows.shape[1]
    )
    weighting = jnp.where(target >= 0, gates, 0.0)
    return jnp.sum(picked.astype(jnp.float32) * weighting[..., None], axis=1)


def by_slots(
    queries,
    new_keys,
    new_values,
    cache_keys,
    cache_values,
    lengths,
    out_weight,
    residual,
    norm_gain,
    expert_ids,
    gate_weights,
    w_gate,
    w_up,
    w_down,
):
    attended = attend(queries, new_keys, new_values, cache_keys, cache_values, lengths)
    partial_mix = jnp.dot(
        lax.all_gather(attended, "half", axis=0, tiled=True),
        out_weight,
        preferred_element_type=jnp.float32,
    )
    mixed = lax.psum(partial_mix.astype(jnp.bfloat16), "tp").astype(jnp.float32)
    hidden = residual.astype(jnp.float32) + mixed
    squares = lax.psum(jnp.sum(hidden * hidden, axis=1), "half")
    half_width = hidden.shape[1]
    width = half_width * lax.axis_size("half")
    normed = (hidden * lax.rsqrt(squares / width + EPSILON)[:, None] * norm_gain[None, :]).astype(
        jnp.bfloat16
    )
    token_rows, top_count = expert_ids.shape
    ep_count = lax.axis_size("ep")
    tp_count = lax.axis_size("tp")
    local_experts = w_gate.shape[0]
    capacity = token_rows * top_count * 3 // (2 * EXPERTS)
    slot_count = ep_count * local_experts * capacity
    flat_ids = expert_ids.reshape(-1)
    one_hot = (flat_ids[:, None] == lax.iota(jnp.int32, EXPERTS)[None, :]).astype(jnp.int32)
    earlier = jnp.cumsum(one_hot, axis=0) - one_hot
    slot = jnp.sum(earlier * one_hot, axis=1)
    owner_ep = flat_ids // (local_experts * tp_count)
    owner_tp = flat_ids // local_experts % tp_count
    target = owner_ep * (local_experts * capacity) + flat_ids % local_experts * capacity + slot
    target = jnp.where(owner_tp == lax.axis_index("tp"), target, -1).reshape(token_rows, top_count)
    dispatch_matrix = jnp.any(
        lax.iota(jnp.int32, slot_count)[:, None, None] == target[None, :, :], axis=2
    ).astype(jnp.bfloat16)
    gates = gate_weights / jnp.sum(gate_weights, axis=1, keepdims=True)
    full_rows = lax.all_gather(normed, "half", axis=1, tiled=True)
    outgoing = jnp.dot(dispatch_matrix, full_rows, preferred_element_type=jnp.float32).astype(
        jnp.bfloat16
    )
    arrived = lax.all_to_all(
        outgoing.reshape(ep_count, local_experts, capacity, width),
        "ep",
        split_axis=0,
        concat_axis=0,
        tiled=True,
    )
    gate_part = jnp.einsum("secd,efd->secf", arrived, w_gate, preferred_element_type=jnp.float32)
    up_part = jnp.einsum("secd,efd->secf", arrived, w_up, preferred_element_type=jnp.float32)
    activation = (jax.nn.silu(gate_part) * up_part).astype(jnp.bfloat16)
    expert_out = jnp.einsum(
        "secf,efd->secd", activation, w_down, preferred_element_type=jnp.float32
    ).astype(jnp.bfloat16)
    summed = lax.psum_scatter(
        expert_out.astype(jnp.float32).astype(jnp.bfloat16), "half", scatter_dimension=3, tiled=True
    ).astype(jnp.float32)
    returned = lax.all_to_all(
        summed.reshape(ep_count, local_experts * capacity, half_width).astype(jnp.bfloat16),
        "ep",
        split_axis=0,
        concat_axis=0,
        tiled=True,
    ).astype(jnp.float32)
    term = combine_rows(returned.reshape(slot_count, half_width), target, gates)
    expert_sum = lax.psum_scatter(
        term.astype(jnp.bfloat16), "tp", scatter_dimension=1, tiled=True
    ).astype(jnp.float32)
    slice_width = expert_sum.shape[1]
    own_columns = lax.dynamic_slice_in_dim(
        hidden, lax.axis_index("tp") * slice_width, slice_width, 1
    )
    return (own_columns + expert_sum).astype(jnp.bfloat16)


VMEM_SPEC = pl.BlockSpec(memory_space=pltpu.VMEM)
HBM_SPEC = pl.BlockSpec(memory_space=pltpu.HBM)
SMEM_SPEC = pl.BlockSpec(memory_space=pltpu.SMEM)
NT = (((1,), (1,)), ((), ()))
TN = (((0,), (0,)), ((), ()))
F32 = jnp.float32
BF16 = jnp.bfloat16


def kernel_call(body, outs, specs=None, scratch=(), flops=1000, vmem=8, args=()):
    return pallas_kernel(body, outs, specs, scratch, flops, vmem, args)


def pallas_kernel(body, outs, specs, scratch, flops, vmem, args):
    return pl.pallas_call(
        body,
        out_shape=tuple(jax.ShapeDtypeStruct(s, d) for s, d in outs),
        in_specs=specs or [VMEM_SPEC] * len(args),
        out_specs=tuple(VMEM_SPEC for _ in outs),
        scratch_shapes=list(scratch),
        cost_estimate=pl.CostEstimate(flops=flops, bytes_accessed=1000, transcendentals=0),
        compiler_params=pltpu.CompilerParams(vmem_limit_bytes=vmem * MIB),
    )(*args)


def load_body(*refs):
    count = len(refs) // 2
    sems = refs[-1]
    copies = [
        pltpu.make_async_copy(refs[i], refs[count + i], sems.at[i]) for i in range(count)
    ]
    for copy in copies:
        copy.start()
    for copy in copies:
        copy.wait()


def attend_body(sharing, context, q_ref, nk_ref, nv_ref, k_ref, v_ref, len_ref, out_ref):
    requests = q_ref.shape[0]
    head_size = nk_ref.shape[1]
    group = 8
    rows = group * sharing
    keys = group * context
    score_scale = 1.0 / math.sqrt(head_size)
    lane = lax.broadcasted_iota(jnp.int32, (rows, keys), 1)
    position = jnp.where(
        lane // context == lax.broadcasted_iota(jnp.int32, (rows, keys), 0) % group,
        lane % context,
        context,
    )
    request = lax.broadcasted_iota(jnp.int32, (group, requests), 1)
    offset = request - lax.broadcasted_iota(jnp.int32, (group, requests), 0)
    for j in range(requests // group):
        here = slice(group * j, group * (j + 1))
        q = q_ref[here, :].astype(F32)
        q = jnp.concatenate(
            [q[:, g * head_size : (g + 1) * head_size] for g in range(sharing)], axis=0
        )
        own_key = jnp.concatenate([nk_ref[here, :].astype(F32)] * sharing, axis=0)
        own_value = jnp.concatenate([nv_ref[here, :].astype(F32)] * sharing, axis=0)
        length = jnp.sum(
            jnp.where(offset == group * j, len_ref[...], 0).astype(F32), axis=1, keepdims=True
        ).astype(jnp.int32)
        length = jnp.concatenate([length] * sharing, axis=0)
        scores = (
            lax.dot_general(
                q.astype(BF16), k_ref[keys * j : keys * (j + 1), :], NT, preferred_element_type=F32
            )
            * score_scale
        )
        scores = jnp.where(position < length, scores, -1e30)
        own_score = jnp.sum(q * own_key, axis=1, keepdims=True) * score_scale
        highest = jnp.maximum(jnp.max(scores, axis=1, keepdims=True), own_score)
        weights = jnp.exp(scores - highest)
        own_weight = jnp.exp(own_score - highest)
        inverse = 1.0 / (jnp.sum(weights, axis=1, keepdims=True) + own_weight)
        probs = (weights * inverse).astype(BF16)
        own_prob = (own_weight * inverse).astype(BF16).astype(F32)
        mixture = jnp.dot(probs, v_ref[keys * j : keys * (j + 1), :], preferred_element_type=F32)
        mixture = (mixture + own_prob * own_value).astype(BF16)
        for g in range(sharing):
            out_ref[here, g * head_size : (g + 1) * head_size] = mixture[group * g : group * (g + 1), :]


def project_body(own_ref, other_ref, w_ref, keep_ref, send_ref, rows_ref):
    x = lax.axis_index("half")
    t = lax.axis_index("tp")
    count = own_ref.shape[0]
    cols = keep_ref.shape[1]
    rows_ref[pl.ds(pl.multiple_of(x * count, count), count), :] = own_ref[...]
    rows_ref[pl.ds(pl.multiple_of((1 - x) * count, count), count), :] = other_ref[...]
    rows = rows_ref[...]
    send_ref[...] = jnp.dot(
        rows, w_ref[:, pl.ds(pl.multiple_of((1 - t) * cols, cols), cols)], preferred_element_type=F32
    )
    keep_ref[...] = jnp.dot(
        rows, w_ref[:, pl.ds(pl.multiple_of(t * cols, cols), cols)], preferred_element_type=F32
    )


LANES = 128
TAIL = 8


def route_body(ids_ref, gw_ref, out_ref, tail_ref):
    rows = ids_ref.shape[1]
    gw = gw_ref[...]
    gates = gw / jnp.sum(gw, axis=0, keepdims=True)
    high = gates.astype(BF16).astype(F32)
    tail_ref[...] = jnp.zeros(tail_ref.shape, F32)
    tail_ref[:, 0:rows] = ids_ref[...].astype(F32)
    tail_ref[:, LANES : LANES + rows] = high
    tail_ref[:, 2 * LANES : 2 * LANES + rows] = gates - high
    out_ref[...] = tail_ref[...].astype(BF16)


def stack_body(first_ref, second_ref, out_ref):
    out_ref[0:TAIL, :] = first_ref[...]
    out_ref[TAIL:, :] = second_ref[...]


def hidden_body(res_ref, gain_ref, keep_ref, got_ref, h32_ref, h16_ref, load_ref, tail_ref):
    t = lax.axis_index("tp")
    rows, cols = keep_ref.shape
    here = pl.ds(pl.multiple_of(t * cols, cols), cols)
    hidden = res_ref[:, here].astype(F32) + (keep_ref[...] + got_ref[...])
    h32_ref[...] = hidden
    h16_ref[...] = hidden.astype(BF16)
    load_ref[0:rows, :] = hidden.astype(BF16)
    gain = gain_ref[:, here]
    gain_high = gain.astype(BF16).astype(F32)
    tail_ref[...] = jnp.zeros(tail_ref.shape, F32)
    for i in range(cols // LANES):
        part = slice(LANES * i, LANES * (i + 1))
        tail_ref[i : i + 1, 0:LANES] = gain_high[:, part]
        tail_ref[TAIL // 2 + i : TAIL // 2 + i + 1, 0:LANES] = (gain - gain_high)[:, part]
    load_ref[rows:, :] = tail_ref[...].astype(BF16)


def merge_body(*refs):
    all_ref = refs[-1]
    rows = refs[0].shape[0]
    for j, ref in enumerate(refs[:-1]):
        all_ref[rows * j : rows * (j + 1), :] = ref[...]


def join_body(load_ref, *refs):
    out_ref = refs[-1]
    rows = load_ref.shape[0] - TAIL
    out_ref[0:rows, :] = load_ref[0:rows, :]
    for j, ref in enumerate(refs[:-1]):
        out_ref[rows * (j + 1) : rows * (j + 2), :] = ref[...]
    out_ref[out_ref.shape[0] - TAIL :, :] = load_ref[rows:, :]


def pick_body(mine_ref, theirs_ref, pick_ref, gate_ref):
    slot_rows, tokens = pick_ref.shape
    blocks = 2 * mine_ref.shape[0] // TAIL
    token_rows = tokens // blocks
    experts = EXPERTS // (lax.axis_size("ep") * lax.axis_size("tp"))
    slots = slot_rows // experts
    low = lax.broadcasted_iota(jnp.int32, (TAIL, LANES), 1) < token_rows
    tails = [
        ref[start : start + TAIL, :].astype(F32)
        for start in range(0, mine_ref.shape[0], TAIL)
        for ref in (mine_ref, theirs_ref)
    ]

    def side_by_side(values):
        pairs = [
            jnp.where(low, values[j], pltpu.roll(values[j + 1], LANES - token_rows, 1))
            for j in range(0, blocks, 2)
        ]
        return jnp.concatenate(pairs, axis=1)

    ids = side_by_side([v[:, 0:LANES] for v in tails])
    gates = side_by_side([v[:, LANES : 2 * LANES] + v[:, 2 * LANES : 3 * LANES] for v in tails])
    first = (lax.axis_index("ep") * lax.axis_size("tp") + lax.axis_index("tp")) * experts
    number = (first + lax.broadcasted_iota(jnp.int32, (experts, TAIL, tokens), 0)).astype(F32)
    named = ids[None] == number
    chosen = jnp.sum(jnp.where(named, 1.0, 0.0), axis=1)
    gate = jnp.sum(jnp.where(named, gates[None], 0.0), axis=1)
    before = (
        lax.broadcasted_iota(jnp.int32, (tokens, tokens), 0)
        < lax.broadcasted_iota(jnp.int32, (tokens, tokens), 1)
    )
    earlier = jnp.dot(
        chosen.astype(BF16), jnp.where(before, 1.0, 0.0).astype(BF16), preferred_element_type=F32
    )
    place = jnp.where(chosen > 0.0, earlier, -1.0)
    slot = lax.broadcasted_iota(jnp.int32, (experts, slots, tokens), 1).astype(F32)
    pick = jnp.where(slot == place[:, None, :], 1.0, 0.0)
    gate_ref[...] = jnp.sum(pick * gate[:, None, :], axis=2, keepdims=True).reshape(
        slot_rows, 1
    )
    pick_ref[...] = pick.reshape(slot_rows, tokens).astype(BF16)


def gathered_rows(pick, parts, rows_ref):
    total = 0.0
    tokens = pick.shape[1]
    for owner, ref, gain in parts:
        cols = ref.shape[1]
        rows = jnp.dot(pick, ref[0:tokens, :], preferred_element_type=F32)
        total = total + jnp.sum(rows * rows, axis=1, keepdims=True)
        rows_ref[:, pl.ds(pl.multiple_of(owner * cols, cols), cols)] = (rows * gain).astype(BF16)
    return total


def tail_gain(ref):
    rows, cols = ref.shape
    tail = ref[rows - TAIL :, 0:LANES].astype(F32)
    gain = tail + pltpu.roll(tail, TAIL // 2, 0)
    return jnp.concatenate([gain[i : i + 1, :] for i in range(cols // LANES)], axis=1)


def products(rows_ref, w_ref, e, slots, start):
    half_width = rows_ref.shape[1]
    return lax.dot_general(
        w_ref[e, :, pl.ds(pl.multiple_of(start, half_width), half_width)],
        rows_ref[slots * e : slots * (e + 1), :],
        NT,
        preferred_element_type=F32,
    ).T


def first_half_body(
    slots, mine_ref, theirs_ref, gain_ref, wg_ref, wu_ref, pick_ref, squares_ref, rows_ref, ga_ref, ua_ref
):
    t = lax.axis_index("tp")
    cols = mine_ref.shape[1]
    parts = [
        (owner, ref, gain_ref[:, pl.ds(pl.multiple_of(owner * cols, cols), cols)])
        for owner, ref in ((t, mine_ref), (1 - t, theirs_ref))
    ]
    squares_ref[...] = gathered_rows(pick_ref[...], parts, rows_ref)
    start = lax.axis_index("half") * rows_ref.shape[1]
    for e in range(ga_ref.shape[0] // slots):
        here = slice(slots * e, slots * (e + 1))
        ga_ref[here, :] = products(rows_ref, wg_ref, e, slots, start)
        ua_ref[here, :] = products(rows_ref, wu_ref, e, slots, start)


def more_first_half_body(slots, done, rows_ref, wg_ref, wu_ref, ga_ref, ua_ref):
    start = lax.axis_index("half") * rows_ref.shape[1]
    for e in range(ga_ref.shape[0] // slots):
        here = slice(slots * e, slots * (e + 1))
        ga_ref[here, :] = products(rows_ref, wg_ref, done + e, slots, start)
        ua_ref[here, :] = products(rows_ref, wu_ref, done + e, slots, start)


def second_half_body(
    slots, mine_ref, theirs_ref, wg_ref, wu_ref, pick_ref, squares_ref, ga_ref, ua_ref, gb_ref, ub_ref,
    act_ref, rows_ref, inv_ref,
):
    experts, _, width = wg_ref.shape
    t = lax.axis_index("tp")
    parts = [(t, mine_ref, tail_gain(mine_ref)), (1 - t, theirs_ref, tail_gain(theirs_ref))]
    squares = gathered_rows(pick_ref[...], parts, rows_ref)
    inv_ref[...] = lax.rsqrt((squares_ref[...] + squares) / width + EPSILON)
    start = (1 - lax.axis_index("half")) * rows_ref.shape[1]
    done = ga_ref.shape[0] // slots
    for e in range(experts):
        here = slice(slots * e, slots * (e + 1))
        gate_acc, up_acc = (ga_ref, ua_ref) if e < done else (gb_ref, ub_ref)
        row = slots * (e if e < done else e - done)
        there = slice(row, row + slots)
        inverse = inv_ref[here, :]
        gate_part = inverse * (gate_acc[there, :] + products(rows_ref, wg_ref, e, slots, start))
        up_part = inverse * (up_acc[there, :] + products(rows_ref, wu_ref, e, slots, start))
        act_ref[here, :] = (jax.nn.silu(gate_part) * up_part).astype(BF16)


def down_body(other_half, other_core, act_ref, gate_ref, pick_ref, wd_ref, out_ref, y_ref):
    experts = wd_ref.shape[0]
    cols = out_ref.shape[1]
    slots = pick_ref.shape[0] // experts
    x, t = lax.axis_index("half"), lax.axis_index("tp")
    quarter = (1 - x if other_half else x) * lax.axis_size("tp") + (1 - t if other_core else t)
    columns = pl.ds(pl.multiple_of(quarter * cols, cols), cols)

    def one(e, carry):
        here = pl.ds(pl.multiple_of(e * slots, slots), slots)
        y = jnp.dot(act_ref[here, :], wd_ref[e, :, columns], preferred_element_type=F32)
        y_ref[here, :] = (y * gate_ref[here, :]).astype(BF16)
        return carry

    lax.fori_loop(0, experts, one, 0, unroll=True)
    out_ref[...] = lax.dot_general(
        pick_ref[...], y_ref[...], TN, preferred_element_type=F32
    ).astype(out_ref.dtype)


def pair_sum_body(keep_ref, got_ref, *outs):
    start = 0
    for out in outs:
        here = slice(start, start + out.shape[0])
        out[...] = (keep_ref[here, :] + got_ref[here, :].astype(F32)).astype(BF16)
        start += out.shape[0]


def block_sum_body(start, keep_ref, got_ref, other_ref, out_ref):
    here = slice(start, start + out_ref.shape[0])
    total = keep_ref[here, :] + got_ref[here, :].astype(F32) + other_ref[...].astype(F32)
    out_ref[...] = total.astype(BF16)


def final_body(h32_ref, keep_ref, got_ref, *refs):
    out_ref = refs[-1]
    here = slice(0, out_ref.shape[0])
    total = keep_ref[here, :] + got_ref[here, :].astype(F32)
    for ref in refs[:-1]:
        total = total + ref[...].astype(F32)
    out_ref[...] = (h32_ref[...] + total).astype(BF16)


def swap(value, axis, partner=1):
    return lax.ppermute(
        value, axis, [(i, i ^ partner) for i in range(lax.axis_size(axis))]
    )


def by_rows(
    queries,
    new_keys,
    new_values,
    cache_keys,
    cache_values,
    lengths,
    out_weight,
    residual,
    norm_gain,
    expert_ids,
    gate_weights,
    w_gate,
    w_up,
    w_down,
):
    requests, _, context, head_size = cache_keys.shape
    sharing = queries.shape[1] // head_size
    token_rows, top_count = expert_ids.shape
    blocks = lax.axis_size("ep")
    tokens = blocks * token_rows
    experts, hidden_units, _ = w_gate.shape
    half_width = residual.shape[1]
    cols = half_width // lax.axis_size("tp")
    slots = token_rows * top_count * 3 // (2 * EXPERTS) * blocks
    slot_rows = experts * slots
    w_gate, w_up, w_down = (
        pltpu.with_memory_space_constraint(w, pltpu.VMEM) for w in (w_gate, w_up, w_down)
    )

    gain = norm_gain.reshape(1, half_width)
    cache = (requests * context, head_size)
    sources = tuple(
        pltpu.with_memory_space_constraint(v, pltpu.HBM)
        for v in (
            queries,
            new_keys,
            new_values,
            cache_keys.reshape(cache),
            cache_values.reshape(cache),
            lengths.reshape(1, requests),
        )
    )
    loaded = kernel_call(
        load_body,
        [(v.shape, v.dtype) for v in sources],
        specs=[HBM_SPEC] * len(sources),
        scratch=[pltpu.SemaphoreType.DMA((len(sources),))],
        args=sources,
    )
    (attended,) = kernel_call(
        functools.partial(attend_body, sharing, context),
        [((requests, sharing * head_size), BF16)],
        flops=10**11,
        args=loaded,
    )
    other_attended = swap(attended, "half")
    (route,) = kernel_call(
        route_body,
        [((TAIL, 4 * LANES), BF16)],
        scratch=[pltpu.VMEM((TAIL, 4 * LANES), F32)],
        args=(expert_ids.T, gate_weights.T),
    )
    (routes,) = kernel_call(
        stack_body, [((2 * TAIL, 4 * LANES), BF16)], args=(route, swap(route, "ep", 2))
    )
    keep, send = kernel_call(
        project_body,
        [((token_rows, cols), F32)] * 2,
        scratch=[pltpu.VMEM((token_rows, sharing * head_size), BF16)],
        args=(attended, other_attended, out_weight),
    )
    h32, h16, payload = kernel_call(
        hidden_body,
        [((token_rows, cols), F32), ((token_rows, cols), BF16), ((token_rows + TAIL, cols), BF16)],
        scratch=[pltpu.VMEM((TAIL, cols), F32)],
        args=(residual, gain, keep, swap(send, "tp")),
    )
    arrived = [h16] + [swap(h16, "ep", j) for j in range(1, blocks)]
    from_x = [swap(payload if j == 0 else v, "half") for j, v in enumerate(arrived)]
    (mine,) = kernel_call(merge_body, [((tokens, cols), BF16)], args=arrived)
    theirs = swap(mine, "tp")
    pick, gate = kernel_call(
        pick_body,
        [((slot_rows, tokens), BF16), ((slot_rows, 1), F32)],
        args=(routes, swap(routes, "ep", 1)),
    )
    early = experts * 3 // 4
    squares, rows, gate_a, up_a = kernel_call(
        functools.partial(first_half_body, slots),
        [
            ((slot_rows, 1), F32),
            ((slot_rows, half_width), BF16),
            ((slots * early, hidden_units), F32),
            ((slots * early, hidden_units), F32),
        ],
        args=(mine, theirs, gain, w_gate, w_up, pick),
    )
    from_x, squares = lax.optimization_barrier((from_x, squares))
    (mine_x,) = kernel_call(join_body, [((tokens + TAIL, cols), BF16)], args=from_x)
    theirs_x = swap(mine_x, "tp")
    gate_b, up_b = kernel_call(
        functools.partial(more_first_half_body, slots, early),
        [((slots * (experts - early), hidden_units), F32)] * 2,
        args=(rows, w_gate, w_up),
    )
    (act,) = kernel_call(
        functools.partial(second_half_body, slots),
        [((slot_rows, hidden_units), BF16)],
        scratch=[pltpu.VMEM((slot_rows, half_width), BF16), pltpu.VMEM((slot_rows, 1), F32)],
        args=(
            mine_x, theirs_x, w_gate, w_up, pick, squares, gate_a, up_a, gate_b, up_b,
        ),
    )

    def down(act, other_half, other_core):
        return kernel_call(
            functools.partial(down_body, other_half, other_core),
            [((tokens, cols), BF16 if other_core else F32)],
            scratch=[pltpu.VMEM((slot_rows, cols), BF16)],
            flops=10**9,
            args=(act, gate, pick, w_down),
        )[0]

    got_a = swap(down(act, True, True), "tp")
    keep_a = down(act, True, False)
    sums = kernel_call(pair_sum_body, [((token_rows, cols), BF16)] * blocks, args=(keep_a, got_a))
    act, sums = lax.optimization_barrier((act, sums))
    from_x = [swap(v, "half") for v in sums]
    got_b = swap(down(act, False, True), "tp")
    keep_b = down(act, False, False)

    home = []
    for j in range(blocks - 1, 0, -1):
        (total,) = kernel_call(
            functools.partial(block_sum_body, j * token_rows),
            [((token_rows, cols), BF16)],
            args=(keep_b, got_b, from_x[j]),
        )
        home.append(swap(total, "ep", j))
    (out,) = kernel_call(
        final_body, [((token_rows, cols), BF16)], args=(h32, keep_b, got_b, from_x[0], *home)
    )
    return out


def solution(mesh):
    placed = (
        P(("groups", "ep", "half"), "tp"),
        P(("groups", "ep", "half"), "tp"),
        P(("groups", "ep", "half"), "tp"),
        P(("groups", "ep", "half"), "tp", None, None),
        P(("groups", "ep", "half"), "tp", None, None),
        P(("groups", "ep", "half")),
        P("tp", "half"),
        P(("groups", "ep"), "half"),
        P("half"),
        P(("groups", "ep"), None),
        P(("groups", "ep"), None),
        P(("ep", "tp"), "half", None),
        P(("ep", "tp"), "half", None),
        P(("ep", "tp"), "half", None),
    )
    few = mesh.shape["half"] == 2 and mesh.shape["tp"] == 2 and mesh.shape["ep"] == 4

    def on_device(*args):
        return by_rows(*args) if few else by_slots(*args)

    return jax.shard_map(
        on_device,
        mesh=mesh,
        in_specs=placed,
        out_specs=P(("groups", "ep"), ("half", "tp")),
        check_vma=False,
    )
```

```python
import functools
import math

import jax
import jax.numpy as jnp
from jax import lax
from jax.experimental import pallas as pl
from jax.experimental.pallas import tpu as pltpu
from jax.sharding import PartitionSpec as P


EXPERTS = 64


EPSILON = 1e-06

MIB = 2**20


def attend(queries, new_keys, new_values, cache_keys, cache_values, lengths):
    requests, key_heads, context, head_size = cache_keys.shape
    sharing = queries.shape[1] // (key_heads * head_size)
    query_blocks = queries.reshape(requests, key_heads, sharing, head_size)
    score_scale = 1.0 / math.sqrt(head_size)
    scores = (
        jnp.einsum("rkgd,rkcd->rkgc", query_blocks, cache_keys, preferred_element_type=jnp.float32)
        * score_scale
    )
    own_score = (
        jnp.einsum(
            "rkgd,rkd->rkg",
            query_blocks,
            new_keys.reshape(requests, key_heads, head_size),
            preferred_element_type=jnp.float32,
        )
        * score_scale
    )
    valid = lax.iota(jnp.int32, context)[None, :] < lengths[:, None]
    scores = jnp.where(valid[:, None, None, :], scores, -1e30)
    highest = jnp.maximum(jnp.max(scores, axis=-1), own_score)
    weights = jnp.exp(scores - highest[..., None])
    own_weight = jnp.exp(own_score - highest)
    denominator = jnp.sum(weights, axis=-1) + own_weight
    probs = (weights / denominator[..., None]).astype(jnp.bfloat16)
    own_prob = (own_weight / denominator).astype(jnp.bfloat16)
    mixture = jnp.einsum("rkgc,rkcd->rkgd", probs, cache_values, preferred_element_type=jnp.float32)
    mixture = mixture + own_prob.astype(jnp.float32)[..., None] * new_values.reshape(
        requests, key_heads, 1, head_size
    ).astype(jnp.float32)
    return mixture.astype(jnp.bfloat16).reshape(requests, key_heads * sharing * head_size)


def combine_rows(returned_rows, target, gates):
    token_rows, top_count = target.shape
    safe_target = jnp.maximum(target, 0).reshape(-1)
    picked = jnp.take(returned_rows, safe_target, axis=0).reshape(
        token_rows, top_count, returned_rows.shape[1]
    )
    weighting = jnp.where(target >= 0, gates, 0.0)
    return jnp.sum(picked.astype(jnp.float32) * weighting[..., None], axis=1)


def by_slots(
    queries,
    new_keys,
    new_values,
    cache_keys,
    cache_values,
    lengths,
    out_weight,
    residual,
    norm_gain,
    expert_ids,
    gate_weights,
    w_gate,
    w_up,
    w_down,
):
    attended = attend(queries, new_keys, new_values, cache_keys, cache_values, lengths)
    partial_mix = jnp.dot(
        lax.all_gather(attended, "half", axis=0, tiled=True),
        out_weight,
        preferred_element_type=jnp.float32,
    )
    mixed = lax.psum(partial_mix.astype(jnp.bfloat16), "tp").astype(jnp.float32)
    hidden = residual.astype(jnp.float32) + mixed
    squares = lax.psum(jnp.sum(hidden * hidden, axis=1), "half")
    half_width = hidden.shape[1]
    width = half_width * lax.axis_size("half")
    normed = (hidden * lax.rsqrt(squares / width + EPSILON)[:, None] * norm_gain[None, :]).astype(
        jnp.bfloat16
    )
    token_rows, top_count = expert_ids.shape
    ep_count = lax.axis_size("ep")
    tp_count = lax.axis_size("tp")
    local_experts = w_gate.shape[0]
    capacity = token_rows * top_count * 3 // (2 * EXPERTS)
    slot_count = ep_count * local_experts * capacity
    flat_ids = expert_ids.reshape(-1)
    one_hot = (flat_ids[:, None] == lax.iota(jnp.int32, EXPERTS)[None, :]).astype(jnp.int32)
    earlier = jnp.cumsum(one_hot, axis=0) - one_hot
    slot = jnp.sum(earlier * one_hot, axis=1)
    owner_ep = flat_ids // (local_experts * tp_count)
    owner_tp = flat_ids // local_experts % tp_count
    target = owner_ep * (local_experts * capacity) + flat_ids % local_experts * capacity + slot
    target = jnp.where(owner_tp == lax.axis_index("tp"), target, -1).reshape(token_rows, top_count)
    dispatch_matrix = jnp.any(
        lax.iota(jnp.int32, slot_count)[:, None, None] == target[None, :, :], axis=2
    ).astype(jnp.bfloat16)
    gates = gate_weights / jnp.sum(gate_weights, axis=1, keepdims=True)
    full_rows = lax.all_gather(normed, "half", axis=1, tiled=True)
    outgoing = jnp.dot(dispatch_matrix, full_rows, preferred_element_type=jnp.float32).astype(
        jnp.bfloat16
    )
    arrived = lax.all_to_all(
        outgoing.reshape(ep_count, local_experts, capacity, width),
        "ep",
        split_axis=0,
        concat_axis=0,
        tiled=True,
    )
    gate_part = jnp.einsum("secd,efd->secf", arrived, w_gate, preferred_element_type=jnp.float32)
    up_part = jnp.einsum("secd,efd->secf", arrived, w_up, preferred_element_type=jnp.float32)
    activation = (jax.nn.silu(gate_part) * up_part).astype(jnp.bfloat16)
    expert_out = jnp.einsum(
        "secf,efd->secd", activation, w_down, preferred_element_type=jnp.float32
    ).astype(jnp.bfloat16)
    summed = lax.psum_scatter(
        expert_out.astype(jnp.float32).astype(jnp.bfloat16), "half", scatter_dimension=3, tiled=True
    ).astype(jnp.float32)
    returned = lax.all_to_all(
        summed.reshape(ep_count, local_experts * capacity, half_width).astype(jnp.bfloat16),
        "ep",
        split_axis=0,
        concat_axis=0,
        tiled=True,
    ).astype(jnp.float32)
    term = combine_rows(returned.reshape(slot_count, half_width), target, gates)
    expert_sum = lax.psum_scatter(
        term.astype(jnp.bfloat16), "tp", scatter_dimension=1, tiled=True
    ).astype(jnp.float32)
    slice_width = expert_sum.shape[1]
    own_columns = lax.dynamic_slice_in_dim(
        hidden, lax.axis_index("tp") * slice_width, slice_width, 1
    )
    return (own_columns + expert_sum).astype(jnp.bfloat16)


VMEM_SPEC = pl.BlockSpec(memory_space=pltpu.VMEM)
HBM_SPEC = pl.BlockSpec(memory_space=pltpu.HBM)
SMEM_SPEC = pl.BlockSpec(memory_space=pltpu.SMEM)
NT = (((1,), (1,)), ((), ()))
TN = (((0,), (0,)), ((), ()))
F32 = jnp.float32
BF16 = jnp.bfloat16


def kernel_call(body, outs, specs=None, scratch=(), flops=1000, vmem=8, args=()):
    return pallas_kernel(body, outs, specs, scratch, flops, vmem, args)


def pallas_kernel(body, outs, specs, scratch, flops, vmem, args):
    return pl.pallas_call(
        body,
        out_shape=tuple(jax.ShapeDtypeStruct(s, d) for s, d in outs),
        in_specs=specs or [VMEM_SPEC] * len(args),
        out_specs=tuple(VMEM_SPEC for _ in outs),
        scratch_shapes=list(scratch),
        cost_estimate=pl.CostEstimate(flops=flops, bytes_accessed=1000, transcendentals=0),
        compiler_params=pltpu.CompilerParams(vmem_limit_bytes=vmem * MIB),
    )(*args)


def load_body(*refs):
    count = len(refs) // 2
    sems = refs[-1]
    copies = [
        pltpu.make_async_copy(refs[i], refs[count + i], sems.at[i]) for i in range(count)
    ]
    for copy in copies:
        copy.start()
    for copy in copies:
        copy.wait()


def attend_body(sharing, context, q_ref, nk_ref, nv_ref, k_ref, v_ref, len_ref, out_ref):
    requests = q_ref.shape[0]
    head_size = nk_ref.shape[1]
    group = 8
    rows = group * sharing
    keys = group * context
    score_scale = 1.0 / math.sqrt(head_size)
    lane = lax.broadcasted_iota(jnp.int32, (rows, keys), 1)
    position = jnp.where(
        lane // context == lax.broadcasted_iota(jnp.int32, (rows, keys), 0) % group,
        lane % context,
        context,
    )
    request = lax.broadcasted_iota(jnp.int32, (group, requests), 1)
    offset = request - lax.broadcasted_iota(jnp.int32, (group, requests), 0)
    for j in range(requests // group):
        here = slice(group * j, group * (j + 1))
        q = q_ref[here, :].astype(F32)
        q = jnp.concatenate(
            [q[:, g * head_size : (g + 1) * head_size] for g in range(sharing)], axis=0
        )
        own_key = jnp.concatenate([nk_ref[here, :].astype(F32)] * sharing, axis=0)
        own_value = jnp.concatenate([nv_ref[here, :].astype(F32)] * sharing, axis=0)
        length = jnp.sum(
            jnp.where(offset == group * j, len_ref[...], 0).astype(F32), axis=1, keepdims=True
        ).astype(jnp.int32)
        length = jnp.concatenate([length] * sharing, axis=0)
        scores = (
            lax.dot_general(
                q.astype(BF16), k_ref[keys * j : keys * (j + 1), :], NT, preferred_element_type=F32
            )
            * score_scale
        )
        scores = jnp.where(position < length, scores, -1e30)
        own_score = jnp.sum(q * own_key, axis=1, keepdims=True) * score_scale
        highest = jnp.maximum(jnp.max(scores, axis=1, keepdims=True), own_score)
        weights = jnp.exp(scores - highest)
        own_weight = jnp.exp(own_score - highest)
        inverse = 1.0 / (jnp.sum(weights, axis=1, keepdims=True) + own_weight)
        probs = (weights * inverse).astype(BF16)
        own_prob = (own_weight * inverse).astype(BF16).astype(F32)
        mixture = jnp.dot(probs, v_ref[keys * j : keys * (j + 1), :], preferred_element_type=F32)
        mixture = (mixture + own_prob * own_value).astype(BF16)
        for g in range(sharing):
            out_ref[here, g * head_size : (g + 1) * head_size] = mixture[group * g : group * (g + 1), :]


def project_body(own_ref, other_ref, w_ref, keep_ref, send_ref, rows_ref):
    x = lax.axis_index("half")
    t = lax.axis_index("tp")
    count = own_ref.shape[0]
    cols = keep_ref.shape[1]
    rows_ref[pl.ds(pl.multiple_of(x * count, count), count), :] = own_ref[...]
    rows_ref[pl.ds(pl.multiple_of((1 - x) * count, count), count), :] = other_ref[...]
    rows = rows_ref[...]
    send_ref[...] = jnp.dot(
        rows, w_ref[:, pl.ds(pl.multiple_of((1 - t) * cols, cols), cols)], preferred_element_type=F32
    )
    keep_ref[...] = jnp.dot(
        rows, w_ref[:, pl.ds(pl.multiple_of(t * cols, cols), cols)], preferred_element_type=F32
    )


LANES = 128
TAIL = 8


def route_body(ids_ref, gw_ref, out_ref, tail_ref):
    rows = ids_ref.shape[1]
    gw = gw_ref[...]
    gates = gw / jnp.sum(gw, axis=0, keepdims=True)
    high = gates.astype(BF16).astype(F32)
    tail_ref[...] = jnp.zeros(tail_ref.shape, F32)
    tail_ref[:, 0:rows] = ids_ref[...].astype(F32)
    tail_ref[:, LANES : LANES + rows] = high
    tail_ref[:, 2 * LANES : 2 * LANES + rows] = gates - high
    out_ref[...] = tail_ref[...].astype(BF16)


def stack_body(first_ref, second_ref, out_ref):
    out_ref[0:TAIL, :] = first_ref[...]
    out_ref[TAIL:, :] = second_ref[...]


def hidden_body(res_ref, gain_ref, keep_ref, got_ref, h32_ref, h16_ref, load_ref, tail_ref):
    t = lax.axis_index("tp")
    rows, cols = keep_ref.shape
    here = pl.ds(pl.multiple_of(t * cols, cols), cols)
    hidden = res_ref[:, here].astype(F32) + (keep_ref[...] + got_ref[...])
    h32_ref[...] = hidden
    h16_ref[...] = hidden.astype(BF16)
    load_ref[0:rows, :] = hidden.astype(BF16)
    gain = gain_ref[:, here]
    gain_high = gain.astype(BF16).astype(F32)
    tail_ref[...] = jnp.zeros(tail_ref.shape, F32)
    for i in range(cols // LANES):
        part = slice(LANES * i, LANES * (i + 1))
        tail_ref[i : i + 1, 0:LANES] = gain_high[:, part]
        tail_ref[TAIL // 2 + i : TAIL // 2 + i + 1, 0:LANES] = (gain - gain_high)[:, part]
    load_ref[rows:, :] = tail_ref[...].astype(BF16)


def merge_body(*refs):
    all_ref = refs[-1]
    rows = refs[0].shape[0]
    for j, ref in enumerate(refs[:-1]):
        all_ref[rows * j : rows * (j + 1), :] = ref[...]


def join_body(load_ref, *refs):
    out_ref = refs[-1]
    rows = load_ref.shape[0] - TAIL
    out_ref[0:rows, :] = load_ref[0:rows, :]
    for j, ref in enumerate(refs[:-1]):
        out_ref[rows * (j + 1) : rows * (j + 2), :] = ref[...]
    out_ref[out_ref.shape[0] - TAIL :, :] = load_ref[rows:, :]


def pick_body(mine_ref, theirs_ref, pick_ref, gate_ref):
    slot_rows, tokens = pick_ref.shape
    blocks = 2 * mine_ref.shape[0] // TAIL
    token_rows = tokens // blocks
    experts = EXPERTS // (lax.axis_size("ep") * lax.axis_size("tp"))
    slots = slot_rows // experts
    low = lax.broadcasted_iota(jnp.int32, (TAIL, LANES), 1) < token_rows
    tails = [
        ref[start : start + TAIL, :].astype(F32)
        for start in range(0, mine_ref.shape[0], TAIL)
        for ref in (mine_ref, theirs_ref)
    ]

    def side_by_side(values):
        pairs = [
            jnp.where(low, values[j], pltpu.roll(values[j + 1], LANES - token_rows, 1))
            for j in range(0, blocks, 2)
        ]
        return jnp.concatenate(pairs, axis=1)

    ids = side_by_side([v[:, 0:LANES] for v in tails])
    gates = side_by_side([v[:, LANES : 2 * LANES] + v[:, 2 * LANES : 3 * LANES] for v in tails])
    first = (lax.axis_index("ep") * lax.axis_size("tp") + lax.axis_index("tp")) * experts
    number = (first + lax.broadcasted_iota(jnp.int32, (experts, TAIL, tokens), 0)).astype(F32)
    named = ids[None] == number
    chosen = jnp.sum(jnp.where(named, 1.0, 0.0), axis=1)
    gate = jnp.sum(jnp.where(named, gates[None], 0.0), axis=1)
    before = (
        lax.broadcasted_iota(jnp.int32, (tokens, tokens), 0)
        < lax.broadcasted_iota(jnp.int32, (tokens, tokens), 1)
    )
    earlier = jnp.dot(
        chosen.astype(BF16), jnp.where(before, 1.0, 0.0).astype(BF16), preferred_element_type=F32
    )
    place = jnp.where(chosen > 0.0, earlier, -1.0)
    slot = lax.broadcasted_iota(jnp.int32, (experts, slots, tokens), 1).astype(F32)
    pick = jnp.where(slot == place[:, None, :], 1.0, 0.0)
    gate_ref[...] = jnp.sum(pick * gate[:, None, :], axis=2, keepdims=True).reshape(
        slot_rows, 1
    )
    pick_ref[...] = pick.reshape(slot_rows, tokens).astype(BF16)


def gathered_rows(pick, parts, rows_ref):
    total = 0.0
    tokens = pick.shape[1]
    for owner, ref, gain in parts:
        cols = ref.shape[1]
        rows = jnp.dot(pick, ref[0:tokens, :], preferred_element_type=F32)
        total = total + jnp.sum(rows * rows, axis=1, keepdims=True)
        rows_ref[:, pl.ds(pl.multiple_of(owner * cols, cols), cols)] = (rows * gain).astype(BF16)
    return total


def tail_gain(ref):
    rows, cols = ref.shape
    tail = ref[rows - TAIL :, 0:LANES].astype(F32)
    gain = tail + pltpu.roll(tail, TAIL // 2, 0)
    return jnp.concatenate([gain[i : i + 1, :] for i in range(cols // LANES)], axis=1)


def products(rows_ref, w_ref, e, slots, start):
    half_width = rows_ref.shape[1]
    return lax.dot_general(
        w_ref[e, :, pl.ds(pl.multiple_of(start, half_width), half_width)],
        rows_ref[slots * e : slots * (e + 1), :],
        NT,
        preferred_element_type=F32,
    ).T


def first_half_body(
    slots, mine_ref, theirs_ref, gain_ref, wg_ref, wu_ref, pick_ref, squares_ref, rows_ref, ga_ref, ua_ref
):
    t = lax.axis_index("tp")
    cols = mine_ref.shape[1]
    parts = [
        (owner, ref, gain_ref[:, pl.ds(pl.multiple_of(owner * cols, cols), cols)])
        for owner, ref in ((t, mine_ref), (1 - t, theirs_ref))
    ]
    squares_ref[...] = gathered_rows(pick_ref[...], parts, rows_ref)
    start = lax.axis_index("half") * rows_ref.shape[1]
    for e in range(ga_ref.shape[0] // slots):
        here = slice(slots * e, slots * (e + 1))
        ga_ref[here, :] = products(rows_ref, wg_ref, e, slots, start)
        ua_ref[here, :] = products(rows_ref, wu_ref, e, slots, start)


def more_first_half_body(slots, done, rows_ref, wg_ref, wu_ref, ga_ref, ua_ref):
    start = lax.axis_index("half") * rows_ref.shape[1]
    for e in range(ga_ref.shape[0] // slots):
        here = slice(slots * e, slots * (e + 1))
        ga_ref[here, :] = products(rows_ref, wg_ref, done + e, slots, start)
        ua_ref[here, :] = products(rows_ref, wu_ref, done + e, slots, start)


def second_half_body(
    slots, mine_ref, theirs_ref, wg_ref, wu_ref, pick_ref, squares_ref, ga_ref, ua_ref, gb_ref, ub_ref,
    act_ref, rows_ref, inv_ref,
):
    experts, _, width = wg_ref.shape
    t = lax.axis_index("tp")
    parts = [(t, mine_ref, tail_gain(mine_ref)), (1 - t, theirs_ref, tail_gain(theirs_ref))]
    squares = gathered_rows(pick_ref[...], parts, rows_ref)
    inv_ref[...] = lax.rsqrt((squares_ref[...] + squares) / width + EPSILON)
    start = (1 - lax.axis_index("half")) * rows_ref.shape[1]
    done = ga_ref.shape[0] // slots
    for e in range(experts):
        here = slice(slots * e, slots * (e + 1))
        gate_acc, up_acc = (ga_ref, ua_ref) if e < done else (gb_ref, ub_ref)
        row = slots * (e if e < done else e - done)
        there = slice(row, row + slots)
        inverse = inv_ref[here, :]
        gate_part = inverse * (gate_acc[there, :] + products(rows_ref, wg_ref, e, slots, start))
        up_part = inverse * (up_acc[there, :] + products(rows_ref, wu_ref, e, slots, start))
        act_ref[here, :] = (jax.nn.silu(gate_part) * up_part).astype(BF16)


def down_body(other_half, other_core, act_ref, gate_ref, pick_ref, wd_ref, out_ref, y_ref):
    experts = wd_ref.shape[0]
    cols = out_ref.shape[1]
    slots = pick_ref.shape[0] // experts
    x, t = lax.axis_index("half"), lax.axis_index("tp")
    quarter = (1 - x if other_half else x) * lax.axis_size("tp") + (1 - t if other_core else t)
    columns = pl.ds(pl.multiple_of(quarter * cols, cols), cols)

    def one(e, carry):
        here = pl.ds(pl.multiple_of(e * slots, slots), slots)
        y = jnp.dot(act_ref[here, :], wd_ref[e, :, columns], preferred_element_type=F32)
        y_ref[here, :] = (y * gate_ref[here, :]).astype(BF16)
        return carry

    lax.fori_loop(0, experts, one, 0, unroll=True)
    out_ref[...] = lax.dot_general(
        pick_ref[...], y_ref[...], TN, preferred_element_type=F32
    ).astype(out_ref.dtype)


def pair_sum_body(keep_ref, got_ref, *outs):
    start = 0
    for out in outs:
        here = slice(start, start + out.shape[0])
        out[...] = (keep_ref[here, :] + got_ref[here, :].astype(F32)).astype(BF16)
        start += out.shape[0]


def block_sum_body(start, keep_ref, got_ref, other_ref, *outs):
    rows = outs[0].shape[0]
    for j, out in enumerate(outs):
        here = slice(start + rows * j, start + rows * (j + 1))
        total = keep_ref[here, :] + got_ref[here, :].astype(F32)
        total = total + other_ref[rows * j : rows * (j + 1), :].astype(F32)
        out[...] = total.astype(BF16)


def final_body(h32_ref, keep_ref, got_ref, *refs):
    out_ref = refs[-1]
    here = slice(0, out_ref.shape[0])
    total = keep_ref[here, :] + got_ref[here, :].astype(F32)
    for ref in refs[:-1]:
        total = total + ref[...].astype(F32)
    out_ref[...] = (h32_ref[...] + total).astype(BF16)


def swap(value, axis, partner=1):
    return lax.ppermute(
        value, axis, [(i, i ^ partner) for i in range(lax.axis_size(axis))]
    )


def by_rows(
    queries,
    new_keys,
    new_values,
    cache_keys,
    cache_values,
    lengths,
    out_weight,
    residual,
    norm_gain,
    expert_ids,
    gate_weights,
    w_gate,
    w_up,
    w_down,
):
    requests, _, context, head_size = cache_keys.shape
    sharing = queries.shape[1] // head_size
    token_rows, top_count = expert_ids.shape
    blocks = lax.axis_size("ep")
    tokens = blocks * token_rows
    experts, hidden_units, _ = w_gate.shape
    half_width = residual.shape[1]
    cols = half_width // lax.axis_size("tp")
    slots = token_rows * top_count * 3 // (2 * EXPERTS) * blocks
    slot_rows = experts * slots
    w_gate, w_up, w_down = (
        pltpu.with_memory_space_constraint(w, pltpu.VMEM) for w in (w_gate, w_up, w_down)
    )

    gain = norm_gain.reshape(1, half_width)
    cache = (requests * context, head_size)
    sources = tuple(
        pltpu.with_memory_space_constraint(v, pltpu.HBM)
        for v in (
            queries,
            new_keys,
            new_values,
            cache_keys.reshape(cache),
            cache_values.reshape(cache),
            lengths.reshape(1, requests),
        )
    )
    loaded = kernel_call(
        load_body,
        [(v.shape, v.dtype) for v in sources],
        specs=[HBM_SPEC] * len(sources),
        scratch=[pltpu.SemaphoreType.DMA((len(sources),))],
        args=sources,
    )
    (attended,) = kernel_call(
        functools.partial(attend_body, sharing, context),
        [((requests, sharing * head_size), BF16)],
        flops=10**11,
        args=loaded,
    )
    other_attended = swap(attended, "half")
    (route,) = kernel_call(
        route_body,
        [((TAIL, 4 * LANES), BF16)],
        scratch=[pltpu.VMEM((TAIL, 4 * LANES), F32)],
        args=(expert_ids.T, gate_weights.T),
    )
    (routes,) = kernel_call(
        stack_body, [((2 * TAIL, 4 * LANES), BF16)], args=(route, swap(route, "ep", 2))
    )
    keep, send = kernel_call(
        project_body,
        [((token_rows, cols), F32)] * 2,
        scratch=[pltpu.VMEM((token_rows, sharing * head_size), BF16)],
        args=(attended, other_attended, out_weight),
    )
    h32, h16, payload = kernel_call(
        hidden_body,
        [((token_rows, cols), F32), ((token_rows, cols), BF16), ((token_rows + TAIL, cols), BF16)],
        scratch=[pltpu.VMEM((TAIL, cols), F32)],
        args=(residual, gain, keep, swap(send, "tp")),
    )
    arrived = [h16] + [swap(h16, "ep", j) for j in range(1, blocks)]
    from_x = [swap(payload if j == 0 else v, "half") for j, v in enumerate(arrived)]
    (mine,) = kernel_call(merge_body, [((tokens, cols), BF16)], args=arrived)
    theirs = swap(mine, "tp")
    pick, gate = kernel_call(
        pick_body,
        [((slot_rows, tokens), BF16), ((slot_rows, 1), F32)],
        args=(routes, swap(routes, "ep", 1)),
    )
    early = experts * 3 // 4
    squares, rows, gate_a, up_a = kernel_call(
        functools.partial(first_half_body, slots),
        [
            ((slot_rows, 1), F32),
            ((slot_rows, half_width), BF16),
            ((slots * early, hidden_units), F32),
            ((slots * early, hidden_units), F32),
        ],
        args=(mine, theirs, gain, w_gate, w_up, pick),
    )
    from_x, squares = lax.optimization_barrier((from_x, squares))
    (mine_x,) = kernel_call(join_body, [((tokens + TAIL, cols), BF16)], args=from_x)
    theirs_x = swap(mine_x, "tp")
    gate_b, up_b = kernel_call(
        functools.partial(more_first_half_body, slots, early),
        [((slots * (experts - early), hidden_units), F32)] * 2,
        args=(rows, w_gate, w_up),
    )
    (act,) = kernel_call(
        functools.partial(second_half_body, slots),
        [((slot_rows, hidden_units), BF16)],
        scratch=[pltpu.VMEM((slot_rows, half_width), BF16), pltpu.VMEM((slot_rows, 1), F32)],
        args=(
            mine_x, theirs_x, w_gate, w_up, pick, squares, gate_a, up_a, gate_b, up_b,
        ),
    )

    def down(act, other_half, other_core):
        return kernel_call(
            functools.partial(down_body, other_half, other_core),
            [((tokens, cols), BF16 if other_core else F32)],
            scratch=[pltpu.VMEM((slot_rows, cols), BF16)],
            flops=10**9,
            args=(act, gate, pick, w_down),
        )[0]

    got_a = swap(down(act, True, True), "tp")
    keep_a = down(act, True, False)
    sums = kernel_call(
        pair_sum_body,
        [((n * token_rows, cols), BF16) for n in (1, blocks - 2, 1)],
        args=(keep_a, got_a),
    )
    act, sums = lax.optimization_barrier((act, sums))
    from_x = [swap(v, "half") for v in sums]
    got_b = swap(down(act, False, True), "tp")
    keep_b = down(act, False, False)

    totals = []
    for start, count, other in ((blocks - 1, 1, from_x[2]), (1, blocks - 2, from_x[1])):
        totals += kernel_call(
            functools.partial(block_sum_body, start * token_rows),
            [((token_rows, cols), BF16)] * count,
            args=(keep_b, got_b, other),
        )
    partners = (blocks - 1, *range(1, blocks - 1))
    home = [swap(v, "ep", j) for j, v in zip(partners, totals)]
    (out,) = kernel_call(
        final_body, [((token_rows, cols), BF16)], args=(h32, keep_b, got_b, from_x[0], *home)
    )
    return out


def rows_fit(*args):
    residual, expert_ids = args[7], args[9]
    token_rows, top_count = expert_ids.shape
    cols = residual.shape[1] // lax.axis_size("tp")
    return 2 * token_rows == LANES and top_count == TAIL and cols == TAIL // 2 * LANES


def solution(mesh):
    placed = (
        P(("groups", "ep", "half"), "tp"),
        P(("groups", "ep", "half"), "tp"),
        P(("groups", "ep", "half"), "tp"),
        P(("groups", "ep", "half"), "tp", None, None),
        P(("groups", "ep", "half"), "tp", None, None),
        P(("groups", "ep", "half")),
        P("tp", "half"),
        P(("groups", "ep"), "half"),
        P("half"),
        P(("groups", "ep"), None),
        P(("groups", "ep"), None),
        P(("ep", "tp"), "half", None),
        P(("ep", "tp"), "half", None),
        P(("ep", "tp"), "half", None),
    )
    few = mesh.shape["half"] == 2 and mesh.shape["tp"] == 2 and mesh.shape["ep"] == 4

    def on_device(*args):
        return by_rows(*args) if few and rows_fit(*args) else by_slots(*args)

    return jax.shard_map(
        on_device,
        mesh=mesh,
        in_specs=placed,
        out_specs=P(("groups", "ep"), ("half", "tp")),
        check_vma=False,
    )
```

```python
import functools
import math

import jax
import jax.numpy as jnp
from jax import lax
from jax.experimental import pallas as pl
from jax.experimental.pallas import tpu as pltpu
from jax.sharding import PartitionSpec as P


EXPERTS = 64


EPSILON = 1e-06

MIB = 2**20


def attend(queries, new_keys, new_values, cache_keys, cache_values, lengths):
    requests, key_heads, context, head_size = cache_keys.shape
    sharing = queries.shape[1] // (key_heads * head_size)
    query_blocks = queries.reshape(requests, key_heads, sharing, head_size)
    score_scale = 1.0 / math.sqrt(head_size)
    scores = (
        jnp.einsum("rkgd,rkcd->rkgc", query_blocks, cache_keys, preferred_element_type=jnp.float32)
        * score_scale
    )
    own_score = (
        jnp.einsum(
            "rkgd,rkd->rkg",
            query_blocks,
            new_keys.reshape(requests, key_heads, head_size),
            preferred_element_type=jnp.float32,
        )
        * score_scale
    )
    valid = lax.iota(jnp.int32, context)[None, :] < lengths[:, None]
    scores = jnp.where(valid[:, None, None, :], scores, -1e30)
    highest = jnp.maximum(jnp.max(scores, axis=-1), own_score)
    weights = jnp.exp(scores - highest[..., None])
    own_weight = jnp.exp(own_score - highest)
    denominator = jnp.sum(weights, axis=-1) + own_weight
    probs = (weights / denominator[..., None]).astype(jnp.bfloat16)
    own_prob = (own_weight / denominator).astype(jnp.bfloat16)
    mixture = jnp.einsum("rkgc,rkcd->rkgd", probs, cache_values, preferred_element_type=jnp.float32)
    mixture = mixture + own_prob.astype(jnp.float32)[..., None] * new_values.reshape(
        requests, key_heads, 1, head_size
    ).astype(jnp.float32)
    return mixture.astype(jnp.bfloat16).reshape(requests, key_heads * sharing * head_size)


def combine_rows(returned_rows, target, gates):
    token_rows, top_count = target.shape
    safe_target = jnp.maximum(target, 0).reshape(-1)
    picked = jnp.take(returned_rows, safe_target, axis=0).reshape(
        token_rows, top_count, returned_rows.shape[1]
    )
    weighting = jnp.where(target >= 0, gates, 0.0)
    return jnp.sum(picked.astype(jnp.float32) * weighting[..., None], axis=1)


def by_slots(
    queries,
    new_keys,
    new_values,
    cache_keys,
    cache_values,
    lengths,
    out_weight,
    residual,
    norm_gain,
    expert_ids,
    gate_weights,
    w_gate,
    w_up,
    w_down,
):
    attended = attend(queries, new_keys, new_values, cache_keys, cache_values, lengths)
    partial_mix = jnp.dot(
        lax.all_gather(attended, "half", axis=0, tiled=True),
        out_weight,
        preferred_element_type=jnp.float32,
    )
    mixed = lax.psum(partial_mix.astype(jnp.bfloat16), "tp").astype(jnp.float32)
    hidden = residual.astype(jnp.float32) + mixed
    squares = lax.psum(jnp.sum(hidden * hidden, axis=1), "half")
    half_width = hidden.shape[1]
    width = half_width * lax.axis_size("half")
    normed = (hidden * lax.rsqrt(squares / width + EPSILON)[:, None] * norm_gain[None, :]).astype(
        jnp.bfloat16
    )
    token_rows, top_count = expert_ids.shape
    ep_count = lax.axis_size("ep")
    tp_count = lax.axis_size("tp")
    local_experts = w_gate.shape[0]
    capacity = token_rows * top_count * 3 // (2 * EXPERTS)
    slot_count = ep_count * local_experts * capacity
    flat_ids = expert_ids.reshape(-1)
    one_hot = (flat_ids[:, None] == lax.iota(jnp.int32, EXPERTS)[None, :]).astype(jnp.int32)
    earlier = jnp.cumsum(one_hot, axis=0) - one_hot
    slot = jnp.sum(earlier * one_hot, axis=1)
    owner_ep = flat_ids // (local_experts * tp_count)
    owner_tp = flat_ids // local_experts % tp_count
    target = owner_ep * (local_experts * capacity) + flat_ids % local_experts * capacity + slot
    target = jnp.where(owner_tp == lax.axis_index("tp"), target, -1).reshape(token_rows, top_count)
    dispatch_matrix = jnp.any(
        lax.iota(jnp.int32, slot_count)[:, None, None] == target[None, :, :], axis=2
    ).astype(jnp.bfloat16)
    gates = gate_weights / jnp.sum(gate_weights, axis=1, keepdims=True)
    full_rows = lax.all_gather(normed, "half", axis=1, tiled=True)
    outgoing = jnp.dot(dispatch_matrix, full_rows, preferred_element_type=jnp.float32).astype(
        jnp.bfloat16
    )
    arrived = lax.all_to_all(
        outgoing.reshape(ep_count, local_experts, capacity, width),
        "ep",
        split_axis=0,
        concat_axis=0,
        tiled=True,
    )
    gate_part = jnp.einsum("secd,efd->secf", arrived, w_gate, preferred_element_type=jnp.float32)
    up_part = jnp.einsum("secd,efd->secf", arrived, w_up, preferred_element_type=jnp.float32)
    activation = (jax.nn.silu(gate_part) * up_part).astype(jnp.bfloat16)
    expert_out = jnp.einsum(
        "secf,efd->secd", activation, w_down, preferred_element_type=jnp.float32
    ).astype(jnp.bfloat16)
    summed = lax.psum_scatter(
        expert_out.astype(jnp.float32).astype(jnp.bfloat16), "half", scatter_dimension=3, tiled=True
    ).astype(jnp.float32)
    returned = lax.all_to_all(
        summed.reshape(ep_count, local_experts * capacity, half_width).astype(jnp.bfloat16),
        "ep",
        split_axis=0,
        concat_axis=0,
        tiled=True,
    ).astype(jnp.float32)
    term = combine_rows(returned.reshape(slot_count, half_width), target, gates)
    expert_sum = lax.psum_scatter(
        term.astype(jnp.bfloat16), "tp", scatter_dimension=1, tiled=True
    ).astype(jnp.float32)
    slice_width = expert_sum.shape[1]
    own_columns = lax.dynamic_slice_in_dim(
        hidden, lax.axis_index("tp") * slice_width, slice_width, 1
    )
    return (own_columns + expert_sum).astype(jnp.bfloat16)


VMEM_SPEC = pl.BlockSpec(memory_space=pltpu.VMEM)
HBM_SPEC = pl.BlockSpec(memory_space=pltpu.HBM)
SMEM_SPEC = pl.BlockSpec(memory_space=pltpu.SMEM)
NT = (((1,), (1,)), ((), ()))
TN = (((0,), (0,)), ((), ()))
F32 = jnp.float32
BF16 = jnp.bfloat16


def kernel_call(body, outs, specs=None, scratch=(), flops=1000, vmem=8, args=()):
    return pallas_kernel(body, outs, specs, scratch, flops, vmem, args)


def pallas_kernel(body, outs, specs, scratch, flops, vmem, args):
    return pl.pallas_call(
        body,
        out_shape=tuple(jax.ShapeDtypeStruct(s, d) for s, d in outs),
        in_specs=specs or [VMEM_SPEC] * len(args),
        out_specs=tuple(VMEM_SPEC for _ in outs),
        scratch_shapes=list(scratch),
        cost_estimate=pl.CostEstimate(flops=flops, bytes_accessed=1000, transcendentals=0),
        compiler_params=pltpu.CompilerParams(vmem_limit_bytes=vmem * MIB),
    )(*args)


def load_body(*refs):
    count = len(refs) // 2
    sems = refs[-1]
    copies = [
        pltpu.make_async_copy(refs[i], refs[count + i], sems.at[i]) for i in range(count)
    ]
    for copy in copies:
        copy.start()
    for copy in copies:
        copy.wait()


def attend_body(sharing, context, q_ref, nk_ref, nv_ref, k_ref, v_ref, len_ref, out_ref):
    requests = q_ref.shape[0]
    head_size = nk_ref.shape[1]
    group = 8
    rows = group * sharing
    keys = group * context
    score_scale = 1.0 / math.sqrt(head_size)
    lane = lax.broadcasted_iota(jnp.int32, (rows, keys), 1)
    position = jnp.where(
        lane // context == lax.broadcasted_iota(jnp.int32, (rows, keys), 0) % group,
        lane % context,
        context,
    )
    request = lax.broadcasted_iota(jnp.int32, (group, requests), 1)
    offset = request - lax.broadcasted_iota(jnp.int32, (group, requests), 0)
    for j in range(requests // group):
        here = slice(group * j, group * (j + 1))
        q = q_ref[here, :].astype(F32)
        q = jnp.concatenate(
            [q[:, g * head_size : (g + 1) * head_size] for g in range(sharing)], axis=0
        )
        own_key = jnp.concatenate([nk_ref[here, :].astype(F32)] * sharing, axis=0)
        own_value = jnp.concatenate([nv_ref[here, :].astype(F32)] * sharing, axis=0)
        length = jnp.sum(
            jnp.where(offset == group * j, len_ref[...], 0).astype(F32), axis=1, keepdims=True
        ).astype(jnp.int32)
        length = jnp.concatenate([length] * sharing, axis=0)
        scores = (
            lax.dot_general(
                q.astype(BF16), k_ref[keys * j : keys * (j + 1), :], NT, preferred_element_type=F32
            )
            * score_scale
        )
        scores = jnp.where(position < length, scores, -1e30)
        own_score = jnp.sum(q * own_key, axis=1, keepdims=True) * score_scale
        highest = jnp.maximum(jnp.max(scores, axis=1, keepdims=True), own_score)
        weights = jnp.exp(scores - highest)
        own_weight = jnp.exp(own_score - highest)
        inverse = 1.0 / (jnp.sum(weights, axis=1, keepdims=True) + own_weight)
        probs = (weights * inverse).astype(BF16)
        own_prob = (own_weight * inverse).astype(BF16).astype(F32)
        mixture = jnp.dot(probs, v_ref[keys * j : keys * (j + 1), :], preferred_element_type=F32)
        mixture = (mixture + own_prob * own_value).astype(BF16)
        for g in range(sharing):
            out_ref[here, g * head_size : (g + 1) * head_size] = mixture[group * g : group * (g + 1), :]


def project_body(own_ref, other_ref, w_ref, keep_ref, send_ref, rows_ref):
    x = lax.axis_index("half")
    t = lax.axis_index("tp")
    count = own_ref.shape[0]
    cols = keep_ref.shape[1]
    rows_ref[pl.ds(pl.multiple_of(x * count, count), count), :] = own_ref[...]
    rows_ref[pl.ds(pl.multiple_of((1 - x) * count, count), count), :] = other_ref[...]
    rows = rows_ref[...]
    send_ref[...] = jnp.dot(
        rows, w_ref[:, pl.ds(pl.multiple_of((1 - t) * cols, cols), cols)], preferred_element_type=F32
    ).astype(BF16)
    keep_ref[...] = jnp.dot(
        rows, w_ref[:, pl.ds(pl.multiple_of(t * cols, cols), cols)], preferred_element_type=F32
    )


LANES = 128
TAIL = 8


def route_body(ids_ref, gw_ref, out_ref, tail_ref):
    rows = ids_ref.shape[1]
    gw = gw_ref[...]
    gates = gw / jnp.sum(gw, axis=0, keepdims=True)
    high = gates.astype(BF16).astype(F32)
    tail_ref[...] = jnp.zeros(tail_ref.shape, F32)
    tail_ref[:, 0:rows] = ids_ref[...].astype(F32)
    tail_ref[:, LANES : LANES + rows] = high
    tail_ref[:, 2 * LANES : 2 * LANES + rows] = gates - high
    out_ref[...] = tail_ref[...].astype(BF16)


def stack_body(first_ref, second_ref, out_ref):
    out_ref[0:TAIL, :] = first_ref[...]
    out_ref[TAIL:, :] = second_ref[...]


def hidden_body(res_ref, gain_ref, keep_ref, got_ref, h32_ref, h16_ref, load_ref, tail_ref):
    t = lax.axis_index("tp")
    rows, cols = keep_ref.shape
    here = pl.ds(pl.multiple_of(t * cols, cols), cols)
    hidden = res_ref[:, here].astype(F32) + (keep_ref[...] + got_ref[...].astype(F32))
    h32_ref[...] = hidden
    h16_ref[...] = hidden.astype(BF16)
    load_ref[0:rows, :] = hidden.astype(BF16)
    gain = gain_ref[:, here]
    gain_high = gain.astype(BF16).astype(F32)
    tail_ref[...] = jnp.zeros(tail_ref.shape, F32)
    for i in range(cols // LANES):
        part = slice(LANES * i, LANES * (i + 1))
        tail_ref[i : i + 1, 0:LANES] = gain_high[:, part]
        tail_ref[TAIL // 2 + i : TAIL // 2 + i + 1, 0:LANES] = (gain - gain_high)[:, part]
    load_ref[rows:, :] = tail_ref[...].astype(BF16)


def merge_body(*refs):
    all_ref = refs[-1]
    rows = refs[0].shape[0]
    for j, ref in enumerate(refs[:-1]):
        all_ref[rows * j : rows * (j + 1), :] = ref[...]


def join_body(load_ref, *refs):
    out_ref = refs[-1]
    rows = load_ref.shape[0] - TAIL
    out_ref[0:rows, :] = load_ref[0:rows, :]
    start = rows
    for ref in refs[:-1]:
        out_ref[start : start + ref.shape[0], :] = ref[...]
        start += ref.shape[0]
    out_ref[start:, :] = load_ref[rows:, :]


def pick_body(mine_ref, theirs_ref, pick_ref, gate_ref):
    slot_rows, tokens = pick_ref.shape
    blocks = 2 * mine_ref.shape[0] // TAIL
    token_rows = tokens // blocks
    experts = EXPERTS // (lax.axis_size("ep") * lax.axis_size("tp"))
    slots = slot_rows // experts
    low = lax.broadcasted_iota(jnp.int32, (TAIL, LANES), 1) < token_rows
    tails = [
        ref[start : start + TAIL, :].astype(F32)
        for start in range(0, mine_ref.shape[0], TAIL)
        for ref in (mine_ref, theirs_ref)
    ]

    def side_by_side(values):
        pairs = [
            jnp.where(low, values[j], pltpu.roll(values[j + 1], LANES - token_rows, 1))
            for j in range(0, blocks, 2)
        ]
        return jnp.concatenate(pairs, axis=1)

    ids = side_by_side([v[:, 0:LANES] for v in tails])
    gates = side_by_side([v[:, LANES : 2 * LANES] + v[:, 2 * LANES : 3 * LANES] for v in tails])
    first = (lax.axis_index("ep") * lax.axis_size("tp") + lax.axis_index("tp")) * experts
    number = (first + lax.broadcasted_iota(jnp.int32, (experts, TAIL, tokens), 0)).astype(F32)
    named = ids[None] == number
    chosen = jnp.sum(jnp.where(named, 1.0, 0.0), axis=1)
    gate = jnp.sum(jnp.where(named, gates[None], 0.0), axis=1)
    before = (
        lax.broadcasted_iota(jnp.int32, (tokens, tokens), 0)
        < lax.broadcasted_iota(jnp.int32, (tokens, tokens), 1)
    )
    earlier = jnp.dot(
        chosen.astype(BF16), jnp.where(before, 1.0, 0.0).astype(BF16), preferred_element_type=F32
    )
    place = jnp.where(chosen > 0.0, earlier, -1.0)
    slot = lax.broadcasted_iota(jnp.int32, (experts, slots, tokens), 1).astype(F32)
    pick = jnp.where(slot == place[:, None, :], 1.0, 0.0)
    gate_ref[...] = jnp.sum(pick * gate[:, None, :], axis=2, keepdims=True).reshape(
        slot_rows, 1
    )
    pick_ref[...] = pick.reshape(slot_rows, tokens).astype(BF16)


def gathered_rows(pick, parts, rows_ref):
    total = 0.0
    tokens = pick.shape[1]
    for owner, ref, gain in parts:
        cols = ref.shape[1]
        rows = jnp.dot(pick, ref[0:tokens, :], preferred_element_type=F32)
        total = total + jnp.sum(rows * rows, axis=1, keepdims=True)
        rows_ref[:, pl.ds(pl.multiple_of(owner * cols, cols), cols)] = (rows * gain).astype(BF16)
    return total


def tail_gain(ref):
    rows, cols = ref.shape
    tail = ref[rows - TAIL :, 0:LANES].astype(F32)
    gain = tail + pltpu.roll(tail, TAIL // 2, 0)
    return jnp.concatenate([gain[i : i + 1, :] for i in range(cols // LANES)], axis=1)


def products(rows_ref, w_ref, e, slots, start):
    half_width = rows_ref.shape[1]
    return lax.dot_general(
        w_ref[e, :, pl.ds(pl.multiple_of(start, half_width), half_width)],
        rows_ref[slots * e : slots * (e + 1), :],
        NT,
        preferred_element_type=F32,
    ).T


def first_half_body(
    slots, mine_ref, theirs_ref, gain_ref, wg_ref, wu_ref, pick_ref, squares_ref, rows_ref, ga_ref, ua_ref
):
    t = lax.axis_index("tp")
    cols = mine_ref.shape[1]
    parts = [
        (owner, ref, gain_ref[:, pl.ds(pl.multiple_of(owner * cols, cols), cols)])
        for owner, ref in ((t, mine_ref), (1 - t, theirs_ref))
    ]
    squares_ref[...] = gathered_rows(pick_ref[...], parts, rows_ref)
    start = lax.axis_index("half") * rows_ref.shape[1]
    for e in range(ga_ref.shape[0] // slots):
        here = slice(slots * e, slots * (e + 1))
        ga_ref[here, :] = products(rows_ref, wg_ref, e, slots, start)
        ua_ref[here, :] = products(rows_ref, wu_ref, e, slots, start)


def more_first_half_body(slots, done, rows_ref, wg_ref, wu_ref, ga_ref, ua_ref):
    start = lax.axis_index("half") * rows_ref.shape[1]
    for e in range(ga_ref.shape[0] // slots):
        here = slice(slots * e, slots * (e + 1))
        ga_ref[here, :] = products(rows_ref, wg_ref, done + e, slots, start)
        ua_ref[here, :] = products(rows_ref, wu_ref, done + e, slots, start)


def second_half_body(
    slots, mine_ref, theirs_ref, wg_ref, wu_ref, pick_ref, squares_ref, ga_ref, ua_ref, gb_ref, ub_ref,
    act_ref, rows_ref, inv_ref,
):
    experts, _, width = wg_ref.shape
    t = lax.axis_index("tp")
    parts = [(t, mine_ref, tail_gain(mine_ref)), (1 - t, theirs_ref, tail_gain(theirs_ref))]
    squares = gathered_rows(pick_ref[...], parts, rows_ref)
    inv_ref[...] = lax.rsqrt((squares_ref[...] + squares) / width + EPSILON)
    start = (1 - lax.axis_index("half")) * rows_ref.shape[1]
    done = ga_ref.shape[0] // slots
    for e in range(experts):
        here = slice(slots * e, slots * (e + 1))
        gate_acc, up_acc = (ga_ref, ua_ref) if e < done else (gb_ref, ub_ref)
        row = slots * (e if e < done else e - done)
        there = slice(row, row + slots)
        inverse = inv_ref[here, :]
        gate_part = inverse * (gate_acc[there, :] + products(rows_ref, wg_ref, e, slots, start))
        up_part = inverse * (up_acc[there, :] + products(rows_ref, wu_ref, e, slots, start))
        act_ref[here, :] = (jax.nn.silu(gate_part) * up_part).astype(BF16)


def down_body(other_half, other_core, act_ref, gate_ref, pick_ref, wd_ref, out_ref, y_ref):
    experts = wd_ref.shape[0]
    cols = out_ref.shape[1]
    slots = pick_ref.shape[0] // experts
    x, t = lax.axis_index("half"), lax.axis_index("tp")
    quarter = (1 - x if other_half else x) * lax.axis_size("tp") + (1 - t if other_core else t)
    columns = pl.ds(pl.multiple_of(quarter * cols, cols), cols)

    def one(e, carry):
        here = pl.ds(pl.multiple_of(e * slots, slots), slots)
        y = jnp.dot(act_ref[here, :], wd_ref[e, :, columns], preferred_element_type=F32)
        y_ref[here, :] = (y * gate_ref[here, :]).astype(BF16)
        return carry

    lax.fori_loop(0, experts, one, 0, unroll=True)
    out_ref[...] = lax.dot_general(
        pick_ref[...], y_ref[...], TN, preferred_element_type=F32
    ).astype(out_ref.dtype)


def pair_sum_body(keep_ref, got_ref, *outs):
    start = 0
    for out in outs:
        here = slice(start, start + out.shape[0])
        out[...] = (keep_ref[here, :] + got_ref[here, :].astype(F32)).astype(BF16)
        start += out.shape[0]


def block_sum_body(start, keep_ref, got_ref, other_ref, *outs):
    rows = outs[0].shape[0]
    for j, out in enumerate(outs):
        here = slice(start + rows * j, start + rows * (j + 1))
        total = keep_ref[here, :] + got_ref[here, :].astype(F32)
        total = total + other_ref[rows * j : rows * (j + 1), :].astype(F32)
        out[...] = total.astype(BF16)


def final_body(h32_ref, keep_ref, got_ref, *refs):
    out_ref = refs[-1]
    here = slice(0, out_ref.shape[0])
    total = keep_ref[here, :] + got_ref[here, :].astype(F32)
    for ref in refs[:-1]:
        total = total + ref[...].astype(F32)
    out_ref[...] = (h32_ref[...] + total).astype(BF16)


def swap(value, axis, partner=1):
    return lax.ppermute(
        value, axis, [(i, i ^ partner) for i in range(lax.axis_size(axis))]
    )


def by_rows(
    queries,
    new_keys,
    new_values,
    cache_keys,
    cache_values,
    lengths,
    out_weight,
    residual,
    norm_gain,
    expert_ids,
    gate_weights,
    w_gate,
    w_up,
    w_down,
):
    requests, _, context, head_size = cache_keys.shape
    sharing = queries.shape[1] // head_size
    token_rows, top_count = expert_ids.shape
    blocks = lax.axis_size("ep")
    tokens = blocks * token_rows
    experts, hidden_units, _ = w_gate.shape
    half_width = residual.shape[1]
    cols = half_width // lax.axis_size("tp")
    slots = token_rows * top_count * 3 // (2 * EXPERTS) * blocks
    slot_rows = experts * slots
    w_gate, w_up, w_down = (
        pltpu.with_memory_space_constraint(w, pltpu.VMEM) for w in (w_gate, w_up, w_down)
    )

    gain = norm_gain.reshape(1, half_width)
    cache = (requests * context, head_size)
    sources = tuple(
        pltpu.with_memory_space_constraint(v, pltpu.HBM)
        for v in (
            queries,
            new_keys,
            new_values,
            cache_keys.reshape(cache),
            cache_values.reshape(cache),
            lengths.reshape(1, requests),
        )
    )
    loaded = kernel_call(
        load_body,
        [(v.shape, v.dtype) for v in sources],
        specs=[HBM_SPEC] * len(sources),
        scratch=[pltpu.SemaphoreType.DMA((len(sources),))],
        args=sources,
    )
    (attended,) = kernel_call(
        functools.partial(attend_body, sharing, context),
        [((requests, sharing * head_size), BF16)],
        flops=10**11,
        args=loaded,
    )
    other_attended = swap(attended, "half")
    (route,) = kernel_call(
        route_body,
        [((TAIL, 4 * LANES), BF16)],
        scratch=[pltpu.VMEM((TAIL, 4 * LANES), F32)],
        args=(expert_ids.T, gate_weights.T),
    )
    (routes,) = kernel_call(
        stack_body, [((2 * TAIL, 4 * LANES), BF16)], args=(route, swap(route, "ep", 2))
    )
    keep, send = kernel_call(
        project_body,
        [((token_rows, cols), F32), ((token_rows, cols), BF16)],
        scratch=[pltpu.VMEM((token_rows, sharing * head_size), BF16)],
        args=(attended, other_attended, out_weight),
    )
    h32, h16, payload = kernel_call(
        hidden_body,
        [((token_rows, cols), F32), ((token_rows, cols), BF16), ((token_rows + TAIL, cols), BF16)],
        scratch=[pltpu.VMEM((TAIL, cols), F32)],
        args=(residual, gain, keep, swap(send, "tp")),
    )
    arrived = [h16] + [swap(h16, "ep", j) for j in range(1, blocks)]
    (middle,) = kernel_call(
        merge_body, [(((blocks - 2) * token_rows, cols), BF16)], args=arrived[1:-1]
    )
    from_x = [swap(v, "half") for v in (payload, middle, arrived[-1])]
    (mine,) = kernel_call(merge_body, [((tokens, cols), BF16)], args=arrived)
    theirs = swap(mine, "tp")
    pick, gate = kernel_call(
        pick_body,
        [((slot_rows, tokens), BF16), ((slot_rows, 1), F32)],
        args=(routes, swap(routes, "ep", 1)),
    )
    early = experts * 3 // 4
    squares, rows, gate_a, up_a = kernel_call(
        functools.partial(first_half_body, slots),
        [
            ((slot_rows, 1), F32),
            ((slot_rows, half_width), BF16),
            ((slots * early, hidden_units), F32),
            ((slots * early, hidden_units), F32),
        ],
        args=(mine, theirs, gain, w_gate, w_up, pick),
    )
    from_x, squares = lax.optimization_barrier((from_x, squares))
    (mine_x,) = kernel_call(join_body, [((tokens + TAIL, cols), BF16)], args=from_x)
    theirs_x = swap(mine_x, "tp")
    gate_b, up_b = kernel_call(
        functools.partial(more_first_half_body, slots, early),
        [((slots * (experts - early), hidden_units), F32)] * 2,
        args=(rows, w_gate, w_up),
    )
    (act,) = kernel_call(
        functools.partial(second_half_body, slots),
        [((slot_rows, hidden_units), BF16)],
        scratch=[pltpu.VMEM((slot_rows, half_width), BF16), pltpu.VMEM((slot_rows, 1), F32)],
        args=(
            mine_x, theirs_x, w_gate, w_up, pick, squares, gate_a, up_a, gate_b, up_b,
        ),
    )

    def down(act, other_half, other_core):
        return kernel_call(
            functools.partial(down_body, other_half, other_core),
            [((tokens, cols), BF16 if other_core else F32)],
            scratch=[pltpu.VMEM((slot_rows, cols), BF16)],
            flops=10**9,
            args=(act, gate, pick, w_down),
        )[0]

    got_a = swap(down(act, True, True), "tp")
    keep_a = down(act, True, False)
    sums = kernel_call(
        pair_sum_body,
        [((n * token_rows, cols), BF16) for n in (1, blocks - 2, 1)],
        args=(keep_a, got_a),
    )
    act, sums = lax.optimization_barrier((act, sums))
    from_x = [swap(v, "half") for v in sums]
    got_b = swap(down(act, False, True), "tp")
    keep_b = down(act, False, False)

    totals = []
    for start, count, other in ((blocks - 1, 1, from_x[2]), (1, blocks - 2, from_x[1])):
        totals += kernel_call(
            functools.partial(block_sum_body, start * token_rows),
            [((token_rows, cols), BF16)] * count,
            args=(keep_b, got_b, other),
        )
    partners = (blocks - 1, *range(1, blocks - 1))
    home = [swap(v, "ep", j) for j, v in zip(partners, totals)]
    (out,) = kernel_call(
        final_body, [((token_rows, cols), BF16)], args=(h32, keep_b, got_b, from_x[0], *home)
    )
    return out


def rows_fit(*args):
    residual, expert_ids = args[7], args[9]
    token_rows, top_count = expert_ids.shape
    cols = residual.shape[1] // lax.axis_size("tp")
    return 2 * token_rows == LANES and top_count == TAIL and cols == TAIL // 2 * LANES


def solution(mesh):
    placed = (
        P(("groups", "ep", "half"), "tp"),
        P(("groups", "ep", "half"), "tp"),
        P(("groups", "ep", "half"), "tp"),
        P(("groups", "ep", "half"), "tp", None, None),
        P(("groups", "ep", "half"), "tp", None, None),
        P(("groups", "ep", "half")),
        P("tp", "half"),
        P(("groups", "ep"), "half"),
        P("half"),
        P(("groups", "ep"), None),
        P(("groups", "ep"), None),
        P(("ep", "tp"), "half", None),
        P(("ep", "tp"), "half", None),
        P(("ep", "tp"), "half", None),
    )
    few = mesh.shape["half"] == 2 and mesh.shape["tp"] == 2 and mesh.shape["ep"] == 4

    def on_device(*args):
        return by_rows(*args) if few and rows_fit(*args) else by_slots(*args)

    return jax.shard_map(
        on_device,
        mesh=mesh,
        in_specs=placed,
        out_specs=P(("groups", "ep"), ("half", "tp")),
        check_vma=False,
    )
```
